32 devices in a mesh: fsdp: 4 (over y, core), ctx: 2 (over x), tp: 4 (over z).
Axes of the slice: x: 2, y: 2, z: 4, core: 2. Of those that a mesh axis runs over, the one named last changes fastest.
Arguments:
- tokens: bfloat16 [1024, 8, 768], P('ctx', 'fsdp'), may hold values from -11 to 11
- cotangent: bfloat16 [1024, 8, 768], P(('ctx', 'tp'), 'fsdp'), may hold values from -6 to 6
- segment_ids: int32 [8, 1024], P('fsdp', 'ctx'), may hold values from 0 to 3, never falling along the last dimension, each value on 1 to 512 neighbouring positions
- valid_mask: int32 [8, 1024], P('fsdp', 'ctx'), may hold values from 0 to 1, as said below
- latent_qkv: float32 [768, 3, 768], P('fsdp', None, 'tp'), may hold values from -1 to 1
- latent_out: float32 [768, 768], P('fsdp', 'tp'), may hold values from -1 to 1
- latent_up: float32 [768, 3072], P('fsdp', 'tp'), may hold values from -1 to 1
- latent_down: float32 [768, 3072], P('fsdp', 'tp'), may hold values from -1 to 1
- qkv_quant: float32 [2, 3, 768], P(None, None, 'tp'), may hold values from -0.3 to 2, as said below
- up_quant: float32 [2, 3072], P(None, 'tp'), may hold values from -0.3 to 2, as said below
- out_quant: float32 [2, 768], P(None, 'fsdp'), may hold values from -0.3 to 2, as said below
- down_quant: float32 [2, 768], P(None, 'fsdp'), may hold values from -0.3 to 2, as said below
- bias_qv: float32 [2, 768], P(None, 'tp'), may hold values from -1.5 to 1.5
- bias_up: float32 [3072], P('tp'), may hold values from -1.5 to 1.5
- row_params: float32 [6, 768], replicated, may hold values from -2 to 2, as said below
- clip_in: float32 [768], replicated, may hold values from 2 to 4
- clip_ctx: float32 [768], P('tp'), may hold values from 0.3 to 1.5
- clip_hidden: float32 [3072], P('tp'), may hold values from 1 to 3
- t_qkv: bfloat16 [768, 3, 768], P('fsdp', None, 'tp'), may hold values from -0.21875 to 0.21875
- t_out: bfloat16 [768, 768], P('fsdp', 'tp'), may hold values from -1.75 to 1.75
- t_up: bfloat16 [768, 3072], P('fsdp', 'tp'), may hold values from -0.21875 to 0.21875
- t_down: bfloat16 [768, 3072], P('fsdp', 'tp'), may hold values from -0.109375 to 0.109375
- t_bias_qv: float32 [2, 768], P(None, 'tp'), may hold values from -1.5 to 1.5
- t_bias_up: float32 [3072], P('tp'), may hold values from -1.5 to 1.5
- t_rows: float32 [6, 768], replicated, may hold values from -2 to 2, as said below
Outputs:
- layer_out: bfloat16 [1024, 8, 768], P(('ctx', 'tp'), 'fsdp')
- input_grad: float32 [1024, 8, 768], P(('ctx', 'tp'), 'fsdp')
- grad_qkv: float32 [768, 3, 768], P('fsdp', None, 'tp')
- grad_out: float32 [768, 768], P('fsdp', 'tp')
- grad_up: float32 [768, 3072], P('fsdp', 'tp')
- grad_down: float32 [768, 3072], P('fsdp', 'tp')
- grad_rows: float32 [6, 768], P(None, 'fsdp')
- grad_qv: float32 [2, 768], P(None, 'tp')
- grad_bias_up: float32 [3072], P('tp')
- statistics: float32 [4], replicated
The draws below stay inside these ranges and needn't reach their ends.
Inputs may be any that keep to these rules, and one draw needn't show every extreme that they name: `valid_mask`: the valid positions of each sequence are its first ones, half of its 1024 positions or more. `segment_ids`: segment numbers never fall along a sequence. `qkv_quant`: row 1 is positive. `up_quant`: row 1 is positive. `out_quant`: row 1 is positive. `down_quant`: row 1 is positive. `row_params`: rows 2 and 4 are positive. `t_rows`: rows 2 and 4 are positive.
All inputs are finite; a program needn't handle non-finite values.
Results may differ from the reference program's by a relative error of at most 0.023.
Values may be sent and summed in bfloat16 or wider, within the bound.
No kernel may reach another device: no remote copies, remote signals or barrier semaphores. Data moves between devices by JAX's collectives and lax.ppermute only.
A program may use at most 192 MiB of HBM per device.

```python
import math
import jax
import jax.numpy as jnp
import numpy as np
from jax import lax

D = 768
HEAD_DIM = 64
FF = 3072
LEN = 1024
SEQS = 8
DOCS = 4
DOC_MOST = 512


def draw_tokens(key, part):
    first = jax.random.fold_in(key, 0)
    place = (jnp.arange(SEQS)[None, :] * LEN + jnp.arange(LEN)[:, None]).astype(jnp.float32) / (SEQS * LEN)
    level = (0.6 * jnp.exp(jnp.log(3.0) * place))[:, :, None]
    base = jnp.clip(jax.random.normal(first, (LEN, SEQS, D), jnp.float32), -6.0, 6.0)
    return (base * level).astype(jnp.bfloat16)


def draw_valid_mask(key, part):
    pads = jax.random.randint(key, (SEQS, 1), 0, LEN // 2 + 1)
    return (jnp.arange(LEN)[None, :] < LEN - pads).astype(jnp.int32)


def quant_pair(key, shape, low_scale, high_scale):
    first, second = jax.random.split(key)
    shift = jax.random.uniform(first, shape, jnp.float32, -0.3, 0.3)
    spread = jax.random.uniform(second, shape, jnp.float32, 0.0, 1.0)
    scales = low_scale * jnp.exp(spread * jnp.log(high_scale / low_scale))
    return jnp.stack([shift, scales]).astype(jnp.float32)


def draw_qkv_quant(key, part):
    return quant_pair(key, (3, D), 0.5 / D ** 0.5, 2.0 / D ** 0.5)


def draw_up_quant(key, part):
    return quant_pair(key, (FF,), 0.5 / D ** 0.5, 2.0 / D ** 0.5)


def draw_out_quant(key, part):
    return quant_pair(key, (D,), 4.0 / D ** 0.5, 16.0 / D ** 0.5)


def draw_down_quant(key, part):
    return quant_pair(key, (D,), 0.8 / FF ** 0.5, 3.2 / FF ** 0.5)


def vector_rows(key):
    first, second = jax.random.split(key)
    shifts = 0.3 * jnp.clip(jax.random.normal(first, (6, D), jnp.float32), -5.0, 5.0)
    gains = 1.0 + 0.2 * jnp.clip(jax.random.normal(second, (6, D), jnp.float32), -2.5, 2.5)
    pick = jnp.array([0.0, 0.0, 1.0, 0.0, 1.0, 0.0], jnp.float32)[:, None]
    return (pick * gains + (1.0 - pick) * shifts).astype(jnp.float32)


def draw_row_params(key, part):
    return vector_rows(jax.random.fold_in(key, 11))


def draw_t_rows(key, part):
    return vector_rows(jax.random.fold_in(key, 23))


def block_scale(own_key, dims, cuts, smallest, high):
    factor_of = 1.0
    for axis_at, blocks in cuts:
        heights = jax.random.uniform(jax.random.fold_in(jax.random.fold_in(own_key, 6), axis_at), (blocks,), jnp.float32, smallest / len(cuts), high / len(cuts))
        factor_of = factor_of * jnp.repeat(jnp.exp(heights), dims[axis_at] // blocks).reshape((-1,) + (1,) * (len(dims) - 1 - axis_at))
    return factor_of


def profile(count, total, bound, skew):
    loads = [(1 << 20) // math.isqrt(rank ** skew) + 1 for rank in range(2, count + 1)]
    rest, given = total - bound - (count - 1), [1] * (count - 1)
    while rest > 0:
        candidates = [i for i in range(count - 1) if given[i] < bound]
        pool, left = sum([loads[i] for i in candidates]), rest
        for i in candidates:
            addition = min(bound - given[i], max(1, left * loads[i] // pool), rest)
            given[i] = given[i] + addition
            rest = rest - addition
    return np.array([bound] + given)


def ragged(key, count, total, bound, slope):
    if count == 2:
        one = jax.random.randint(key, (), max(1, total - bound), min(bound, total - 1) + 1)
        return jnp.stack([one, total - one])
    sizes = jnp.asarray(profile(count, total, bound, slope), jnp.int32)
    couples = (count - 1) // 2
    donor, taker = sizes[1:1 + 2 * couples:2], sizes[2:2 + 2 * couples:2]
    room = jnp.minimum(donor - 1, bound - taker)
    passed = jax.random.randint(jax.random.fold_in(key, 1), (couples,), 0, 1 << 20) % (room + 1)
    sizes = sizes.at[1:1 + 2 * couples:2].set(donor - passed).at[2:2 + 2 * couples:2].set(taker + passed)
    return sizes[jax.random.permutation(jax.random.fold_in(key, 2), count)]


def scatter_about(stream_key, extent, deviation, most, pieces=(), kind=jnp.bfloat16):
    loudness = block_scale(stream_key, extent, pieces, -0.22, 0.18) if pieces else 1.0
    values = jax.random.normal(stream_key, extent, jnp.float32) * deviation * loudness
    return jnp.minimum(jnp.maximum(values, -most), most).astype(kind)


def setup_inputs(seed: int = 0) -> dict:
    splits = jax.random.split(jax.random.key(seed), 26)
    return {
        "tokens": draw_tokens(jax.random.fold_in(splits[25], 71), 0),
        "cotangent": scatter_about(splits[1], (LEN, SEQS, D), 1.0, 6.0, ((0, 8), (1, 4))),
        "segment_ids": jax.vmap(lambda own: jnp.searchsorted(jnp.cumsum(ragged(own, DOCS, LEN, DOC_MOST, 2)), jnp.arange(LEN), side="right"))(jax.random.split(splits[2], SEQS)).reshape((SEQS, LEN)).astype(jnp.int32),
        "valid_mask": draw_valid_mask(jax.random.fold_in(splits[25], 71), 0),
        "latent_qkv": jnp.clip(jax.random.uniform(splits[4], (D, 3, D), jnp.float32, -1.0, 1.0) * block_scale(splits[4], (D, 3, D), ((0, 4), (2, 4)), -0.4, 0.0), -1.0, 1.0),
        "latent_out": jnp.clip(jax.random.uniform(splits[5], (D, D), jnp.float32, -1.0, 1.0) * block_scale(splits[5], (D, D), ((0, 4), (1, 4)), -0.4, 0.0), -1.0, 1.0),
        "latent_up": jnp.clip(jax.random.uniform(splits[6], (D, FF), jnp.float32, -1.0, 1.0) * block_scale(splits[6], (D, FF), ((0, 4), (1, 4)), -0.4, 0.0), -1.0, 1.0),
        "latent_down": jnp.clip(jax.random.uniform(splits[7], (D, FF), jnp.float32, -1.0, 1.0) * block_scale(splits[7], (D, FF), ((0, 4), (1, 4)), -0.4, 0.0), -1.0, 1.0),
        "qkv_quant": draw_qkv_quant(jax.random.fold_in(splits[25], 71), 0),
        "up_quant": draw_up_quant(jax.random.fold_in(splits[25], 71), 0),
        "out_quant": draw_out_quant(jax.random.fold_in(splits[25], 71), 0),
        "down_quant": draw_down_quant(jax.random.fold_in(splits[25], 71), 0),
        "bias_qv": scatter_about(splits[12], (2, D), 0.3, 1.5, ((1, 4),), jnp.float32),
        "bias_up": scatter_about(splits[13], (FF,), 0.3, 1.5, ((0, 4),), jnp.float32),
        "row_params": draw_row_params(jax.random.fold_in(splits[25], 71), 0),
        "clip_in": jnp.clip(jnp.exp(jax.random.uniform(splits[15], (D,), jnp.float32, math.log(2.0), math.log(4.0))), 2.0, 4.0),
        "clip_ctx": jnp.clip(jnp.exp(math.log(1.5) - 1.60943787 * jax.random.uniform(splits[16], (D,), jnp.float32) ** block_scale(splits[16], (D,), ((0, 4),), -0.2, 0.2)), 0.3, 1.5),
        "clip_hidden": jnp.clip(jnp.exp(math.log(3.0) - 1.0986123 * jax.random.uniform(splits[17], (FF,), jnp.float32) ** block_scale(splits[17], (FF,), ((0, 4),), -0.2, 0.2)), 1.0, 3.0),
        "t_qkv": scatter_about(splits[18], (D, 3, D), D ** -0.5, 0.21875, ((0, 4), (2, 4))),
        "t_out": scatter_about(splits[19], (D, D), (D // 64) ** -0.5, 1.75, ((0, 4), (1, 4))),
        "t_up": scatter_about(splits[20], (D, FF), D ** -0.5, 0.21875, ((0, 4), (1, 4))),
        "t_down": scatter_about(splits[21], (D, FF), FF ** -0.5, 0.109375, ((0, 4), (1, 4))),
        "t_bias_qv": scatter_about(splits[22], (2, D), 0.3, 1.5, ((1, 4),), jnp.float32),
        "t_bias_up": scatter_about(splits[23], (FF,), 0.3, 1.5, ((0, 4),), jnp.float32),
        "t_rows": draw_t_rows(jax.random.fold_in(splits[25], 71), 0),
    }


@jax.custom_vjp
def low(v):
    return lax.optimization_barrier(v.astype(jnp.bfloat16)).astype(jnp.float32)

@jax.custom_vjp
def low_back(v):
    return v

def low_keep(v):
    return (low(v), None)

def low_pass(kept, grad):
    return (grad,)

def back_keep(v):
    return (v, None)

def back_low(kept, grad):
    return (low(grad),)
low.defvjp(low_keep, low_pass)
low_back.defvjp(back_keep, back_low)
epsilon = 1e-05
floor_score = -1e+30

def exact_product(left, right, form):
    return jnp.einsum(form, left, right, precision=lax.Precision.HIGHEST)

def layer_norm(stream, gains, biases):
    centred = stream - lax.optimization_barrier(jnp.mean(stream, axis=-1, keepdims=True))
    spread = lax.optimization_barrier(jnp.mean(centred * centred, axis=-1, keepdims=True))
    return centred * lax.rsqrt(spread + epsilon) * gains + biases

def exact_gelu(values):
    return jax.nn.gelu(values, approximate=False)

def binarize(moving, frozen, shift, scales):
    fixed = frozen - shift
    value = jnp.sign(fixed) + jnp.clip(moving - shift, -1.0, 1.0) - jnp.clip(fixed, -1.0, 1.0)
    return low(scales * value)

def attend(queries, keys, values, seg, keep_key):
    length = queries.shape[0]
    heads = queries.shape[1] // HEAD_DIM
    block = math.gcd(length, 512)
    scale = HEAD_DIM ** (-0.5)
    key_heads = keys.reshape(length, heads, HEAD_DIM)
    value_heads = values.reshape(length, heads, HEAD_DIM)
    positions = jnp.arange(length, dtype=jnp.int32)
    key_tag = jnp.where(keep_key > 0, seg, -1)

    def one_block(index):
        start = (index * block).astype(jnp.int32)
        rows = lax.dynamic_slice_in_dim(queries, start, block, 0).reshape(block, heads, HEAD_DIM)
        row_seg = lax.dynamic_slice_in_dim(seg, start, block, 0)
        row_pos = start + jnp.arange(block, dtype=jnp.int32)
        scores = low_back(exact_product(rows, key_heads, 'qhe,khe->hqk') * scale)
        allowed = (row_seg[:, None] == key_tag[None, :]) | (row_pos[:, None] == positions[None, :])
        scores = jnp.where(allowed[None], scores, floor_score)
        probs = low(jax.nn.softmax(scores, axis=-1))
        return exact_product(probs, value_heads, 'hqk,khe->qhe').reshape(block, heads * HEAD_DIM)
    blocks = lax.map(jax.checkpoint(one_block), jnp.arange(length // block, dtype=jnp.int32))
    return blocks.reshape(length, heads * HEAD_DIM)

def student_seq(stream, seg, keep, matrices, bias_qv, bias_up, rows, clips):
    b_qkv, b_out, b_up, b_down = matrices
    clip_in, clip_ctx, clip_hidden = clips
    a_in = low(jnp.clip(stream, -clip_in, clip_in))
    proj = exact_product(a_in, b_qkv, 'ld,dkh->lkh')
    queries = low_back(low(proj[:, 0] + bias_qv[0]))
    keys = low_back(low(proj[:, 1]))
    values = low_back(low(proj[:, 2] + bias_qv[1]))
    attended = low_back(attend(queries, keys, values, seg, keep))
    context = low(clip_ctx * jnp.tanh(attended / clip_ctx))
    attn = low_back(exact_product(context, b_out, 'lh,dh->ld') + rows[0])
    h_one = layer_norm(stream + attn, rows[2], rows[3])
    upper = low_back(exact_product(low(h_one), b_up, 'ld,df->lf') + bias_up)
    hidden = low(clip_hidden * jnp.tanh(exact_gelu(upper) / clip_hidden))
    ffn = low_back(exact_product(hidden, b_down, 'lf,df->ld') + rows[1])
    out = layer_norm(h_one + ffn, rows[4], rows[5])
    return (out, attn, ffn)

def teacher_seq(stream, seg, keep, matrices, t_bias_qv, t_bias_up, t_rows):
    w_qkv, w_out, w_up, w_down = matrices
    proj = exact_product(stream, w_qkv, 'ld,dkh->lkh')
    queries = low(proj[:, 0] + t_bias_qv[0])
    keys = low(proj[:, 1])
    values = low(proj[:, 2] + t_bias_qv[1])
    attended = attend(queries, keys, values, seg, keep)
    attn = exact_product(low(attended), w_out, 'lh,dh->ld') + t_rows[0]
    h_one = layer_norm(stream + attn, t_rows[2], t_rows[3])
    upper = exact_product(low(h_one), w_up, 'ld,df->lf') + t_bias_up
    ffn = exact_product(low(exact_gelu(upper)), w_down, 'lf,df->ld') + t_rows[1]
    return layer_norm(h_one + ffn, t_rows[4], t_rows[5])

def reference(tokens, cotangent, segment_ids, valid_mask, latent_qkv, latent_out, latent_up, latent_down, qkv_quant, up_quant, out_quant, down_quant, bias_qv, bias_up, row_params, clip_in, clip_ctx, clip_hidden, t_qkv, t_out, t_up, t_down, t_bias_qv, t_bias_up, t_rows):
    streams = jnp.transpose(tokens.astype(jnp.float32), (1, 0, 2))
    arriving = jnp.transpose(cotangent.astype(jnp.float32), (1, 0, 2))
    teacher_mats = (t_qkv.astype(jnp.float32), t_out.astype(jnp.float32), t_up.astype(jnp.float32), t_down.astype(jnp.float32))

    def teacher_one(item):
        return teacher_seq(item[0], item[1], item[2], teacher_mats, t_bias_qv, t_bias_up, t_rows)
    teacher_out = lax.map(teacher_one, (streams, segment_ids, valid_mask))
    clips = (clip_in, clip_ctx, clip_hidden)

    def forward(moving_qkv, moving_out, moving_up, moving_down, moving_qv, moving_up_bias, moving_rows, stream_all):
        b_qkv = binarize(moving_qkv, latent_qkv, qkv_quant[0][None], qkv_quant[1][None])
        b_out = binarize(moving_out, latent_out, out_quant[0][:, None], out_quant[1][:, None])
        b_up = binarize(moving_up, latent_up, up_quant[0][None], up_quant[1][None])
        b_down = binarize(moving_down, latent_down, down_quant[0][:, None], down_quant[1][:, None])
        matrices = (b_qkv, b_out, b_up, b_down)

        def one_seq(item):
            return student_seq(item[0], item[1], item[2], matrices, moving_qv, moving_up_bias, moving_rows, clips)
        return lax.map(jax.checkpoint(one_seq), (stream_all, segment_ids, valid_mask))
    (out, attn, ffn), pull = jax.vjp(forward, latent_qkv, latent_out, latent_up, latent_down, bias_qv, bias_up, row_params, streams)
    keep = valid_mask.astype(jnp.float32)[..., None]
    grads = pull((arriving + keep * (out - teacher_out), jnp.zeros_like(attn), jnp.zeros_like(ffn)))
    denom = jnp.sum(keep) * D
    statistics = jnp.stack([jnp.sqrt(jnp.sum(keep * streams * streams) / denom), jnp.sqrt(jnp.sum(keep * attn * attn) / denom), jnp.sqrt(jnp.sum(keep * ffn * ffn) / denom), jnp.sum(keep * (out - teacher_out) ** 2) / denom])
    layer_out = jnp.transpose(out, (1, 0, 2)).astype(jnp.bfloat16)
    input_grad = jnp.transpose(grads[7], (1, 0, 2))
    return (layer_out, input_grad, grads[0], grads[1], grads[2], grads[3], grads[6], grads[4], grads[5], statistics)
```

```python
import functools
import math

import jax
import jax.numpy as jnp
from jax import lax
from jax.experimental import pallas as pl
from jax.experimental.pallas import tpu as pltpu
from jax.sharding import PartitionSpec as P

HEAD_DIM = 64


epsilon = 1e-05
floor_score = -1e30


def binarize(latent, shift, scales):
    return (scales * jnp.sign(latent - shift)).astype(jnp.bfloat16)


def straight(summed, latent, shift, scales):
    inside = (jnp.abs(latent - shift) < 1.0).astype(jnp.float32)
    return summed * scales * inside


def layer_norm(stream, gains, biases):
    centred = stream - jnp.mean(stream, axis=-1, keepdims=True)
    spread = jnp.mean(centred * centred, axis=-1, keepdims=True)
    return centred * lax.rsqrt(spread + epsilon) * gains + biases


def exact_gelu(values):
    return jax.nn.gelu(values, approximate=False)


def key_block(count):
    return math.gcd(count, 512)


def headed(array):
    return array.reshape(array.shape[0], array.shape[1], array.shape[2] // HEAD_DIM, HEAD_DIM)


def allowed_pairs(query_seg, query_pos, key_tags, key_pos):
    same = query_seg[:, :, None] == jnp.transpose(key_tags)[:, None, :]
    diagonal = query_pos[:, None] == key_pos[None, :]
    return (same | diagonal[None])[:, None]


def online_step(state, queries, keys, values, allowed, scale):
    running, total, accum = state
    scores = (
        jnp.einsum("tshe,kshe->shtk", queries, keys, preferred_element_type=jnp.float32) * scale
    )
    scores = jnp.where(allowed, scores, floor_score)
    newest = jnp.maximum(running, jnp.max(scores, axis=-1))
    weights = jnp.where(allowed, jnp.exp(scores - newest[..., None]), 0.0)
    factor = jnp.exp(running - newest)
    total = total * factor + jnp.sum(weights, axis=-1)
    accum = accum * factor[..., None] + jnp.einsum(
        "shtk,kshe->shte", weights.astype(jnp.bfloat16), values, preferred_element_type=jnp.float32
    )
    return (newest, total, accum)


def finish(state):
    running, total, accum = state
    merged = accum / total[..., None]
    return (jnp.transpose(merged, (2, 0, 1, 3)), running + jnp.log(total))


def vmem_specs(count):
    return [pl.BlockSpec(memory_space=pltpu.VMEM)] * count


def call_kernel(kernel, place, inputs, outs, scratch=(), flops=0, moved=0, exps=0):
    return pl.pallas_call(
        kernel,
        out_shape=outs,
        in_specs=[pl.BlockSpec(memory_space=pltpu.SMEM)] + vmem_specs(len(inputs)),
        out_specs=jax.tree.map(lambda _: pl.BlockSpec(memory_space=pltpu.VMEM), outs),
        scratch_shapes=list(scratch),
        compiler_params=pltpu.CompilerParams(vmem_limit_bytes=60 * 2**20),
        cost_estimate=pl.CostEstimate(flops=flops, bytes_accessed=moved, transcendentals=exps),
    )(place, *inputs)


def shaped(shape, dtype):
    return jax.ShapeDtypeStruct(shape, dtype)


NT = (((1,), (1,)), ((), ()))


def dot_nt(left, right):
    return lax.dot_general(left, right, NT, preferred_element_type=jnp.float32)


def dot_nn(left, right):
    return jnp.dot(left, right, preferred_element_type=jnp.float32)


def place_rows(place_ref, pieces, target, index=()):
    size = pieces[0].shape[-2]
    for distance, piece in zip((0, 2, 1, 3), pieces):
        start = pl.multiple_of((place_ref[0] ^ distance) * size, 64)
        target[(*index, pl.ds(start, size), slice(None))] = piece[...] if not index else piece[index]


def masked_bias(code_col, code_row, block, count, size):
    segments = code_row >> 1
    tags = jnp.where((code_col & 1) > 0, code_col >> 1, -1)
    key_at = lax.broadcasted_iota(jnp.int32, (count, size), 0)
    query_at = lax.broadcasted_iota(jnp.int32, (count, size), 1) + block * size
    allowed = (tags == segments) | (key_at == query_at)
    return jnp.where(allowed, 0.0, floor_score)


def attention_kernel(
    student,
    place_ref,
    own_ref,
    other_ref,
    w0_ref,
    w2_ref,
    w1_ref,
    w3_ref,
    bias_ref,
    clip_in_ref,
    clip_ref,
    col_ref,
    row_ref,
    *refs,
):
    if student:
        c_ref, a_ref, q_ref, k_ref, v_ref, ratio_ref, lse_ref, w_ref, vt_ref, mask_ref = refs
    else:
        c_ref, w_ref, q_ref, k_ref, v_ref, vt_ref, mask_ref = refs
    half = own_ref.shape[0]
    count = 2 * half
    cols = w_ref.shape[-1]
    heads = cols // HEAD_DIM
    size = 256
    bf16 = jnp.bfloat16
    for kind in range(3):
        for distance, piece in zip((0, 2, 1, 3), (w0_ref, w2_ref, w1_ref, w3_ref)):
            rows = piece.shape[1]
            start = pl.multiple_of((place_ref[0] ^ distance) * rows, 64)
            w_ref[kind, pl.ds(start, rows), :] = piece[kind]
    for part, source in enumerate((own_ref, other_ref)):
        inputs = source[...]
        base = part * half
        if student:
            wide = inputs.astype(jnp.float32)
            inputs = jnp.clip(wide, -clip_in_ref[...], clip_in_ref[...]).astype(bf16)
            a_ref[base : base + half, :] = inputs
        queries = (dot_nn(inputs, w_ref[0]) + bias_ref[0:1, :]).astype(bf16)
        keys = dot_nn(inputs, w_ref[1]).astype(bf16)
        values = (dot_nn(inputs, w_ref[2]) + bias_ref[1:2, :]).astype(bf16)
        for head in range(heads):
            lanes = slice(head * HEAD_DIM, (head + 1) * HEAD_DIM)
            q_ref[head, base : base + half, :] = queries[:, lanes] * (HEAD_DIM**-0.5)
            k_ref[head, base : base + half, :] = keys[:, lanes]
            v_ref[head, base : base + half, :] = values[:, lanes]
    eye = (
        lax.broadcasted_iota(jnp.int32, (HEAD_DIM, HEAD_DIM), 0)
        == lax.broadcasted_iota(jnp.int32, (HEAD_DIM, HEAD_DIM), 1)
    ).astype(bf16)
    for head in range(heads):
        vt_ref[head] = dot_nt(eye, v_ref[head]).astype(bf16)

    def one_block(block, carry):
        at = pl.multiple_of(block * size, size)
        mask_ref[...] = masked_bias(col_ref[...], row_ref[:, pl.ds(at, size)], block, count, size)
        outs = []
        for head in range(heads):
            scores = dot_nt(k_ref[head], q_ref[head, pl.ds(at, size), :]) + mask_ref[...]
            top = jnp.max(scores, axis=0, keepdims=True)
            weights = jnp.exp(scores - top)
            total = jnp.sum(weights, axis=0, keepdims=True)
            merged = dot_nn(vt_ref[head], weights.astype(bf16)) * (1.0 / total)
            outs.append(merged)
            if student:
                lse_ref[pl.ds(head, 1), pl.ds(at, size)] = top + jnp.log(total)
        merged = jnp.concatenate(outs + [jnp.zeros((256 - cols, size), jnp.float32)], axis=0)
        merged = jnp.transpose(merged)[:, :cols]
        if student:
            ratio = jnp.tanh(merged / clip_ref[...])
            ratio_ref[pl.ds(at, size), :] = ratio
            merged = clip_ref[...] * ratio
        merged = merged.astype(bf16)
        part, pair = block >> 1, block & 1
        share = size // 2
        c_ref[2 * pair, part] = merged[:share]
        c_ref[2 * pair + 1, part] = merged[share:]
        return carry

    lax.fori_loop(0, count // size, one_block, 0)


def attention_forward(student, place, own, other, pieces, bias, clip_in, clip, code_col, code_row):
    half, width = own.shape
    cols = pieces[0].shape[-1]
    heads = cols // HEAD_DIM
    count = 2 * half
    bf16, f32 = jnp.bfloat16, jnp.float32
    head_shape = (heads, count, HEAD_DIM)
    c_shape = shaped((4, 2, half // 4, cols), bf16)
    w = pltpu.VMEM((3, width, cols), bf16)
    vt = pltpu.VMEM((heads, HEAD_DIM, count), bf16)
    mask = pltpu.VMEM((count, 256), f32)
    if student:
        outs = (
            c_shape,
            shaped((count, width), bf16),
            shaped(head_shape, bf16),
            shaped(head_shape, bf16),
            shaped(head_shape, bf16),
            shaped((count, cols), f32),
            shaped((8, count), f32),
        )
        scratch = (w, vt, mask)
    else:
        outs = (c_shape,)
        scratch = (w,) + (pltpu.VMEM(head_shape, bf16),) * 3 + (vt, mask)
    return call_kernel(
        functools.partial(attention_kernel, student),
        place,
        (own, other, *pieces, bias, clip_in, clip, code_col, code_row),
        outs,
        scratch,
        flops=2 * count * width * cols * 3 + 4 * count * count * cols,
        moved=6 * count * width,
        exps=heads * count * count,
    )


def attention_pull_kernel(
    place_ref,
    a_ref,
    q_ref,
    k_ref,
    v_ref,
    ratio_ref,
    lse_ref,
    col_ref,
    row_ref,
    d0_ref,
    d1_ref,
    d2_ref,
    d3_ref,
    w0_ref,
    w2_ref,
    w1_ref,
    w3_ref,
    back_ref,
    dproj_ref,
    sums_ref,
    w_ref,
    grad_ref,
    kt_ref,
    mask_ref,
    dk_ref,
    dv_ref,
):
    heads, count, _ = q_ref.shape
    cols = heads * HEAD_DIM
    size = 256
    share = size // 2
    bf16, f32 = jnp.bfloat16, jnp.float32
    for kind in range(3):
        for distance, piece in zip((0, 2, 1, 3), (w0_ref, w2_ref, w1_ref, w3_ref)):
            rows = piece.shape[1]
            start = pl.multiple_of((place_ref[0] ^ distance) * rows, 64)
            w_ref[kind, pl.ds(start, rows), :] = piece[kind]
    eye = (
        lax.broadcasted_iota(jnp.int32, (HEAD_DIM, HEAD_DIM), 0)
        == lax.broadcasted_iota(jnp.int32, (HEAD_DIM, HEAD_DIM), 1)
    ).astype(bf16)
    for head in range(heads):
        kt_ref[head] = dot_nt(eye, k_ref[head]).astype(bf16)
    for distance, source in enumerate((d0_ref, d1_ref, d2_ref, d3_ref)):
        for part in range(2):
            at = part * (count // 2) + distance * share
            ratio = ratio_ref[at : at + share, :]
            grad = source[part].astype(f32) * (1.0 - ratio * ratio)
            for head in range(heads):
                lanes = slice(head * HEAD_DIM, (head + 1) * HEAD_DIM)
                grad_ref[head, at : at + share, :] = grad[:, lanes].astype(bf16)
    dk_ref[...] = jnp.zeros_like(dk_ref)
    dv_ref[...] = jnp.zeros_like(dv_ref)

    def one_block(block, carry):
        at = pl.multiple_of(block * size, size)
        mask_ref[...] = masked_bias(col_ref[...], row_ref[:, pl.ds(at, size)], block, count, size)
        outs = []
        for head in range(heads):
            query = q_ref[head, pl.ds(at, size), :]
            grad = grad_ref[head, pl.ds(at, size), :]
            lse = lse_ref[pl.ds(head, 1), pl.ds(at, size)]
            probs = jnp.exp(dot_nt(k_ref[head], query) + mask_ref[...] - lse)
            d_probs = dot_nt(v_ref[head], grad)
            delta = jnp.sum(probs * d_probs, axis=0, keepdims=True)
            d_scores = (probs * (d_probs - delta)).astype(bf16)
            dv_ref[head] += dot_nn(probs.astype(bf16), grad)
            dk_ref[head] += dot_nn(d_scores, query)
            outs.append(dot_nn(kt_ref[head], d_scores) * (HEAD_DIM**-0.5))
        merged = jnp.concatenate(outs + [jnp.zeros((256 - cols, size), f32)], axis=0)
        dproj_ref[0, pl.ds(at, size), :] = jnp.transpose(merged)[:, :cols].astype(bf16)
        return carry

    lax.fori_loop(0, count // size, one_block, 0)
    for head in range(heads):
        lanes = slice(head * HEAD_DIM, (head + 1) * HEAD_DIM)
        dproj_ref[1, :, lanes] = dk_ref[head].astype(bf16)
        dproj_ref[2, :, lanes] = dv_ref[head].astype(bf16)
    sums_ref[0:1, :] = jnp.sum(dproj_ref[0].astype(f32), axis=0, keepdims=True)
    sums_ref[1:2, :] = jnp.sum(dproj_ref[2].astype(f32), axis=0, keepdims=True)
    for part in range(2):
        at = slice(part * (count // 2), (part + 1) * (count // 2))
        back = (
            dot_nt(dproj_ref[0, at, :], w_ref[0])
            + dot_nt(dproj_ref[1, at, :], w_ref[1])
            + dot_nt(dproj_ref[2, at, :], w_ref[2])
        ).astype(bf16)
        for distance in range(4):
            back_ref[distance, part] = back[distance * share : (distance + 1) * share]


def attention_backward(place, a_in, q, k, v, ratio, lse, code_col, code_row, grads, pieces):
    heads, count, _ = q.shape
    cols = heads * HEAD_DIM
    width = a_in.shape[1]
    bf16, f32 = jnp.bfloat16, jnp.float32
    return call_kernel(
        attention_pull_kernel,
        place,
        (a_in, q, k, v, ratio, lse, code_col, code_row, *grads, *pieces),
        (
            shaped((4, 2, count // 8, width), bf16),
            shaped((3, count, cols), bf16),
            shaped((2, cols), f32),
        ),
        (
            pltpu.VMEM((3, width, cols), bf16),
            pltpu.VMEM((heads, count, HEAD_DIM), bf16),
            pltpu.VMEM((heads, HEAD_DIM, count), bf16),
            pltpu.VMEM((count, 256), f32),
            pltpu.VMEM((heads, count, HEAD_DIM), f32),
            pltpu.VMEM((heads, count, HEAD_DIM), f32),
        ),
        flops=2 * count * width * cols * 3 + 10 * count * count * cols,
        moved=8 * count * width,
        exps=heads * count * count,
    )


def unit_of(stream):
    mean = jnp.mean(stream, axis=-1, keepdims=True)
    centred = stream - mean
    scale = lax.rsqrt(jnp.mean(centred * centred, axis=-1, keepdims=True) + epsilon)
    return centred * scale, scale


def column_sum(value):
    return jnp.sum(value, axis=0, keepdims=True)


def dot_tn(left, right):
    return lax.dot_general(left, right, (((0,), (0,)), ((), ())), preferred_element_type=jnp.float32)


def out_norm_kernel(student, model, place_ref, c0, c1, c2, c3, w0, w2, w1, w3, own_ref, other_ref, valid_ref, params_ref, *refs):
    if student:
        w_ref, unit_ref, scale_ref, low_ref, sums_ref = refs
    else:
        wide_ref, low_ref, w_ref = refs
    share = own_ref.shape[0]
    total = None
    for r, source in enumerate((c0, c1, c2, c3)):
        for distance, piece in zip((0, 2, 1, 3), (w0, w2, w1, w3)):
            size = piece.shape[2]
            start = pl.multiple_of((place_ref[0] ^ distance) * size, 64)
            w_ref[r, pl.ds(start, size), :] = piece[r, model]
        context = jnp.concatenate([source[0], source[1]], axis=0)
        term = dot_nt(context, w_ref[r])
        total = term if total is None else total + term
    attn = total + params_ref[0:1, :]
    stream = jnp.concatenate([own_ref[...], other_ref[...]], axis=0).astype(jnp.float32)
    unit, scale = unit_of(stream + attn)
    wide = unit * params_ref[2:3, :] + params_ref[3:4, :]
    low_ref[...] = wide.astype(jnp.bfloat16)
    if student:
        unit_ref[...] = unit
        scale_ref[...] = scale
        valid = valid_ref[...]
        sums_ref[0:1, :] = column_sum(valid * jnp.ones_like(stream))
        sums_ref[1:2, :] = column_sum(valid * stream * stream)
        sums_ref[2:3, :] = column_sum(valid * attn * attn)
    else:
        wide_ref[...] = wide


def out_norm(student, place, contexts, pieces, own, other, valid, params):
    share, width = own.shape
    rows = 2 * share
    cols = contexts[0].shape[-1]
    f32, bf16 = jnp.float32, jnp.bfloat16
    w = (4, width, cols)
    if student:
        outs = (
            shaped(w, bf16),
            shaped((rows, width), f32),
            shaped((rows, 1), f32),
            shaped((rows, width), bf16),
            shaped((3, width), f32),
        )
        scratch = ()
    else:
        outs = (shaped((rows, width), f32), shaped((rows, width), bf16))
        scratch = (pltpu.VMEM(w, bf16),)
    return call_kernel(
        functools.partial(out_norm_kernel, student, 0 if student else 1),
        place,
        (*contexts, *pieces, own, other, valid, params),
        outs,
        scratch,
        flops=2 * rows * width * cols * 4,
        moved=12 * rows * width,
    )


def gelu_parts(values):
    cdf = 0.5 * (1.0 + lax.erf(values * (2.0**-0.5)))
    return values * cdf, cdf


def hidden_kernel(student, assemble, far, place_ref, h_ref, *refs):
    refs = list(refs)
    pieces = [refs.pop(0) for _ in range(8 if assemble else 1)]
    bias_ref = refs.pop(0)
    clip_ref = refs.pop(0) if student else None
    w_ref = refs.pop(0) if assemble else pieces[0]
    if student:
        hid_ref, slope_ref = refs.pop(0), refs.pop(0)
    part_ref = refs.pop(0)
    bf16 = jnp.bfloat16
    total = None
    inputs = h_ref[...]
    for r in range(4):
        if assemble:
            group = pieces[:4] if r < 2 else pieces[4:]
            for mat in range(2):
                for distance, piece in zip((0, 2, 1, 3), group):
                    size = piece.shape[2]
                    start = pl.multiple_of((place_ref[0] ^ distance) * size, 64)
                    w_ref[r, mat, pl.ds(start, size), :] = piece[r & 1, mat]
        upper = dot_nn(inputs, w_ref[r, 0]) + bias_ref[r : r + 1, :]
        active, cdf = gelu_parts(upper)
        if student:
            clip = clip_ref[r : r + 1, :]
            ratio = jnp.tanh(active / clip)
            pdf = jnp.exp(-0.5 * upper * upper) * ((2.0 * math.pi) ** -0.5)
            slope_ref[r] = ((1.0 - ratio * ratio) * (cdf + upper * pdf)).astype(bf16)
            hidden = (clip * ratio).astype(bf16)
            hid_ref[r] = hidden
        else:
            hidden = active.astype(bf16)
        term = dot_nt(hidden, w_ref[r, 1])
        total = term if total is None else total + term
    part_ref[...] = total.astype(part_ref.dtype)


def hidden_layer(student, far, place, h, weights, bias, clip):
    rows, width = h.shape
    half = bias.shape[-1]
    f32, bf16 = jnp.float32, jnp.bfloat16
    assemble = isinstance(weights, tuple)
    outs = []
    if assemble:
        outs.append(shaped((4, 2, width, half), bf16))
    if student:
        outs += [shaped((4, rows, half), bf16)] * 2
    outs.append(shaped((rows, width), bf16 if far else f32))
    inputs = (h, *(weights if assemble else (weights,)), bias) + ((clip,) if student else ())
    return call_kernel(
        functools.partial(hidden_kernel, student, assemble, far),
        place,
        inputs,
        tuple(outs),
        flops=2 * rows * width * half * 8,
        moved=8 * width * half * 2 + 16 * rows * half,
        exps=(3 if student else 1) * rows * half * 4,
    )


def loss_kernel(
    place_ref, unit_ref, ffn_ref, got_ref, ht_ref, ffnt_ref, gott_ref, cot_ref, cot_other_ref, valid_ref, params_ref, t_ref,
    layer_ref, layer_other_ref, dz_ref, low_ref, sums_ref,
):
    share = cot_ref.shape[0]
    f32, bf16 = jnp.float32, jnp.bfloat16
    h_one = unit_ref[...] * params_ref[2:3, :] + params_ref[3:4, :]
    ffn = ffn_ref[...] + got_ref[...].astype(f32) + params_ref[1:2, :]
    unit, scale = unit_of(h_one + ffn)
    out = unit * params_ref[4:5, :] + params_ref[5:6, :]
    low = out.astype(bf16)
    layer_ref[...] = low[:share]
    layer_other_ref[...] = low[share:]
    t_unit, _ = unit_of(ht_ref[...] + ffnt_ref[...] + gott_ref[...].astype(f32) + t_ref[1:2, :])
    difference = out - (t_unit * t_ref[4:5, :] + t_ref[5:6, :])
    valid = valid_ref[...]
    gap = valid * difference
    arriving = jnp.concatenate([cot_ref[...], cot_other_ref[...]], axis=0).astype(f32)
    grad = arriving + gap
    inner = grad * params_ref[4:5, :]
    dz = scale * (
        inner
        - jnp.mean(inner, axis=-1, keepdims=True)
        - unit * jnp.mean(inner * unit, axis=-1, keepdims=True)
    )
    dz_ref[...] = dz
    dz_low = dz.astype(bf16)
    low_ref[...] = dz_low
    sums_ref[0:1, :] = column_sum(dz_low.astype(f32))
    sums_ref[1:2, :] = column_sum(grad * unit)
    sums_ref[2:3, :] = column_sum(grad)
    sums_ref[3:4, :] = column_sum(valid * ffn * ffn)
    sums_ref[4:5, :] = column_sum(gap * difference)


def loss_step(place, unit, ffn, got, ht, ffnt, gott, cot, cot_other, valid, params, t_rows):
    rows, width = unit.shape
    share = cot.shape[0]
    f32, bf16 = jnp.float32, jnp.bfloat16
    return call_kernel(
        loss_kernel,
        place,
        (unit, ffn, got, ht, ffnt, gott, cot, cot_other, valid, params, t_rows),
        (
            shaped((share, width), bf16),
            shaped((share, width), bf16),
            shaped((rows, width), f32),
            shaped((rows, width), bf16),
            shaped((5, width), f32),
        ),
        flops=60 * rows * width,
        moved=30 * rows * width,
    )


def hidden_pull_kernel(place_ref, grad_ref, w_ref, slope_ref, du_ref, part_ref, sums_ref):
    grad = grad_ref[...]
    total = None
    for r in range(4):
        upper = (dot_nn(grad, w_ref[r, 1]) * slope_ref[r].astype(jnp.float32)).astype(jnp.bfloat16)
        du_ref[r] = upper
        sums_ref[r : r + 1, :] = column_sum(upper.astype(jnp.float32))
        term = dot_nt(upper, w_ref[r, 0])
        total = term if total is None else total + term
    part_ref[...] = total.astype(part_ref.dtype)


def hidden_pull(far, place, grad, weights, slope):
    rows, width = grad.shape
    half = slope.shape[-1]
    f32, bf16 = jnp.float32, jnp.bfloat16
    return call_kernel(
        hidden_pull_kernel,
        place,
        (grad, weights, slope),
        (shaped((4, rows, half), bf16), shaped((rows, width), bf16 if far else f32), shaped((4, half), f32)),
        flops=2 * rows * width * half * 8,
        moved=8 * width * half * 2 + 16 * rows * half,
    )


def keep_and_send(place_ref, full_ref, keep_ref, send_ref, index):
    size = full_ref.shape[0] // 4
    for slot in range(2):
        for target, distance in ((keep_ref, 2 * slot), (send_ref, 2 * slot + 1)):
            start = pl.multiple_of((place_ref[0] ^ distance) * size, 64)
            target[(slot, *index)] = full_ref[pl.ds(start, size), :].astype(jnp.bfloat16)


def hidden_grads_kernel(place_ref, f0, f1, hid0, hid1, h0, h1, du0, du1, keep_ref, send_ref, full_ref):
    for mat, (left0, left1, right0, right1) in enumerate(((h0, h1, du0, du1), (f0, f1, hid0, hid1))):
        left = jnp.concatenate([left0[...], left1[...]], axis=0)
        for r in range(4):
            right = jnp.concatenate([right0[r], right1[r]], axis=0)
            full_ref[...] = dot_tn(left, right)
            keep_and_send(place_ref, full_ref, keep_ref, send_ref, (mat, r))


def hidden_grads(place, grads, hidden, inputs, d_upper):
    rows, width = grads[0].shape
    half = hidden[0].shape[-1]
    bf16 = jnp.bfloat16
    out = shaped((2, 2, 4, width // 4, half), bf16)
    return call_kernel(
        hidden_grads_kernel,
        place,
        (*grads, *hidden, *inputs, *d_upper),
        (out, out),
        (pltpu.VMEM((width, half), jnp.float32),),
        flops=4 * rows * width * half * 8,
        moved=16 * width * half * 2,
    )


def first_pull_kernel(place_ref, dz_ref, part_ref, got_ref, unit_ref, scale_ref, params_ref, w_ref, first_ref, low_ref, sums_ref, ctx_ref):
    f32, bf16 = jnp.float32, jnp.bfloat16
    grad = dz_ref[...] + part_ref[...] + got_ref[...].astype(f32)
    unit = unit_ref[...]
    inner = grad * params_ref[2:3, :]
    first = scale_ref[...] * (
        inner
        - jnp.mean(inner, axis=-1, keepdims=True)
        - unit * jnp.mean(inner * unit, axis=-1, keepdims=True)
    )
    first_ref[...] = first
    low = first.astype(bf16)
    low_ref[...] = low
    sums_ref[0:1, :] = column_sum(low.astype(f32))
    sums_ref[1:2, :] = column_sum(grad * unit)
    sums_ref[2:3, :] = column_sum(grad)
    share = ctx_ref.shape[2]
    for r in range(4):
        back = dot_nn(low, w_ref[r]).astype(bf16)
        ctx_ref[r, 0] = back[:share]
        ctx_ref[r, 1] = back[share:]


def first_pull(place, dz, part, got, unit, scale, params, weights):
    rows, width = dz.shape
    cols = weights.shape[-1]
    f32, bf16 = jnp.float32, jnp.bfloat16
    return call_kernel(
        first_pull_kernel,
        place,
        (dz, part, got, unit, scale, params, weights),
        (
            shaped((rows, width), f32),
            shaped((rows, width), bf16),
            shaped((3, width), f32),
            shaped((4, 2, rows // 2, cols), bf16),
        ),
        flops=2 * rows * width * cols * 4,
        moved=20 * rows * width,
    )


def out_grads_kernel(place_ref, low_ref, c0, c1, c2, c3, keep_ref, send_ref, full_ref):
    for r, source in enumerate((c0, c1, c2, c3)):
        context = jnp.concatenate([source[0], source[1]], axis=0)
        full_ref[...] = dot_tn(low_ref[...], context)
        keep_and_send(place_ref, full_ref, keep_ref, send_ref, (r,))


def out_grads(place, low, contexts):
    rows, width = low.shape
    cols = contexts[0].shape[-1]
    out = shaped((2, 4, width // 4, cols), jnp.bfloat16)
    return call_kernel(
        out_grads_kernel,
        place,
        (low, *contexts),
        (out, out),
        (pltpu.VMEM((width, cols), jnp.float32),),
        flops=2 * rows * width * cols * 4,
        moved=20 * width * cols,
    )


def in_grads_kernel(place_ref, a_ref, d_ref, keep_ref, send_ref, full_ref):
    for kind in range(3):
        full_ref[...] = dot_tn(a_ref[...], d_ref[kind])
        keep_and_send(place_ref, full_ref, keep_ref, send_ref, (kind,))


def in_grads(place, a_in, d_proj):
    count, width = a_in.shape
    cols = d_proj.shape[-1]
    out = shaped((2, 3, width // 4, cols), jnp.bfloat16)
    return call_kernel(
        in_grads_kernel,
        place,
        (a_in, d_proj),
        (out, out),
        (pltpu.VMEM((width, cols), jnp.float32),),
        flops=2 * count * width * cols * 3,
        moved=4 * count * width,
    )


def input_kernel(place_ref, first_ref, b0, b1, b2, b3, own_ref, other_ref, clip_ref, mine_ref, other_out_ref):
    f32 = jnp.float32
    share = own_ref.shape[0]
    for part, (source, target) in enumerate(((own_ref, mine_ref), (other_ref, other_out_ref))):
        through = b0[part].astype(f32) + b1[part].astype(f32) + b2[part].astype(f32) + b3[part].astype(f32)
        inside = jnp.abs(source[...].astype(f32)) < clip_ref[...]
        first = first_ref[part * share : (part + 1) * share, :]
        target[...] = (first + jnp.where(inside, through, 0.0)).astype(target.dtype)


def input_rows(place, first, backs, own, other, clip_in):
    share, width = own.shape
    return call_kernel(
        input_kernel,
        place,
        (first, *backs, own, other, clip_in),
        (shaped((share, width), jnp.float32), shaped((share, width), jnp.bfloat16)),
        flops=10 * share * width,
        moved=20 * share * width,
    )


def swap_ctx(value):
    return lax.ppermute(value, "ctx", [(0, 1), (1, 0)])


def swap_core(value):
    return lax.ppermute(value, "fsdp", [(i, i ^ 1) for i in range(4)])


def swap_row(value):
    return lax.ppermute(value, "fsdp", [(i, i ^ 2) for i in range(4)])


def swap_tp(value, distance):
    return lax.ppermute(value, "tp", [(i, i ^ distance) for i in range(4)])


def fsdp_pieces(piece):
    far = swap_row(piece)
    return (piece, far, swap_core(piece), swap_core(far))


def tp_pieces(piece):
    return [piece] + [swap_tp(piece, r) for r in (1, 2, 3)]


def exchange_tp(stacked):
    return [stacked[0]] + [swap_tp(stacked[r], r) for r in (1, 2, 3)]


def paired_body(
    tokens,
    cotangent,
    segment_ids,
    valid_mask,
    latent_qkv,
    latent_out,
    latent_up,
    latent_down,
    qkv_quant,
    up_quant,
    out_quant,
    down_quant,
    bias_qv,
    bias_up,
    row_params,
    clip_in,
    clip_ctx,
    clip_hidden,
    t_qkv,
    t_out,
    t_up,
    t_down,
    t_bias_qv,
    t_bias_up,
    t_rows,
):
    local_len, seq_count, width = tokens.shape
    share = cotangent.shape[0]
    col_width = latent_qkv.shape[2]
    hidden_width = latent_up.shape[1]
    half_hidden = hidden_width // 2
    row_width = latent_qkv.shape[0]
    tp_rank = lax.axis_index("tp")
    ctx_rank = lax.axis_index("ctx")
    fsdp_rank = lax.axis_index("fsdp")
    f32, bf16 = jnp.float32, jnp.bfloat16
    place = jnp.stack([fsdp_rank, tp_rank, ctx_rank]).astype(jnp.int32)

    def by_distance(value):
        pairs = value.reshape(2, 2, *value.shape[1:])
        pairs = jnp.where((tp_rank & 1) > 0, pairs[:, ::-1], pairs)
        pairs = jnp.where((tp_rank >> 1) > 0, pairs[::-1], pairs)
        return pairs.reshape(value.shape)

    def mine(value, axis):
        return lax.dynamic_index_in_dim(value, ctx_rank, axis, keepdims=False)

    def theirs(value, axis):
        return lax.dynamic_index_in_dim(value, 1 - ctx_rank, axis, keepdims=False)

    def half_of(weight):
        return mine(weight.reshape(row_width, 2, half_hidden), 1)

    relative = by_distance(tokens.reshape(4, share, seq_count, width))
    own = mine(relative, 2).reshape(local_len, width)
    other = swap_ctx(theirs(relative, 2).reshape(local_len, width))
    code = by_distance(
        jnp.transpose(segment_ids * 2 + (valid_mask > 0).astype(jnp.int32)).reshape(
            4, share, seq_count
        )
    )
    code_all = jnp.concatenate(
        [mine(code, 2).reshape(local_len), swap_ctx(theirs(code, 2)).reshape(local_len)]
    )
    code_col, code_row = code_all[:, None], code_all[None, :]
    valid = (
        jnp.concatenate([code_all[:share], code_all[local_len : local_len + share]]) & 1
    ).astype(f32)[:, None]
    bin_qkv = jnp.transpose(
        binarize(latent_qkv, qkv_quant[0][None], qkv_quant[1][None]), (1, 0, 2)
    )
    student_qkv = fsdp_pieces(bin_qkv)
    teacher_qkv = fsdp_pieces(jnp.transpose(t_qkv, (1, 0, 2)))
    bin_out = binarize(latent_out, out_quant[0][:, None], out_quant[1][:, None])
    bin_up = binarize(latent_up, up_quant[0][None], up_quant[1][None])
    bin_down = binarize(latent_down, down_quant[0][:, None], down_quant[1][:, None])
    out_pieces = fsdp_pieces(jnp.stack(tp_pieces(jnp.stack([bin_out, t_out]))))

    def hidden_pieces(up, down):
        parts = tp_pieces(jnp.stack([half_of(up), half_of(down)]))
        return fsdp_pieces(jnp.stack(parts[:2])) + fsdp_pieces(jnp.stack(parts[2:]))

    student_hidden = hidden_pieces(bin_up, bin_down)
    teacher_hidden = hidden_pieces(t_up, t_down)
    vectors = jnp.stack(
        tp_pieces(
            jnp.stack([mine(v.reshape(2, half_hidden), 0) for v in (bias_up, clip_hidden, t_bias_up)])
        )
    )
    bias_up_all, clip_all, t_bias_up_all = vectors[:, 0], vectors[:, 1], vectors[:, 2]
    clip_in_row, clip_row = clip_in[None], clip_ctx[None]

    context, a_in, q, k, v, ratio, lse = attention_forward(
        True, place, own, other, student_qkv, bias_qv, clip_in_row, clip_row, code_col, code_row
    )
    contexts = exchange_tp(context)
    (teacher_context,) = attention_forward(
        False, place, own, other, teacher_qkv, t_bias_qv, clip_in_row, clip_row, code_col, code_row
    )
    teacher_contexts = exchange_tp(teacher_context)
    own_rows, other_rows = own[:share], other[:share]
    out_full, unit, scale, h_low, first_sums = out_norm(
        True, place, contexts, out_pieces, own_rows, other_rows, valid, row_params
    )
    h_teacher, ht_low = out_norm(
        False, place, teacher_contexts, out_pieces, own_rows, other_rows, valid, t_rows
    )
    h_far = swap_ctx(h_low)
    ht_far = swap_ctx(ht_low)
    hidden_full, hid_own, slope_own, part_own = hidden_layer(
        True, False, place, h_low, student_hidden, bias_up_all, clip_all
    )
    hid_far, slope_far, part_far = hidden_layer(
        True, True, place, h_far, hidden_full, bias_up_all, clip_all
    )
    part_got = swap_ctx(part_far)
    teacher_full, t_part_own = hidden_layer(
        False, False, place, ht_low, teacher_hidden, t_bias_up_all, None
    )
    (t_part_far,) = hidden_layer(False, True, place, ht_far, teacher_full, t_bias_up_all, None)
    t_part_got = swap_ctx(t_part_far)
    cot_own = mine(cotangent, 1)
    cot_other = swap_ctx(theirs(cotangent, 1))
    layer_own, layer_other, d_second, d_ffn, second_sums = loss_step(
        place, unit, part_own, part_got, h_teacher, t_part_own, t_part_got,
        cot_own, cot_other, valid, row_params, t_rows,
    )

    def home(own_part, other_part):
        got = swap_ctx(other_part).astype(own_part.dtype)
        first = jnp.where(ctx_rank == 0, own_part, got)
        second = jnp.where(ctx_rank == 0, got, own_part)
        return jnp.stack([first, second], axis=1)

    layer_out = home(layer_own, layer_other)
    d_ffn_far = swap_ctx(d_ffn)
    du_own, d_part_own, du_sums_own = hidden_pull(False, place, d_ffn, hidden_full, slope_own)
    du_far, d_part_far, du_sums_far = hidden_pull(True, place, d_ffn_far, hidden_full, slope_far)
    d_part_got = swap_ctx(d_part_far)
    keep_hidden, send_hidden = hidden_grads(
        place, (d_ffn, d_ffn_far), (hid_own, hid_far), (h_low, h_far), (du_own, du_far)
    )
    d_first, d_attn, third_sums, d_context = first_pull(
        place, d_second, d_part_own, d_part_got, unit, scale, row_params, out_full
    )
    d_contexts = exchange_tp(d_context)
    keep_out, send_out = out_grads(place, d_attn, contexts)
    back, d_proj, d_bias_qv = attention_backward(
        place, a_in, q, k, v, ratio, lse, code_col, code_row, d_contexts, student_qkv
    )
    backs = exchange_tp(back)
    keep_in, send_in = in_grads(place, a_in, d_proj)
    input_own, input_other = input_rows(place, d_first, backs, own_rows, other_rows, clip_in_row)
    input_grad = home(input_own, input_other)

    def over_fsdp(keep, send):
        got = swap_core(send)
        stay = keep[0].astype(f32) + got[0].astype(f32)
        leave = (keep[1].astype(f32) + got[1].astype(f32)).astype(bf16)
        return stay + swap_row(leave).astype(f32)

    def over_tp(value, axis):
        parts = [lax.index_in_dim(value, r, axis, keepdims=False) for r in range(4)]
        return parts[0] + sum(swap_tp(parts[r].astype(bf16), r).astype(f32) for r in (1, 2, 3))

    low_hidden = over_tp(over_fsdp(keep_hidden, send_hidden), 1).astype(bf16)
    low_far = swap_ctx(low_hidden)
    hidden_halves = [
        jnp.where(ctx_rank == 0, low_hidden, low_far),
        jnp.where(ctx_rank == 0, low_far, low_hidden),
    ]
    grad_hidden = jnp.concatenate(hidden_halves, axis=-1).astype(f32)
    low_out = over_tp(over_fsdp(keep_out, send_out), 0).astype(bf16)
    sum_out = low_out.astype(f32) + swap_ctx(low_out).astype(f32)
    low_in = over_fsdp(keep_in, send_in).astype(bf16)
    sum_in = low_in.astype(f32) + swap_ctx(low_in).astype(f32)
    grad_qkv = straight(
        jnp.transpose(sum_in, (1, 0, 2)), latent_qkv, qkv_quant[0][None], qkv_quant[1][None]
    )
    grad_out = straight(sum_out, latent_out, out_quant[0][:, None], out_quant[1][:, None])
    grad_up = straight(grad_hidden[0], latent_up, up_quant[0][None], up_quant[1][None])
    grad_down = straight(
        grad_hidden[1], latent_down, down_quant[0][:, None], down_quant[1][:, None]
    )
    placed_up = by_distance(du_sums_own + du_sums_far)
    placed_up = jnp.where(
        jnp.arange(2)[None, :, None] == ctx_rank, placed_up[:, None], 0.0
    ).reshape(hidden_width * 4 // width, width)
    vector = jnp.concatenate([third_sums, second_sums, first_sums, placed_up], axis=0)
    vector = vector + swap_core(vector)
    vector = vector + swap_row(vector)
    vector = vector + swap_ctx(vector)
    vector = vector + swap_tp(vector, 1)
    vector = vector + swap_tp(vector, 2)
    qv_sums = d_bias_qv + swap_core(d_bias_qv)
    qv_sums = qv_sums + swap_row(qv_sums)
    grad_qv = qv_sums + swap_ctx(qv_sums)
    vector_sums = jnp.concatenate([vector[0:1], vector[3:4], vector[1:3], vector[4:6]], axis=0)
    stat_sums = jnp.sum(vector[6:11], axis=-1)
    up_sums = vector[11:].reshape(4 * hidden_width)
    grad_rows = lax.dynamic_slice_in_dim(vector_sums, fsdp_rank * row_width, row_width, 1)
    grad_bias_up = lax.dynamic_slice_in_dim(up_sums, tp_rank * hidden_width, hidden_width, 0)
    denom = stat_sums[2]
    statistics = jnp.stack(
        [
            jnp.sqrt(stat_sums[3] / denom),
            jnp.sqrt(stat_sums[4] / denom),
            jnp.sqrt(stat_sums[0] / denom),
            stat_sums[1] / denom,
        ]
    )
    return (
        layer_out,
        input_grad,
        grad_qkv,
        grad_out,
        grad_up,
        grad_down,
        grad_rows,
        grad_qv,
        grad_bias_up,
        statistics,
    )


def general_body(
    tokens,
    cotangent,
    segment_ids,
    valid_mask,
    latent_qkv,
    latent_out,
    latent_up,
    latent_down,
    qkv_quant,
    up_quant,
    out_quant,
    down_quant,
    bias_qv,
    bias_up,
    row_params,
    clip_in,
    clip_ctx,
    clip_hidden,
    t_qkv,
    t_out,
    t_up,
    t_down,
    t_bias_qv,
    t_bias_up,
    t_rows,
):
    local_len, seq_count, width = tokens.shape
    share = cotangent.shape[0]
    col_width = latent_qkv.shape[2]
    hidden_width = latent_up.shape[1]
    row_width = latent_qkv.shape[0]
    local_heads = col_width // HEAD_DIM
    scale = HEAD_DIM ** (-0.5)
    tp_rank = lax.axis_index("tp")
    ctx_rank = lax.axis_index("ctx")
    fsdp_rank = lax.axis_index("fsdp")
    full_len = local_len * lax.axis_size("ctx")
    bin_qkv = binarize(latent_qkv, qkv_quant[0][None], qkv_quant[1][None])
    bin_out = binarize(latent_out, out_quant[0][:, None], out_quant[1][:, None])
    bin_up = binarize(latent_up, up_quant[0][None], up_quant[1][None])
    bin_down = binarize(latent_down, down_quant[0][:, None], down_quant[1][:, None])
    gathered = (
        lax.all_gather(bin_qkv, "fsdp", axis=0, tiled=True),
        lax.all_gather(bin_out, "fsdp", axis=0, tiled=True),
        lax.all_gather(bin_up, "fsdp", axis=0, tiled=True),
        lax.all_gather(bin_down, "fsdp", axis=0, tiled=True),
        lax.all_gather(t_qkv, "fsdp", axis=0, tiled=True),
        lax.all_gather(t_out, "fsdp", axis=0, tiled=True),
        lax.all_gather(t_up, "fsdp", axis=0, tiled=True),
        lax.all_gather(t_down, "fsdp", axis=0, tiled=True),
    )
    full_qkv, full_out, full_up, full_down, teach_qkv, teach_out, teach_up, teach_down = gathered
    stream = tokens.astype(jnp.float32)
    a_in = jnp.clip(stream, -clip_in, clip_in).astype(jnp.bfloat16)
    proj_student = jnp.einsum("tsd,dkh->tskh", a_in, full_qkv, preferred_element_type=jnp.float32)
    proj_teacher = jnp.einsum(
        "tsd,dkh->tskh", tokens, teach_qkv, preferred_element_type=jnp.float32
    )
    student_q = (proj_student[:, :, 0] + bias_qv[0]).astype(jnp.bfloat16)
    student_k = proj_student[:, :, 1].astype(jnp.bfloat16)
    student_v = (proj_student[:, :, 2] + bias_qv[1]).astype(jnp.bfloat16)
    teacher_q = (proj_teacher[:, :, 0] + t_bias_qv[0]).astype(jnp.bfloat16)
    teacher_k = proj_teacher[:, :, 1].astype(jnp.bfloat16)
    teacher_v = (proj_teacher[:, :, 2] + t_bias_qv[1]).astype(jnp.bfloat16)
    student_queries = headed(student_q)
    teacher_queries = headed(teacher_q)
    query_pos = ctx_rank * local_len + jnp.arange(local_len, dtype=jnp.int32)
    key_tags = jnp.transpose(jnp.where(valid_mask > 0, segment_ids, -1))
    empty_state = (
        jnp.full((seq_count, local_heads, local_len), floor_score, jnp.float32),
        jnp.zeros((seq_count, local_heads, local_len), jnp.float32),
        jnp.zeros((seq_count, local_heads, local_len, HEAD_DIM), jnp.float32),
    )
    buffers = (
        jnp.zeros((full_len, seq_count, col_width), jnp.bfloat16),
        jnp.zeros((full_len, seq_count, col_width), jnp.bfloat16),
        jnp.zeros((full_len, seq_count), jnp.int32),
    )
    carry = (empty_state, empty_state, buffers)
    pieces = (
        lax.all_gather(student_k, "ctx", axis=0, tiled=True),
        lax.all_gather(student_v, "ctx", axis=0, tiled=True),
        lax.all_gather(teacher_k, "ctx", axis=0, tiled=True),
        lax.all_gather(teacher_v, "ctx", axis=0, tiled=True),
        lax.all_gather(key_tags, "ctx", axis=0, tiled=True),
    )
    start = jnp.int32(0)
    count = pieces[0].shape[0]
    block = key_block(count)

    def inner(states, index):
        offset = index * block
        parts = [lax.dynamic_slice_in_dim(piece, offset, block, 0) for piece in pieces]
        key_pos = offset + jnp.arange(block, dtype=jnp.int32)
        allowed = allowed_pairs(segment_ids, query_pos, parts[4], key_pos)
        states = (
            online_step(
                states[0], student_queries, headed(parts[0]), headed(parts[1]), allowed, scale
            ),
            online_step(
                states[1], teacher_queries, headed(parts[2]), headed(parts[3]), allowed, scale
            ),
        )
        return (states, None)

    states, _ = lax.scan(inner, (carry[0], carry[1]), jnp.arange(count // block, dtype=jnp.int32))
    kept = tuple(
        (
            lax.dynamic_update_slice_in_dim(buffer, piece, start, 0)
            for buffer, piece in zip(carry[2], (pieces[0], pieces[1], pieces[4]))
        )
    )
    student_state, teacher_state, kept = (states[0], states[1], kept)
    attended, log_total = finish(student_state)
    teacher_attended, _ = finish(teacher_state)
    attended_flat = attended.reshape(local_len, seq_count, col_width)
    ctx_ratio = jnp.tanh(attended_flat / clip_ctx)
    context = (clip_ctx * ctx_ratio).astype(jnp.bfloat16)
    teacher_context = teacher_attended.reshape(local_len, seq_count, col_width).astype(jnp.bfloat16)
    rows_student = context
    rows_teacher = teacher_context
    attn_both = lax.psum_scatter(
        jnp.concatenate(
            [
                jnp.einsum(
                    "tsh,dh->tsd", rows_student, full_out, preferred_element_type=jnp.float32
                ),
                jnp.einsum(
                    "tsh,dh->tsd", rows_teacher, teach_out, preferred_element_type=jnp.float32
                ),
            ],
            axis=-1,
        ).astype(jnp.bfloat16),
        "tp",
        scatter_dimension=0,
        tiled=True,
    ).astype(jnp.float32)
    attn_student = attn_both[..., :width] + row_params[0]
    attn_teacher = attn_both[..., width:] + t_rows[0]
    stream_rows = lax.dynamic_slice_in_dim(stream, tp_rank * share, share, 0)
    first_sum = stream_rows + attn_student
    h_one = layer_norm(first_sum, row_params[2], row_params[3])
    h_teacher = layer_norm(stream_rows + attn_teacher, t_rows[2], t_rows[3])
    h_full, h_teacher_full = (
        lax.all_gather(h_one.astype(jnp.bfloat16), "tp", axis=0, tiled=True),
        lax.all_gather(h_teacher.astype(jnp.bfloat16), "tp", axis=0, tiled=True),
    )
    upper = jnp.einsum("tsd,df->tsf", h_full, full_up, preferred_element_type=jnp.float32) + bias_up
    activated = exact_gelu(upper)
    hid_ratio = jnp.tanh(activated / clip_hidden)
    hidden = (clip_hidden * hid_ratio).astype(jnp.bfloat16)
    upper_teacher = (
        jnp.einsum("tsd,df->tsf", h_teacher_full, teach_up, preferred_element_type=jnp.float32)
        + t_bias_up
    )
    hidden_teacher = exact_gelu(upper_teacher).astype(jnp.bfloat16)
    rows_student = hidden
    rows_teacher = hidden_teacher
    ffn_both = lax.psum_scatter(
        jnp.concatenate(
            [
                jnp.einsum(
                    "tsf,df->tsd", rows_student, full_down, preferred_element_type=jnp.float32
                ),
                jnp.einsum(
                    "tsf,df->tsd", rows_teacher, teach_down, preferred_element_type=jnp.float32
                ),
            ],
            axis=-1,
        ).astype(jnp.bfloat16),
        "tp",
        scatter_dimension=0,
        tiled=True,
    ).astype(jnp.float32)
    ffn_student = ffn_both[..., :width] + row_params[1]
    ffn_teacher = ffn_both[..., width:] + t_rows[1]
    second_sum = h_one + ffn_student
    out = layer_norm(second_sum, row_params[4], row_params[5])
    teacher_out = layer_norm(h_teacher + ffn_teacher, t_rows[4], t_rows[5])
    layer_out = out.astype(jnp.bfloat16)
    valid_rows = jnp.transpose(
        lax.dynamic_slice_in_dim(valid_mask, tp_rank * share, share, 1)
    ).astype(jnp.float32)[..., None]
    difference = out - teacher_out
    grad_out_total = cotangent.astype(jnp.float32) + valid_rows * difference
    stat_terms = jnp.stack(
        [
            jnp.sum(valid_rows) + 0.0 * jnp.sum(stream_rows[:1, :1, :1]),
            jnp.sum(valid_rows * stream_rows * stream_rows),
            jnp.sum(valid_rows * attn_student * attn_student),
            jnp.sum(valid_rows * ffn_student * ffn_student),
            jnp.sum(valid_rows * difference * difference),
        ]
    )
    _, second_pull = jax.vjp(layer_norm, second_sum, row_params[4], row_params[5])
    d_second, d_gain_two, d_bias_two = second_pull(grad_out_total)
    d_ffn = d_second.astype(jnp.bfloat16)
    d_bias_down = jnp.sum(d_ffn.astype(jnp.float32), axis=(0, 1))
    d_ffn_full = lax.all_gather(d_ffn, "tp", axis=0, tiled=True)
    grad_bin_down = jnp.einsum(
        "tsd,tsf->df", d_ffn_full, hidden, preferred_element_type=jnp.float32
    )
    d_hidden = jnp.einsum("tsd,df->tsf", d_ffn_full, full_down, preferred_element_type=jnp.float32)
    d_hidden = d_hidden * (1.0 - hid_ratio * hid_ratio)
    _, gelu_pull = jax.vjp(exact_gelu, upper)
    d_upper = gelu_pull(d_hidden)[0].astype(jnp.bfloat16)
    d_bias_up = jnp.sum(d_upper.astype(jnp.float32), axis=(0, 1))
    grad_bin_up = jnp.einsum("tsd,tsf->df", h_full, d_upper, preferred_element_type=jnp.float32)
    rows = d_upper
    d_h_one = d_second + lax.psum_scatter(
        jnp.einsum("tsf,df->tsd", rows, full_up, preferred_element_type=jnp.float32).astype(
            jnp.bfloat16
        ),
        "tp",
        scatter_dimension=0,
        tiled=True,
    ).astype(jnp.float32)
    _, first_pull = jax.vjp(layer_norm, first_sum, row_params[2], row_params[3])
    d_first, d_gain_one, d_bias_one = first_pull(d_h_one)
    d_attn = d_first.astype(jnp.bfloat16)
    d_bias_out = jnp.sum(d_attn.astype(jnp.float32), axis=(0, 1))
    d_attn_full = lax.all_gather(d_attn, "tp", axis=0, tiled=True)
    grad_bin_out = jnp.einsum(
        "tsd,tsh->dh", d_attn_full, context, preferred_element_type=jnp.float32
    )
    d_context = jnp.einsum("tsd,dh->tsh", d_attn_full, full_out, preferred_element_type=jnp.float32)
    d_attended = (d_context * (1.0 - ctx_ratio * ctx_ratio)).astype(jnp.bfloat16)
    d_attended_heads = headed(d_attended)
    delta = jnp.transpose(
        jnp.sum(d_attended_heads.astype(jnp.float32) * attended, axis=-1), (1, 2, 0)
    )
    key_all, value_all, tag_all = kept
    back_block = key_block(full_len)

    def back_step(grad_q, index):
        offset = index * back_block
        keys = headed(lax.dynamic_slice_in_dim(key_all, offset, back_block, 0))
        values = headed(lax.dynamic_slice_in_dim(value_all, offset, back_block, 0))
        block_tags = lax.dynamic_slice_in_dim(tag_all, offset, back_block, 0)
        key_pos = offset + jnp.arange(back_block, dtype=jnp.int32)
        allowed = allowed_pairs(segment_ids, query_pos, block_tags, key_pos)
        current = grad_q
        scores = (
            jnp.einsum("tshe,kshe->shtk", student_queries, keys, preferred_element_type=jnp.float32)
            * scale
        )
        probs = jnp.where(allowed, jnp.exp(scores - log_total[..., None]), 0.0)
        d_probs = jnp.einsum(
            "tshe,kshe->shtk", d_attended_heads, values, preferred_element_type=jnp.float32
        )
        d_scores = (probs * (d_probs - delta[..., None])).astype(jnp.bfloat16)
        current = (
            current
            + jnp.einsum("shtk,kshe->shte", d_scores, keys, preferred_element_type=jnp.float32)
            * scale
        )
        grad_k = (
            jnp.einsum(
                "shtk,tshe->kshe", d_scores, student_queries, preferred_element_type=jnp.float32
            )
            * scale
        )
        grad_v = jnp.einsum(
            "shtk,tshe->kshe",
            probs.astype(jnp.bfloat16),
            d_attended_heads,
            preferred_element_type=jnp.float32,
        )
        joined = jnp.concatenate(
            [
                grad_k.reshape(back_block, seq_count, col_width),
                grad_v.reshape(back_block, seq_count, col_width),
            ],
            axis=-1,
        )
        return (current, joined)

    grad_q, key_terms = lax.scan(
        back_step,
        jnp.zeros((seq_count, local_heads, local_len, HEAD_DIM), jnp.float32),
        jnp.arange(full_len // back_block, dtype=jnp.int32),
    )
    key_terms = key_terms.reshape(full_len, seq_count, 2 * col_width)
    key_sums = lax.psum_scatter(
        key_terms.astype(jnp.bfloat16), "ctx", scatter_dimension=0, tiled=True
    ).astype(jnp.float32)
    grad_q_flat = jnp.transpose(grad_q, (2, 0, 1, 3)).reshape(local_len, seq_count, col_width)
    d_proj = jnp.stack(
        [grad_q_flat, key_sums[..., :col_width], key_sums[..., col_width:]], axis=2
    ).astype(jnp.bfloat16)
    d_bias_qv = jnp.stack(
        [
            jnp.sum(d_proj[:, :, 0].astype(jnp.float32), axis=(0, 1)),
            jnp.sum(d_proj[:, :, 2].astype(jnp.float32), axis=(0, 1)),
        ]
    )
    grad_bin_qkv = jnp.einsum("tsd,tskh->dkh", a_in, d_proj, preferred_element_type=jnp.float32)
    rows = d_proj
    through = lax.psum_scatter(
        jnp.einsum("tskh,dkh->tsd", rows, full_qkv, preferred_element_type=jnp.float32).astype(
            jnp.bfloat16
        ),
        "tp",
        scatter_dimension=0,
        tiled=True,
    ).astype(jnp.float32)
    input_grad = d_first + through * (jnp.abs(stream_rows) < clip_in).astype(jnp.float32)
    shards = (
        lax.psum_scatter(
            grad_bin_qkv.astype(jnp.bfloat16), "fsdp", scatter_dimension=0, tiled=True
        ).astype(jnp.float32),
        lax.psum_scatter(
            grad_bin_out.astype(jnp.bfloat16), "fsdp", scatter_dimension=0, tiled=True
        ).astype(jnp.float32),
        lax.psum_scatter(
            grad_bin_up.astype(jnp.bfloat16), "fsdp", scatter_dimension=0, tiled=True
        ).astype(jnp.float32),
        lax.psum_scatter(
            grad_bin_down.astype(jnp.bfloat16), "fsdp", scatter_dimension=0, tiled=True
        ).astype(jnp.float32),
    )
    summed = (
        lax.psum(shards[0].astype(jnp.bfloat16), "ctx").astype(jnp.float32),
        lax.psum(shards[1].astype(jnp.bfloat16), "ctx").astype(jnp.float32),
        lax.psum(shards[2].astype(jnp.bfloat16), "ctx").astype(jnp.float32),
        lax.psum(shards[3].astype(jnp.bfloat16), "ctx").astype(jnp.float32),
    )
    grad_qkv = straight(summed[0], latent_qkv, qkv_quant[0][None], qkv_quant[1][None])
    grad_out = straight(summed[1], latent_out, out_quant[0][:, None], out_quant[1][:, None])
    grad_up = straight(summed[2], latent_up, up_quant[0][None], up_quant[1][None])
    grad_down = straight(summed[3], latent_down, down_quant[0][:, None], down_quant[1][:, None])
    vector_grads = jnp.stack(
        [d_bias_out, d_bias_down, d_gain_one, d_bias_one, d_gain_two, d_bias_two]
    )
    placed_qv = lax.dynamic_update_slice_in_dim(
        jnp.zeros((2, width), jnp.float32), d_bias_qv, tp_rank * col_width, 1
    )
    placed_up = lax.dynamic_update_slice_in_dim(
        jnp.zeros((hidden_width * lax.axis_size("tp"),), jnp.float32),
        d_bias_up,
        tp_rank * hidden_width,
        0,
    )
    stat_sums, vector_sums, qv_sums, up_sums = lax.psum(
        (stat_terms, vector_grads, placed_qv, placed_up), ("fsdp", "ctx", "tp")
    )
    grad_rows = lax.dynamic_slice_in_dim(vector_sums, fsdp_rank * row_width, row_width, 1)
    grad_qv = lax.dynamic_slice_in_dim(qv_sums, tp_rank * col_width, col_width, 1)
    grad_bias_up = lax.dynamic_slice_in_dim(up_sums, tp_rank * hidden_width, hidden_width, 0)
    denom = stat_sums[0] * width
    statistics = jnp.stack(
        [
            jnp.sqrt(stat_sums[1] / denom),
            jnp.sqrt(stat_sums[2] / denom),
            jnp.sqrt(stat_sums[3] / denom),
            stat_sums[4] / denom,
        ]
    )
    return (
        layer_out,
        input_grad,
        grad_qkv,
        grad_out,
        grad_up,
        grad_down,
        grad_rows,
        grad_qv,
        grad_bias_up,
        statistics,
    )


def pick_body(mesh):
    sizes = dict(mesh.shape)
    if sizes["fsdp"] == 4 and sizes["tp"] == 4 and sizes["ctx"] == 2:
        return paired_body
    return general_body


def solution(mesh):
    return jax.shard_map(
        pick_body(mesh),
        mesh=mesh,
        in_specs=(
            P("ctx", "fsdp", None),
            P(("ctx", "tp"), "fsdp", None),
            P("fsdp", "ctx"),
            P("fsdp", "ctx"),
            P("fsdp", None, "tp"),
            P("fsdp", "tp"),
            P("fsdp", "tp"),
            P("fsdp", "tp"),
            P(None, None, "tp"),
            P(None, "tp"),
            P(None, "fsdp"),
            P(None, "fsdp"),
            P(None, "tp"),
            P("tp"),
            P(),
            P(),
            P("tp"),
            P("tp"),
            P("fsdp", None, "tp"),
            P("fsdp", "tp"),
            P("fsdp", "tp"),
            P("fsdp", "tp"),
            P(None, "tp"),
            P("tp"),
            P(),
        ),
        out_specs=(
            P(("ctx", "tp"), "fsdp", None),
            P(("ctx", "tp"), "fsdp", None),
            P("fsdp", None, "tp"),
            P("fsdp", "tp"),
            P("fsdp", "tp"),
            P("fsdp", "tp"),
            P(None, "fsdp"),
            P(None, "tp"),
            P("tp"),
            P(),
        ),
        check_vma=False,
    )
```

```python
import functools
import math

import jax
import jax.numpy as jnp
from jax import lax
from jax.experimental import pallas as pl
from jax.experimental.pallas import tpu as pltpu
from jax.sharding import PartitionSpec as P

HEAD_DIM = 64


epsilon = 1e-05
floor_score = -1e30


def binarize(latent, shift, scales):
    return (scales * jnp.sign(latent - shift)).astype(jnp.bfloat16)


def straight(summed, latent, shift, scales):
    inside = (jnp.abs(latent - shift) < 1.0).astype(jnp.float32)
    return summed * scales * inside


def layer_norm(stream, gains, biases):
    centred = stream - jnp.mean(stream, axis=-1, keepdims=True)
    spread = jnp.mean(centred * centred, axis=-1, keepdims=True)
    return centred * lax.rsqrt(spread + epsilon) * gains + biases


def exact_gelu(values):
    return jax.nn.gelu(values, approximate=False)


def key_block(count):
    return math.gcd(count, 512)


def headed(array):
    return array.reshape(array.shape[0], array.shape[1], array.shape[2] // HEAD_DIM, HEAD_DIM)


def allowed_pairs(query_seg, query_pos, key_tags, key_pos):
    same = query_seg[:, :, None] == jnp.transpose(key_tags)[:, None, :]
    diagonal = query_pos[:, None] == key_pos[None, :]
    return (same | diagonal[None])[:, None]


def online_step(state, queries, keys, values, allowed, scale):
    running, total, accum = state
    scores = (
        jnp.einsum("tshe,kshe->shtk", queries, keys, preferred_element_type=jnp.float32) * scale
    )
    scores = jnp.where(allowed, scores, floor_score)
    newest = jnp.maximum(running, jnp.max(scores, axis=-1))
    weights = jnp.where(allowed, jnp.exp(scores - newest[..., None]), 0.0)
    factor = jnp.exp(running - newest)
    total = total * factor + jnp.sum(weights, axis=-1)
    accum = accum * factor[..., None] + jnp.einsum(
        "shtk,kshe->shte", weights.astype(jnp.bfloat16), values, preferred_element_type=jnp.float32
    )
    return (newest, total, accum)


def finish(state):
    running, total, accum = state
    merged = accum / total[..., None]
    return (jnp.transpose(merged, (2, 0, 1, 3)), running + jnp.log(total))


WORK_FACTOR = 4
TOKEN = (8, 128)
ROOM = 8 * 2**20


def vmem_specs(count):
    return [pl.BlockSpec(memory_space=pltpu.VMEM)] * count


def vmem_room(inputs, outs, scratch):
    total = 0
    for array in (*inputs, *jax.tree.leaves(outs), *scratch):
        *lead, rows, lanes = (1, 1, *array.shape)
        size = jnp.dtype(array.dtype).itemsize
        tile = 8 * (4 // size)
        total += math.prod(lead) * size * (-(-rows // tile) * tile) * (-(-lanes // 128) * 128)
    return min(total + ROOM, 60 * 2**20)


def call_kernel(kernel, place, inputs, outs, scratch=(), flops=0, moved=0, exps=0):
    place, after = place if isinstance(place, tuple) else (place, ())

    def body(place_ref, *refs):
        kernel(place_ref, *refs[len(after) :])

    return pl.pallas_call(
        body,
        out_shape=outs,
        in_specs=[pl.BlockSpec(memory_space=pltpu.SMEM)]
        + [pl.BlockSpec(memory_space=pl.ANY)] * len(after)
        + vmem_specs(len(inputs)),
        out_specs=jax.tree.map(lambda _: pl.BlockSpec(memory_space=pltpu.VMEM), outs),
        scratch_shapes=list(scratch),
        compiler_params=pltpu.CompilerParams(vmem_limit_bytes=vmem_room(inputs, outs, scratch)),
        cost_estimate=pl.CostEstimate(
            flops=WORK_FACTOR * flops, bytes_accessed=moved, transcendentals=exps
        ),
    )(place, *after, *inputs)


def shaped(shape, dtype):
    return jax.ShapeDtypeStruct(shape, dtype)


def gate_kernel(place_ref, token_ref):
    token_ref[...] = jnp.zeros_like(token_ref)


def gate(place, *arrays):
    return call_kernel(gate_kernel, (place, arrays), (), shaped(TOKEN, jnp.float32), flops=1, moved=1)


NT = (((1,), (1,)), ((), ()))


def dot_nt(left, right):
    return lax.dot_general(left, right, NT, preferred_element_type=jnp.float32)


def dot_nn(left, right):
    return jnp.dot(left, right, preferred_element_type=jnp.float32)


QUERY_BLOCK = 256


def place_projections(place_ref, pieces, target, first):
    size = pieces[0].shape[1]
    for kind in range(3):
        for distance, piece in zip((0, 2, 1, 3), pieces):
            start = pl.multiple_of((place_ref[0] ^ distance) * size, 64)
            target[kind, pl.ds(start, size), :] = piece[kind + first]


def project_kernel(place_ref, own_ref, w0, w2, w1, w3, bias_ref, clip_in_ref, full_ref, a_ref, q_ref, token_ref):
    place_projections(place_ref, (w0, w2, w1, w3), full_ref, 0)
    clipped = jnp.clip(own_ref[...].astype(jnp.float32), -clip_in_ref[...], clip_in_ref[...])
    clipped = clipped.astype(jnp.bfloat16)
    a_ref[...] = clipped
    write_heads(clipped, full_ref, bias_ref, q_ref, 0)
    token_ref[...] = jnp.zeros_like(token_ref)


def write_heads(inputs, w_ref, bias_ref, target, base):
    rows = inputs.shape[0]
    for kind in range(3):
        values = dot_nn(inputs, w_ref[kind])
        if kind != 1:
            values = values + bias_ref[kind >> 1 : (kind >> 1) + 1, :]
        values = values.astype(jnp.bfloat16)
        if kind == 0:
            values = values * (HEAD_DIM**-0.5)
        for head in range(target.shape[1]):
            target[kind, head, base : base + rows, :] = values[:, head * HEAD_DIM : (head + 1) * HEAD_DIM]


def project_own(place, own, pieces, bias, clip_in):
    half, width = own.shape
    cols = pieces[0].shape[-1]
    heads = cols // HEAD_DIM
    bf16 = jnp.bfloat16
    return call_kernel(
        project_kernel,
        place,
        (own, *pieces, bias, clip_in),
        (
            shaped((3, width, cols), bf16),
            shaped((half, width), bf16),
            shaped((3, heads, half, HEAD_DIM), bf16),
            shaped(TOKEN, jnp.float32),
        ),
        flops=1,
        moved=1,
    )


def unit_matrix():
    shape = (HEAD_DIM, HEAD_DIM)
    ones = lax.broadcasted_iota(jnp.int32, shape, 0) == lax.broadcasted_iota(jnp.int32, shape, 1)
    return ones.astype(jnp.bfloat16)


def block_window(row_ref, place_ref, blocks):
    mask = order_mask(place_ref)
    low, high = [], []
    for block in range(blocks):
        segment = row_ref[:, block * QUERY_BLOCK : (block + 1) * QUERY_BLOCK] >> 1
        low.append(jnp.min(segment))
        high.append(jnp.max(segment))
    windows = []
    for query in range(blocks):
        first, last = jnp.int32(blocks - 1), jnp.int32(0)
        for key in range(blocks):
            meets = (low[key] <= high[query]) & (high[key] >= low[query])
            at = key ^ mask
            first = jnp.where(meets, jnp.minimum(first, at), first)
            last = jnp.where(meets, jnp.maximum(last, at), last)
        windows.append((first, last - first + 1))
    return windows


def order_mask(place_ref):
    return 2 * place_ref[2] + (place_ref[1] >> 1)


def pick(values, index):
    chosen = values[0]
    for at in range(1, len(values)):
        chosen = jnp.where(index == at, values[at], chosen)
    return chosen


def pair_bias(col_ref, row_ref, query, key):
    size = QUERY_BLOCK
    code_col = col_ref[pl.ds(pl.multiple_of(key * size, size), size), :]
    code_row = row_ref[:, pl.ds(pl.multiple_of(query * size, size), size)]
    tags = jnp.where((code_col & 1) > 0, code_col >> 1, -1)
    apart = lax.broadcasted_iota(jnp.int32, (size, size), 0) - lax.broadcasted_iota(
        jnp.int32, (size, size), 1
    )
    allowed = (tags == (code_row >> 1)) | (apart == (query - key) * size)
    return jnp.where(allowed, 0.0, floor_score)


def each_count(windows, query, blocks, body):
    first = pick([w[0] for w in windows], query)
    count = pick([w[1] for w in windows], query)
    for fixed in range(1, blocks + 1):

        @pl.when(count == fixed)
        def _():
            body(first, fixed)


def attention_kernel(
    student, place_ref, other_ref, bias_ref, clip_in_ref, clip_ref, col_ref, row_ref, *refs
):
    if student:
        w_ref, part_ref, *c_refs = refs[:6]
        a_ref, rows_ref, qkv_ref, merged_ref, lse_ref, vt_ref, bias_at, score_ref, sum_ref = refs[6:]
    else:
        pieces, own_ref, c_refs, token_ref = refs[:4], refs[4], refs[5:9], refs[9]
        w_ref, qkv_ref, vt_ref, bias_at, score_ref, sum_ref = refs[10:]
        token_ref[...] = jnp.zeros_like(token_ref)
    half = qkv_ref.shape[2] // 2
    heads = qkv_ref.shape[1]
    cols = heads * HEAD_DIM
    size = QUERY_BLOCK
    blocks = 2 * half // size
    bf16, f32 = jnp.bfloat16, jnp.float32
    inputs = other_ref[0:half, :]
    if student:
        qkv_ref[:, :, 0:half, :] = part_ref[...]
        inputs = jnp.clip(inputs.astype(f32), -clip_in_ref[...], clip_in_ref[...]).astype(bf16)
        a_ref[...] = inputs
        rows_ref[...] = other_ref[0 : half // 4, :]
    else:
        place_projections(place_ref, pieces, w_ref, 3)
        write_heads(own_ref[...], w_ref, bias_ref, qkv_ref, 0)
    write_heads(inputs, w_ref, bias_ref, qkv_ref, half)
    eye = unit_matrix()
    for head in range(heads):
        vt_ref[head] = dot_nt(eye, qkv_ref[2, head]).astype(bf16)
    windows = block_window(row_ref, place_ref, blocks)
    mask = order_mask(place_ref)
    sum_ref[...] = jnp.zeros_like(sum_ref)

    def one_query(query, carry):
        at = pl.multiple_of(query * size, size)

        def body(first, count):
            keys = [(first + step) ^ mask for step in range(count)]
            starts = [pl.multiple_of(key * size, size) for key in keys]
            for step in range(count):
                bias_at[step] = pair_bias(col_ref, row_ref, query, keys[step])
            for head in range(heads):
                queries = qkv_ref[0, head, pl.ds(at, size), :]
                top = None
                for step in range(count):
                    scores = bias_at[step] + dot_nt(
                        qkv_ref[1, head, pl.ds(starts[step], size), :], queries
                    )
                    score_ref[step] = scores
                    part = jnp.max(scores, axis=0, keepdims=True)
                    top = part if top is None else jnp.maximum(top, part)
                total, merged = 0.0, 0.0
                for step in range(count):
                    weights = jnp.exp(score_ref[step] - top)
                    total = total + jnp.sum(weights, axis=0, keepdims=True)
                    merged = merged + dot_nn(
                        vt_ref[head, :, pl.ds(starts[step], size)], weights.astype(bf16)
                    )
                sum_ref[head * HEAD_DIM : (head + 1) * HEAD_DIM, :] = merged * (1.0 / total)
                if student:
                    lse_ref[head : head + 1, pl.ds(at, size)] = top + jnp.log(total)

        each_count(windows, query, blocks, body)
        if student:
            merged_ref[:, pl.ds(at, size)] = sum_ref[0:cols, :]
        merged = jnp.transpose(sum_ref[...])[:, :cols]
        if student:
            merged = clip_ref[...] * jnp.tanh(merged / clip_ref[...])
        merged = merged.astype(bf16)
        part = query >> 1
        share = size // 2
        for pair in range(2):

            @pl.when((query & 1) == pair)
            def _():
                c_refs[2 * pair][part] = merged[:share]
                c_refs[2 * pair + 1][part] = merged[share:]

        return carry

    lax.fori_loop(0, blocks, one_query, 0)


def attention_forward(student, place, other, weights, parts, bias, clip_in, clip, code_col, code_row):
    width = other.shape[1]
    half = parts.shape[2] if student else parts.shape[0]
    cols = weights[0].shape[-1]
    heads = cols // HEAD_DIM
    count = 2 * half
    bf16, f32 = jnp.bfloat16, jnp.float32
    qkv = (3, heads, count, HEAD_DIM)
    c_shape = (shaped((2, half // 4, cols), bf16),) * 4
    scratch = (
        pltpu.VMEM((heads, HEAD_DIM, count), bf16),
        pltpu.VMEM((count // QUERY_BLOCK, QUERY_BLOCK, QUERY_BLOCK), f32),
        pltpu.VMEM((count // QUERY_BLOCK, QUERY_BLOCK, QUERY_BLOCK), f32),
        pltpu.VMEM((256, QUERY_BLOCK), f32),
    )
    if student:
        outs = (
            *c_shape,
            shaped((half, width), bf16),
            shaped((half // 4, width), bf16),
            shaped(qkv, bf16),
            shaped((cols, count), f32),
            shaped((8, count), f32),
        )
        inputs = (weights, parts)
    else:
        outs = (*c_shape, shaped(TOKEN, f32))
        scratch = (pltpu.VMEM((3, width, cols), bf16), pltpu.VMEM(qkv, bf16), *scratch)
        inputs = (*weights, parts)
    return call_kernel(
        functools.partial(attention_kernel, student),
        place,
        (other, bias, clip_in, clip, code_col, code_row, *inputs),
        outs,
        scratch,
        flops=2 * half * width * cols * 3 + 4 * count * count * cols,
        moved=6 * count * width,
        exps=heads * count * count,
    )


def attention_pull_kernel(
    place_ref,
    qkv_ref,
    clip_ref,
    merged_ref,
    lse_ref,
    col_ref,
    row_ref,
    d0_ref,
    d1_ref,
    d2_ref,
    d3_ref,
    w_ref,
    keep_ref,
    send_ref,
    dproj_ref,
    sums_ref,
    grad_ref,
    kt_ref,
    dk_ref,
    dv_ref,
    sum_ref,
    delta_ref,
    bias_at,
):
    _, heads, count, _ = qkv_ref.shape
    cols = heads * HEAD_DIM
    size = QUERY_BLOCK
    share = size // 2
    blocks = count // size
    bf16, f32 = jnp.bfloat16, jnp.float32
    eye = unit_matrix()
    for head in range(heads):
        kt_ref[head] = dot_nt(eye, qkv_ref[1, head]).astype(bf16)
    for distance, source in enumerate((d0_ref, d1_ref, d2_ref, d3_ref)):
        for part in range(2):
            at = part * (count // 2) + distance * share
            merged = merged_ref[:, at : at + share]
            wide = jnp.concatenate([merged, jnp.zeros((256 - cols, share), f32)], axis=0)
            ratio = jnp.tanh(jnp.transpose(wide)[:, :cols] / clip_ref[...])
            grad = (source[part].astype(f32) * (1.0 - ratio * ratio)).astype(bf16)
            for head in range(heads):
                grad_ref[head, at : at + share, :] = grad[:, head * HEAD_DIM : (head + 1) * HEAD_DIM]
            wide = jnp.concatenate(
                [grad.astype(f32), jnp.zeros((share, 256 - cols), f32)], axis=1
            )
            turned = jnp.transpose(wide)[:cols] * merged
            for head in range(heads):
                delta_ref[head : head + 1, at : at + share] = jnp.sum(
                    turned[head * HEAD_DIM : (head + 1) * HEAD_DIM], axis=0, keepdims=True
                )
    dk_ref[...] = jnp.zeros_like(dk_ref)
    dv_ref[...] = jnp.zeros_like(dv_ref)
    windows = block_window(row_ref, place_ref, blocks)
    mask = order_mask(place_ref)
    sum_ref[...] = jnp.zeros_like(sum_ref)

    def one_query(query, carry):
        at = pl.multiple_of(query * size, size)

        def body(first, count):
            keys = [(first + step) ^ mask for step in range(count)]
            starts = [pl.multiple_of(key * size, size) for key in keys]
            for step in range(count):
                bias_at[step] = pair_bias(col_ref, row_ref, query, keys[step])
            for head in range(heads):
                queries = qkv_ref[0, head, pl.ds(at, size), :]
                grad = grad_ref[head, pl.ds(at, size), :]
                lse = lse_ref[head : head + 1, pl.ds(at, size)]
                delta = delta_ref[head : head + 1, pl.ds(at, size)]
                merged = 0.0
                for step in range(count):
                    rows = pl.ds(starts[step], size)
                    probs = jnp.exp(
                        dot_nt(qkv_ref[1, head, rows, :], queries) + (bias_at[step] - lse)
                    )
                    d_probs = dot_nt(qkv_ref[2, head, rows, :], grad)
                    d_scores = (probs * (d_probs - delta)).astype(bf16)
                    dv_ref[head, rows, :] += dot_nn(probs.astype(bf16), grad)
                    dk_ref[head, rows, :] += dot_nn(d_scores, queries)
                    merged = merged + dot_nn(kt_ref[head, :, rows], d_scores)
                sum_ref[head * HEAD_DIM : (head + 1) * HEAD_DIM, :] = merged

        each_count(windows, query, blocks, body)
        merged = jnp.transpose(sum_ref[...])[:, :cols] * (HEAD_DIM**-0.5)
        dproj_ref[0, pl.ds(at, size), :] = merged.astype(bf16)
        return carry

    lax.fori_loop(0, blocks, one_query, 0)
    for head in range(heads):
        lanes = slice(head * HEAD_DIM, (head + 1) * HEAD_DIM)
        dproj_ref[1, :, lanes] = dk_ref[head].astype(bf16)
        dproj_ref[2, :, lanes] = dv_ref[head].astype(bf16)
    sums_ref[0:1, :] = jnp.sum(dproj_ref[0].astype(f32), axis=0, keepdims=True)
    sums_ref[1:2, :] = jnp.sum(dproj_ref[2].astype(f32), axis=0, keepdims=True)
    for part in range(2):
        at = slice(part * (count // 2), (part + 1) * (count // 2))
        back = (
            dot_nt(dproj_ref[0, at, :], w_ref[0])
            + dot_nt(dproj_ref[1, at, :], w_ref[1])
            + dot_nt(dproj_ref[2, at, :], w_ref[2])
        ).astype(bf16)
        for distance in range(4):
            target = send_ref if distance & 1 else keep_ref
            target[distance >> 1, part] = back[distance * share : (distance + 1) * share]


def attention_backward(place, qkv, clip, merged, lse, code_col, code_row, grads, weights):
    _, heads, count, _ = qkv.shape
    cols = heads * HEAD_DIM
    width = weights.shape[1]
    bf16, f32 = jnp.bfloat16, jnp.float32
    return call_kernel(
        attention_pull_kernel,
        place,
        (qkv, clip, merged, lse, code_col, code_row, *grads, weights),
        (
            *(shaped((2, 2, count // 8, width), bf16),) * 2,
            shaped((3, count, cols), bf16),
            shaped((2, cols), f32),
        ),
        (
            pltpu.VMEM((heads, count, HEAD_DIM), bf16),
            pltpu.VMEM((heads, HEAD_DIM, count), bf16),
            pltpu.VMEM((heads, count, HEAD_DIM), f32),
            pltpu.VMEM((heads, count, HEAD_DIM), f32),
            pltpu.VMEM((256, QUERY_BLOCK), f32),
            pltpu.VMEM((8, count), f32),
            pltpu.VMEM((count // QUERY_BLOCK, QUERY_BLOCK, QUERY_BLOCK), f32),
        ),
        flops=2 * count * width * cols * 3 + 10 * count * count * cols,
        moved=8 * count * width,
        exps=heads * count * count,
    )


def unit_of(stream):
    mean = jnp.mean(stream, axis=-1, keepdims=True)
    centred = stream - mean
    scale = lax.rsqrt(jnp.mean(centred * centred, axis=-1, keepdims=True) + epsilon)
    return centred * scale, scale


def column_sum(value):
    return jnp.sum(value, axis=0, keepdims=True)


def dot_tn(left, right):
    return lax.dot_general(left, right, (((0,), (0,)), ((), ())), preferred_element_type=jnp.float32)


def out_norm_kernel(student, place_ref, *refs):
    if student:
        c_refs, pieces = refs[:4], refs[4:12]
        own_ref, other_ref, valid_ref, params_ref = refs[12:16]
        w_ref, unit_ref, scale_ref, low_ref, sums_ref, token_ref = refs[16:]
        token_ref[...] = jnp.zeros_like(token_ref)
    else:
        c_refs, w_ref = refs[:4], refs[4]
        own_ref, other_ref, valid_ref, params_ref, cot_ref = refs[5:10]
        wide_ref, low_ref = refs[10:]
    share = own_ref.shape[0]
    cols = c_refs[0].shape[2]
    size = w_ref.shape[1] // 4
    total = None
    for r, source in enumerate(c_refs):
        if student:
            group = pieces[:4] if r % 2 == 0 else pieces[4:]
            for distance, piece in zip((0, 2, 1, 3), group):
                start = pl.multiple_of((place_ref[0] ^ distance) * size, 64)
                w_ref[r, pl.ds(start, size), :] = piece[r >> 1, 2 * size : 3 * size, :]
            weights = w_ref[r, :, 0:cols]
        else:
            weights = w_ref[r, :, cols : 2 * cols]
        context = jnp.concatenate([source[0], source[1]], axis=0)
        term = dot_nt(context, weights)
        total = term if total is None else total + term
    attn = total + params_ref[0:1, :]
    stream = jnp.concatenate([own_ref[...], other_ref[...]], axis=0).astype(jnp.float32)
    unit, scale = unit_of(stream + attn)
    wide = unit * params_ref[2:3, :] + params_ref[3:4, :]
    low_ref[0 : 2 * share, :] = wide.astype(jnp.bfloat16)
    if student:
        unit_ref[...] = unit
        scale_ref[...] = scale
        valid = valid_ref[...]
        sums_ref[0:1, :] = column_sum(valid * jnp.ones_like(stream))
        sums_ref[1:2, :] = column_sum(valid * stream * stream)
        sums_ref[2:3, :] = column_sum(valid * attn * attn)
    else:
        wide_ref[...] = wide
        low_ref[2 * share :, :] = cot_ref[...]


def out_norm(student, place, contexts, weights, own, other, valid, params, cot=()):
    share, width = own.shape
    rows = 2 * share
    cols = contexts[0].shape[-1]
    f32, bf16 = jnp.float32, jnp.bfloat16
    if student:
        outs = (
            shaped((4, width, 2 * cols), bf16),
            shaped((rows, width), f32),
            shaped((rows, 1), f32),
            shaped((rows, width), bf16),
            shaped((3, width), f32),
            shaped(TOKEN, f32),
        )
    else:
        outs = (shaped((rows, width), f32), shaped((rows + share, width), bf16))
    return call_kernel(
        functools.partial(out_norm_kernel, student),
        place,
        (*contexts, *(weights if student else (weights,)), own, other, valid, params, *cot),
        outs,
        flops=2 * rows * width * cols * 4,
        moved=12 * rows * width,
    )


def gelu_parts(values):
    cdf = 0.5 * (1.0 + lax.erf(values * (2.0**-0.5)))
    return values * cdf, cdf


def hidden_kernel(student, assemble, far, place_ref, h_ref, *refs):
    refs = list(refs)
    pieces = [refs.pop(0) for _ in range(8 if assemble else 1)]
    with_terms = student and assemble
    terms_ref = None if with_terms else refs.pop(0)
    w_ref = refs.pop(0) if assemble else pieces[0]
    if with_terms:
        terms_ref = refs.pop(0)
    if student:
        hid_ref, slope_ref = refs.pop(0), refs.pop(0)
    part_ref, token_ref = refs
    token_ref[...] = jnp.zeros_like(token_ref)
    bf16 = jnp.bfloat16
    total = None
    inputs = h_ref[0 : part_ref.shape[0], :]
    for r in range(4):
        if assemble:
            group = pieces[:4] if r % 2 == 0 else pieces[4:]
            size = w_ref.shape[2] // 4
            for mat in range(2):
                for distance, piece in zip((0, 2, 1, 3), group):
                    start = pl.multiple_of((place_ref[0] ^ distance) * size, 64)
                    w_ref[r, mat, pl.ds(start, size), :] = piece[r >> 1, mat * size : (mat + 1) * size, :]
        if with_terms:
            terms_ref[r] = group[0][r >> 1, 3 * size : 3 * size + 16, :]
        terms = terms_ref[r].astype(jnp.float32)
        base = 0 if student else 6
        bias = terms[base : base + 1] + terms[base + 1 : base + 2] + terms[base + 2 : base + 3]
        upper = dot_nn(inputs, w_ref[r, 0]) + bias
        active, cdf = gelu_parts(upper)
        if student:
            clip = terms[3:4] + terms[4:5] + terms[5:6]
            ratio = jnp.tanh(active / clip)
            pdf = jnp.exp(-0.5 * upper * upper) * ((2.0 * math.pi) ** -0.5)
            slope_ref[r] = ((1.0 - ratio * ratio) * (cdf + upper * pdf)).astype(bf16)
            hidden = (clip * ratio).astype(bf16)
            hid_ref[r] = hidden
        else:
            hidden = active.astype(bf16)
        term = dot_nt(hidden, w_ref[r, 1])
        total = term if total is None else total + term
    part_ref[...] = total.astype(part_ref.dtype)


def hidden_layer(student, far, place, h, rows, weights, terms=None):
    width = h.shape[-1]
    half = weights[0].shape[-1] if isinstance(weights, tuple) else weights.shape[-1]
    f32, bf16 = jnp.float32, jnp.bfloat16
    assemble = isinstance(weights, tuple)
    outs = []
    if assemble:
        outs.append(shaped((4, 2, width, half), bf16))
        if student:
            outs.append(shaped((4, 16, half), bf16))
    if student:
        outs += [shaped((4, rows, half), bf16)] * 2
    outs += [shaped((rows, width), bf16 if far else f32), shaped(TOKEN, f32)]
    inputs = (h, *(weights if assemble else (weights,))) + (() if terms is None else (terms,))
    return call_kernel(
        functools.partial(hidden_kernel, student, assemble, far),
        place,
        inputs,
        tuple(outs),
        flops=2 * rows * width * half * 8,
        moved=8 * width * half * 2 + 16 * rows * half,
        exps=(3 if student else 1) * rows * half * 4,
    )


def loss_kernel(
    place_ref, unit_ref, ffn_ref, got_ref, ht_ref, ffnt_ref, gott_ref, cot_ref, cot_other_ref, valid_ref, params_ref, t_ref,
    layer_ref, dz_ref, low_ref, sums_ref,
):
    share = cot_ref.shape[0]
    rows = 2 * share
    f32, bf16 = jnp.float32, jnp.bfloat16
    h_one = unit_ref[...] * params_ref[2:3, :] + params_ref[3:4, :]
    ffn = ffn_ref[...] + got_ref[...].astype(f32) + params_ref[1:2, :]
    unit, scale = unit_of(h_one + ffn)
    out = unit * params_ref[4:5, :] + params_ref[5:6, :]
    low = out.astype(bf16)
    layer_ref[...] = low[:share]
    low_ref[rows:, :] = low[share:]
    t_unit, _ = unit_of(ht_ref[...] + ffnt_ref[...] + gott_ref[...].astype(f32) + t_ref[1:2, :])
    difference = out - (t_unit * t_ref[4:5, :] + t_ref[5:6, :])
    valid = valid_ref[...]
    gap = valid * difference
    arriving = jnp.concatenate([cot_ref[...], cot_other_ref[rows:, :]], axis=0).astype(f32)
    grad = arriving + gap
    inner = grad * params_ref[4:5, :]
    dz = scale * (
        inner
        - jnp.mean(inner, axis=-1, keepdims=True)
        - unit * jnp.mean(inner * unit, axis=-1, keepdims=True)
    )
    dz_ref[...] = dz
    dz_low = dz.astype(bf16)
    low_ref[0:rows, :] = dz_low
    sums_ref[0:1, :] = column_sum(dz_low.astype(f32))
    sums_ref[1:2, :] = column_sum(grad * unit)
    sums_ref[2:3, :] = column_sum(grad)
    sums_ref[3:4, :] = column_sum(valid * ffn * ffn)
    sums_ref[4:5, :] = column_sum(gap * difference)


def loss_step(place, unit, ffn, got, ht, ffnt, gott, cot, cot_other, valid, params, t_rows):
    rows, width = unit.shape
    share = cot.shape[0]
    f32, bf16 = jnp.float32, jnp.bfloat16
    return call_kernel(
        loss_kernel,
        place,
        (unit, ffn, got, ht, ffnt, gott, cot, cot_other, valid, params, t_rows),
        (
            shaped((share, width), bf16),
            shaped((rows, width), f32),
            shaped((rows + share, width), bf16),
            shaped((5, width), f32),
        ),
        flops=60 * rows * width,
        moved=30 * rows * width,
    )


def hidden_pull_kernel(place_ref, grad_ref, w_ref, slope_ref, du_ref, part_ref, sums_ref):
    grad = grad_ref[0 : part_ref.shape[0], :]
    total = None
    for r in range(4):
        upper = (dot_nn(grad, w_ref[r, 1]) * slope_ref[r].astype(jnp.float32)).astype(jnp.bfloat16)
        du_ref[r] = upper
        sums_ref[r : r + 1, :] = column_sum(upper.astype(jnp.float32))
        term = dot_nt(upper, w_ref[r, 0])
        total = term if total is None else total + term
    part_ref[...] = total.astype(part_ref.dtype)


def hidden_pull(far, place, grad, weights, slope):
    width = grad.shape[-1]
    rows = slope.shape[1]
    half = slope.shape[-1]
    f32, bf16 = jnp.float32, jnp.bfloat16
    return call_kernel(
        hidden_pull_kernel,
        place,
        (grad, weights, slope),
        (shaped((4, rows, half), bf16), shaped((rows, width), bf16 if far else f32), shaped((4, half), f32)),
        flops=2 * rows * width * half * 8,
        moved=8 * width * half * 2 + 16 * rows * half,
    )


def hidden_grads_kernel(mat, place_ref, l0, l1, r0, r1, keep_ref, send_ref, full_ref):
    rows = r0.shape[1]
    left = jnp.transpose(jnp.concatenate([l0[0:rows, :], l1[0:rows, :]], axis=0))
    size = full_ref.shape[0] // 4
    for r in range(4):
        right = jnp.concatenate([r0[r], r1[r]], axis=0)
        full_ref[...] = dot_nn(left, right)
        for slot in range(2):
            for target, distance in ((keep_ref, 2 * slot), (send_ref, 2 * slot + 1)):
                start = pl.multiple_of((place_ref[0] ^ distance) * size, 64)
                target[slot, r] = full_ref[pl.ds(start, size), :].astype(jnp.bfloat16)


def hidden_grads(place, left, right):
    width = left[0].shape[-1]
    rows, half = right[0].shape[1:]
    out = shaped((2, 4, width // 4, half), jnp.bfloat16)
    return call_kernel(
        functools.partial(hidden_grads_kernel, 0),
        place,
        (*left, *right),
        (out, out),
        (pltpu.VMEM((width, half), jnp.float32),),
        flops=16 * rows * width * half * 4,
        moved=8 * width * half * 2,
    )


def first_pull_kernel(place_ref, dz_ref, part_ref, got_ref, unit_ref, scale_ref, params_ref, w_ref, first_ref, low_ref, sums_ref, *ctx_refs):
    f32, bf16 = jnp.float32, jnp.bfloat16
    grad = dz_ref[...] + part_ref[...] + got_ref[...].astype(f32)
    unit = unit_ref[...]
    inner = grad * params_ref[2:3, :]
    first = scale_ref[...] * (
        inner
        - jnp.mean(inner, axis=-1, keepdims=True)
        - unit * jnp.mean(inner * unit, axis=-1, keepdims=True)
    )
    first_ref[...] = first
    low = first.astype(bf16)
    low_ref[...] = low
    sums_ref[0:1, :] = column_sum(low.astype(f32))
    sums_ref[1:2, :] = column_sum(grad * unit)
    sums_ref[2:3, :] = column_sum(grad)
    share, cols = ctx_refs[0].shape[1:]
    for r in range(4):
        back = dot_nn(low, w_ref[r, :, 0:cols]).astype(bf16)
        ctx_refs[r][0] = back[:share]
        ctx_refs[r][1] = back[share:]


def first_pull(place, dz, part, got, unit, scale, params, weights):
    rows, width = dz.shape
    cols = weights.shape[-1] // 2
    f32, bf16 = jnp.float32, jnp.bfloat16
    return call_kernel(
        first_pull_kernel,
        place,
        (dz, part, got, unit, scale, params, weights),
        (
            shaped((rows, width), f32),
            shaped((rows, width), bf16),
            shaped((3, width), f32),
            *(shaped((2, rows // 2, cols), bf16),) * 4,
        ),
        flops=2 * rows * width * cols * 4,
        moved=20 * rows * width,
    )


def last_grads_kernel(place_ref, low_ref, c0, c1, c2, c3, a_ref, a_other_ref, d_ref, qv_ref, keep_ref, send_ref, full_ref):
    size = full_ref.shape[0] // 4
    half = a_ref.shape[0]
    low = jnp.transpose(low_ref[...])
    own, other = jnp.transpose(a_ref[...]), jnp.transpose(a_other_ref[...])
    for entry in range(7):
        if entry < 4:
            source = (c0, c1, c2, c3)[entry]
            full_ref[...] = dot_nn(low, jnp.concatenate([source[0], source[1]], axis=0))
        else:
            full_ref[...] = dot_nn(own, d_ref[entry - 4, 0:half, :]) + dot_nn(
                other, d_ref[entry - 4, half:, :]
            )
        for slot in range(2):
            for target, distance in ((keep_ref, 2 * slot), (send_ref, 2 * slot + 1)):
                start = pl.multiple_of((place_ref[0] ^ distance) * size, 64)
                target[slot, entry * size : (entry + 1) * size, :] = full_ref[
                    pl.ds(start, size), :
                ].astype(jnp.bfloat16)
    sums = jnp.concatenate([qv_ref[...], jnp.zeros((14, qv_ref.shape[1]), jnp.float32)], axis=0)
    for slot in range(2):
        for target in (keep_ref, send_ref):
            target[slot, 7 * size :, :] = sums.astype(jnp.bfloat16)


def last_grads(place, low, contexts, a_in, d_proj, d_bias_qv):
    rows, width = low.shape
    count = d_proj.shape[1]
    cols = d_proj.shape[-1]
    out = shaped((2, 7 * (width // 4) + 16, cols), jnp.bfloat16)
    return call_kernel(
        last_grads_kernel,
        place,
        (low, *contexts, *a_in, d_proj, d_bias_qv),
        (out, out),
        (pltpu.VMEM((width, cols), jnp.float32),),
        flops=2 * (4 * rows + 3 * count) * width * cols,
        moved=4 * count * width,
    )


def input_kernel(place_ref, first_ref, b0, b1, b2, own_ref, other_ref, clip_ref, mine_ref, other_out_ref):
    f32 = jnp.float32
    share = own_ref.shape[0]
    for part, (source, target) in enumerate(((own_ref, mine_ref), (other_ref, other_out_ref))):
        through = b0[0, part].astype(f32) + b1[0, part].astype(f32) + b2[part].astype(f32)
        inside = jnp.abs(source[...].astype(f32)) < clip_ref[...]
        first = first_ref[part * share : (part + 1) * share, :]
        target[...] = (first + jnp.where(inside, through, 0.0)).astype(target.dtype)


def input_rows(place, first, backs, own, other, clip_in):
    share, width = own.shape
    return call_kernel(
        input_kernel,
        place,
        (first, *backs, own, other, clip_in),
        (shaped((share, width), jnp.float32), shaped((share, width), jnp.bfloat16)),
        flops=10 * share * width,
        moved=20 * share * width,
    )


def vector_kernel(place_ref, third_ref, second_ref, first_ref, own_ref, far_ref, out_ref):
    half = own_ref.shape[1]
    out_ref[...] = jnp.zeros_like(out_ref)
    out_ref[0:3, :] = third_ref[...]
    out_ref[3:8, :] = second_ref[...]
    out_ref[8:11, :] = first_ref[...]
    for r in range(4):
        part = own_ref[r : r + 1, :] + far_ref[r : r + 1, :]
        nothing = jnp.zeros_like(part)
        left = jnp.where(place_ref[2] == 0, part, nothing)
        right = jnp.where(place_ref[2] == 0, nothing, part)
        out_ref[pl.ds(11 + (place_ref[1] ^ r), 1), :] = jnp.concatenate([left, right], axis=1)


def vector_rows(place, third, second, first, own, far):
    width = third.shape[1]
    return call_kernel(
        vector_kernel,
        place,
        (third, second, first, own, far),
        shaped((16, width), jnp.float32),
        flops=1,
        moved=1,
    )


def swap_ctx(value):
    return lax.ppermute(value, "ctx", [(0, 1), (1, 0)])


def swap_core(value):
    return lax.ppermute(value, "fsdp", [(i, i ^ 1) for i in range(4)])


def swap_row(value):
    return lax.ppermute(value, "fsdp", [(i, i ^ 2) for i in range(4)])


def swap_tp(value, distance):
    return lax.ppermute(value, "tp", [(i, i ^ distance) for i in range(4)])


def fsdp_pieces(piece):
    far = swap_row(piece)
    return (piece, far, swap_core(piece), swap_core(far))


def exchange_tp(entries):
    return [entries[0]] + [swap_tp(entries[r], r) for r in (1, 2, 3)]


def three_terms(value):
    high = lax.reduce_precision(value, 8, 7)
    rest = value - high
    middle = lax.reduce_precision(rest, 8, 7)
    return [high.astype(jnp.bfloat16), middle.astype(jnp.bfloat16), (rest - middle).astype(jnp.bfloat16)]


def tie(values, *others):
    return lax.optimization_barrier((values, others))[0]


def once(place, *arrays):
    return (place, arrays)


def paired_body(
    tokens,
    cotangent,
    segment_ids,
    valid_mask,
    latent_qkv,
    latent_out,
    latent_up,
    latent_down,
    qkv_quant,
    up_quant,
    out_quant,
    down_quant,
    bias_qv,
    bias_up,
    row_params,
    clip_in,
    clip_ctx,
    clip_hidden,
    t_qkv,
    t_out,
    t_up,
    t_down,
    t_bias_qv,
    t_bias_up,
    t_rows,
):
    local_len, seq_count, width = tokens.shape
    share = cotangent.shape[0]
    col_width = latent_qkv.shape[2]
    hidden_width = latent_up.shape[1]
    half_hidden = hidden_width // 2
    row_width = latent_qkv.shape[0]
    tp_rank = lax.axis_index("tp")
    ctx_rank = lax.axis_index("ctx")
    fsdp_rank = lax.axis_index("fsdp")
    f32, bf16 = jnp.float32, jnp.bfloat16
    place = jnp.stack([fsdp_rank, tp_rank, ctx_rank]).astype(jnp.int32)

    def by_distance(value):
        pairs = value.reshape(2, 2, *value.shape[1:])
        pairs = jnp.where((tp_rank & 1) > 0, pairs[:, ::-1], pairs)
        pairs = jnp.where((tp_rank >> 1) > 0, pairs[::-1], pairs)
        return pairs.reshape(value.shape)

    def mine(value, axis):
        return lax.dynamic_index_in_dim(value, ctx_rank, axis, keepdims=False)

    def theirs(value, axis):
        return lax.dynamic_index_in_dim(value, 1 - ctx_rank, axis, keepdims=False)

    def half_of(weight):
        return jnp.where(ctx_rank == 0, weight[..., :half_hidden], weight[..., half_hidden:])

    def add(left, right):
        return left.astype(f32) + right.astype(f32)

    rows = 2 * share
    bin_up = binarize(latent_up, up_quant[0][None], up_quant[1][None])
    bin_down = binarize(latent_down, down_quant[0][:, None], down_quant[1][:, None])
    terms = [term for v in (bias_up, clip_hidden, t_bias_up) for term in three_terms(half_of(v))]
    vectors = jnp.pad(jnp.stack(terms), ((0, 16 - len(terms)), (0, 0)))
    bin_out = binarize(latent_out, out_quant[0][:, None], out_quant[1][:, None])
    piece = jnp.concatenate(
        [
            half_of(bin_up),
            half_of(bin_down),
            jnp.concatenate([bin_out, t_out], axis=1),
            vectors,
        ],
        axis=0,
    )
    piece_two = swap_tp(piece, 2)
    rows = 2 * share
    tokens_then, segment_then = tie((tokens, segment_ids), piece)
    relative = by_distance(tokens_then.reshape(4, share, seq_count, width))
    own = mine(relative, 2).reshape(local_len, width)
    code = by_distance(
        jnp.transpose(segment_then * 2 + (valid_mask > 0).astype(jnp.int32)).reshape(
            4, share, seq_count
        )
    )
    code_sent = jnp.pad(theirs(code, 2).reshape(1, local_len), ((0, 15), (0, width - local_len)))
    tokens_sent = jnp.concatenate(
        [theirs(relative, 2).reshape(local_len, width), code_sent.astype(bf16)], axis=0
    )
    other = swap_ctx(tokens_sent)
    latent_qkv_then, t_qkv = tie((latent_qkv, t_qkv), tokens_sent)
    bin_qkv = jnp.transpose(
        binarize(latent_qkv_then, qkv_quant[0][None], qkv_quant[1][None]), (1, 0, 2)
    )
    qkv_piece = jnp.concatenate([bin_qkv, jnp.transpose(t_qkv, (1, 0, 2))], axis=0)
    qkv_pieces = fsdp_pieces(qkv_piece)
    t_up, t_down = tie((t_up, t_down), qkv_piece)
    teacher_piece = jnp.concatenate([half_of(t_up), half_of(t_down)], axis=0)
    clip_in_row, clip_row = clip_in[None], clip_ctx[None]

    full_qkv, a_own, qkv_own, token = project_own(place, own, qkv_pieces, bias_qv, clip_in_row)
    other = tie(other, token)
    code_all = jnp.concatenate(
        [mine(code, 2).reshape(local_len), other[local_len, :local_len].astype(jnp.int32)]
    )
    code_col, code_row = code_all[:, None], code_all[None, :]
    valid = (
        jnp.concatenate([code_all[:share], code_all[local_len : local_len + share]]) & 1
    ).astype(f32)[:, None]
    even = jnp.stack([piece, tie(piece_two, token)])
    odd, even_row = swap_tp(even, 1), swap_row(even)
    *context, a_other, other_rows, qkv, merged, lse = attention_forward(
        True, once(place, even, token), other, full_qkv, qkv_own, bias_qv, clip_in_row,
        clip_row, code_col, code_row,
    )
    contexts = exchange_tp(context)
    odd, even_row = tie((odd, even_row), lse)
    even_cores = (swap_core(even), swap_core(even_row))
    odd_row = swap_row(odd)
    *teacher_context, token = attention_forward(
        False, once(place, lse, *even_cores), other, qkv_pieces, own,
        t_bias_qv, clip_in_row, clip_row, code_col, code_row,
    )
    token = gate(place, token, *contexts[1:])
    odd, odd_row, teacher_piece = tie((odd, odd_row, teacher_piece), token)
    teacher_two = swap_tp(teacher_piece, 2)
    pieces = (
        even, even_row, *even_cores,
        odd, odd_row, swap_core(odd), swap_core(odd_row),
    )
    own_rows = own[:share]
    out_full, unit, scale, h_low, first_sums, token = out_norm(
        True, once(place, token), contexts, pieces, own_rows, other_rows, valid, row_params
    )
    h_far = swap_ctx(h_low)
    teacher_contexts = exchange_tp(teacher_context)
    hidden_full, terms, hid_own, slope_own, part_own, _ = hidden_layer(
        True, False, once(place, token), h_low, rows, pieces
    )
    teacher_even = jnp.stack([teacher_piece, tie(teacher_two, terms)])
    teacher_odd, teacher_even_row = swap_tp(teacher_even, 1), swap_row(teacher_even)
    cot_own = mine(cotangent, 1)
    h_teacher, ht_low = out_norm(
        False, once(place, part_own), teacher_contexts, out_full, own_rows, other_rows, valid, t_rows,
        (theirs(cotangent, 1),),
    )
    ht_far = swap_ctx(ht_low)
    hid_far, slope_far, part_far, token = hidden_layer(
        True, True, once(place, ht_low), h_far, rows, hidden_full, terms
    )
    part_got = swap_ctx(part_far)
    teacher_even_row, teacher_odd = tie((teacher_even_row, teacher_odd), token)
    teacher_odd_row = swap_row(teacher_odd)
    teacher_hidden = (
        teacher_even, teacher_even_row, swap_core(teacher_even), swap_core(teacher_even_row),
        teacher_odd, teacher_odd_row, swap_core(teacher_odd), swap_core(teacher_odd_row),
    )
    teacher_full, t_part_far, _ = hidden_layer(
        False, True, once(place, token), ht_far, rows, teacher_hidden, terms
    )
    t_part_got = swap_ctx(t_part_far)
    t_part_own, _ = hidden_layer(
        False, False, once(place, t_part_far), ht_low, rows, teacher_full, terms
    )
    layer_own, d_second, d_ffn, second_sums = loss_step(
        place, unit, part_own, part_got, h_teacher, t_part_own, t_part_got,
        cot_own, ht_far, valid, row_params, t_rows,
    )

    def home(own_part, other_part):
        got = other_part.astype(own_part.dtype)
        first = jnp.where(ctx_rank == 0, own_part, got)
        second = jnp.where(ctx_rank == 0, got, own_part)
        return jnp.stack([first, second], axis=1)

    d_ffn_far = swap_ctx(d_ffn)
    layer_out = home(layer_own, d_ffn_far[rows:])
    du_own, d_part_own, du_sums_own = hidden_pull(False, place, d_ffn, hidden_full, slope_own)
    du_far, d_part_far, du_sums_far = hidden_pull(True, place, d_ffn_far, hidden_full, slope_far)
    d_part_got = swap_ctx(d_part_far)
    keep_down, send_down = hidden_grads(
        once(place, du_sums_far), (d_ffn, d_ffn_far), (hid_own, hid_far)
    )
    got_down = swap_core(send_down)
    leave_down = add(keep_down[1], got_down[1]).astype(bf16)
    d_first, d_attn, third_sums, *d_context = first_pull(
        once(place, send_down), d_second, d_part_own, d_part_got, unit, scale, row_params, out_full
    )
    d_contexts = exchange_tp(d_context)
    keep_up, send_up = hidden_grads(once(place, third_sums), (h_low, h_far), (du_own, du_far))
    got_up = swap_core(send_up)
    leave_up = add(keep_up[1], got_up[1]).astype(bf16)
    vector = vector_rows(place, third_sums, second_sums, first_sums, du_sums_own, du_sums_far)
    keep_back, send_back, d_proj, d_bias_qv = attention_backward(
        once(place, leave_down, leave_up, vector),
        qkv, clip_row, merged, lse, code_col, code_row, d_contexts, full_qkv,
    )
    got_back = swap_tp(send_back, 1)
    got_down_row, got_up_row = tie((swap_row(leave_down), swap_row(leave_up)), d_bias_qv)
    row_down = add(add(keep_down[0], got_down[0]), got_down_row)
    row_up = add(add(keep_up[0], got_up[0]), got_up_row)
    keep_last, send_last = last_grads(
        once(place, send_back, got_down_row, got_up_row),
        d_attn, contexts, (a_own, a_other), d_proj, d_bias_qv,
    )
    got_last, vector_got = swap_core(send_last), swap_core(tie(vector, send_last))
    got_back = tie(got_back, send_last)
    leave_back = add(keep_back[1], got_back[1]).astype(bf16)
    got_back_two = swap_tp(leave_back, 2)
    vector = tie(vector + vector_got, leave_back)
    vector_got = swap_ctx(vector)
    send_both = tie(jnp.stack([row_down[1::2], row_up[1::2]]).astype(bf16), leave_back)
    got_both = swap_tp(send_both, 1)
    leave_last = tie(add(keep_last[1], got_last[1]).astype(bf16), leave_back)
    got_last_row = swap_row(leave_last)
    vector = tie(vector + vector_got, leave_last)
    vector_got = swap_row(vector)
    entry = row_width
    row_last = add(add(keep_last[0], got_last[0]), got_last_row)
    send_one = jnp.stack([row_last[entry : 2 * entry], row_last[3 * entry : 4 * entry]]).astype(bf16)
    got_one = swap_tp(send_one, 1)
    leave_both = tie(
        jnp.stack([add(row_down[2], got_both[0, 1]), add(row_up[2], got_both[1, 1])]).astype(bf16), send_one
    )
    got_both_two = swap_tp(leave_both, 2)
    vector = tie(vector + vector_got, leave_both)
    vector_got = swap_tp(vector, 1)
    input_own, input_other = input_rows(
        once(place, leave_both), d_first, (keep_back, got_back, got_back_two), own_rows, other_rows, clip_in_row
    )
    input_grad = home(input_own, swap_ctx(input_other))
    leave_two = add(row_last[2 * entry : 3 * entry], got_one[1]).astype(bf16)
    got_two = swap_tp(leave_two, 2)
    low_both = add(
        jnp.stack([add(row_down[0], got_both[0, 0]), add(row_up[0], got_both[1, 0])]), got_both_two
    ).astype(bf16)
    low_out = add(add(row_last[0:entry], got_one[0]), got_two)
    low_last = jnp.concatenate([low_out, row_last[4 * entry :]], axis=0).astype(bf16)
    sum_last = add(low_last, swap_ctx(low_last))
    vector = tie(vector + vector_got, low_both)
    vector = vector + swap_tp(vector, 2)

    both_far = swap_ctx(low_both)
    grad_both = jnp.concatenate(
        [
            jnp.where(ctx_rank == 0, low_both, both_far),
            jnp.where(ctx_rank == 0, both_far, low_both),
        ],
        axis=-1,
    ).astype(f32)
    grad_up = straight(grad_both[1], latent_up, up_quant[0][None], up_quant[1][None])
    grad_down = straight(
        grad_both[0], latent_down, down_quant[0][:, None], down_quant[1][:, None]
    )
    grad_qkv = straight(
        jnp.transpose(sum_last[entry : 4 * entry].reshape(3, row_width, col_width), (1, 0, 2)),
        latent_qkv,
        qkv_quant[0][None],
        qkv_quant[1][None],
    )
    grad_out = straight(sum_last[0:entry], latent_out, out_quant[0][:, None], out_quant[1][:, None])
    grad_qv = sum_last[4 * entry : 4 * entry + 2]
    vector_sums = jnp.concatenate([vector[0:1], vector[3:4], vector[1:3], vector[4:6]], axis=0)
    stat_sums = jnp.sum(vector[6:11], axis=-1)
    grad_rows = lax.dynamic_slice_in_dim(vector_sums, fsdp_rank * row_width, row_width, 1)
    grad_bias_up = lax.dynamic_index_in_dim(vector, 11 + tp_rank, 0, keepdims=False)
    denom = stat_sums[2]
    statistics = jnp.stack(
        [
            jnp.sqrt(stat_sums[3] / denom),
            jnp.sqrt(stat_sums[4] / denom),
            jnp.sqrt(stat_sums[0] / denom),
            stat_sums[1] / denom,
        ]
    )
    return (
        layer_out,
        input_grad,
        grad_qkv,
        grad_out,
        grad_up,
        grad_down,
        grad_rows,
        grad_qv,
        grad_bias_up,
        statistics,
    )


def general_body(
    tokens,
    cotangent,
    segment_ids,
    valid_mask,
    latent_qkv,
    latent_out,
    latent_up,
    latent_down,
    qkv_quant,
    up_quant,
    out_quant,
    down_quant,
    bias_qv,
    bias_up,
    row_params,
    clip_in,
    clip_ctx,
    clip_hidden,
    t_qkv,
    t_out,
    t_up,
    t_down,
    t_bias_qv,
    t_bias_up,
    t_rows,
):
    local_len, seq_count, width = tokens.shape
    share = cotangent.shape[0]
    col_width = latent_qkv.shape[2]
    hidden_width = latent_up.shape[1]
    row_width = latent_qkv.shape[0]
    local_heads = col_width // HEAD_DIM
    scale = HEAD_DIM ** (-0.5)
    tp_rank = lax.axis_index("tp")
    ctx_rank = lax.axis_index("ctx")
    fsdp_rank = lax.axis_index("fsdp")
    full_len = local_len * lax.axis_size("ctx")
    bin_qkv = binarize(latent_qkv, qkv_quant[0][None], qkv_quant[1][None])
    bin_out = binarize(latent_out, out_quant[0][:, None], out_quant[1][:, None])
    bin_up = binarize(latent_up, up_quant[0][None], up_quant[1][None])
    bin_down = binarize(latent_down, down_quant[0][:, None], down_quant[1][:, None])
    gathered = (
        lax.all_gather(bin_qkv, "fsdp", axis=0, tiled=True),
        lax.all_gather(bin_out, "fsdp", axis=0, tiled=True),
        lax.all_gather(bin_up, "fsdp", axis=0, tiled=True),
        lax.all_gather(bin_down, "fsdp", axis=0, tiled=True),
        lax.all_gather(t_qkv, "fsdp", axis=0, tiled=True),
        lax.all_gather(t_out, "fsdp", axis=0, tiled=True),
        lax.all_gather(t_up, "fsdp", axis=0, tiled=True),
        lax.all_gather(t_down, "fsdp", axis=0, tiled=True),
    )
    full_qkv, full_out, full_up, full_down, teach_qkv, teach_out, teach_up, teach_down = gathered
    stream = tokens.astype(jnp.float32)
    a_in = jnp.clip(stream, -clip_in, clip_in).astype(jnp.bfloat16)
    proj_student = jnp.einsum("tsd,dkh->tskh", a_in, full_qkv, preferred_element_type=jnp.float32)
    proj_teacher = jnp.einsum(
        "tsd,dkh->tskh", tokens, teach_qkv, preferred_element_type=jnp.float32
    )
    student_q = (proj_student[:, :, 0] + bias_qv[0]).astype(jnp.bfloat16)
    student_k = proj_student[:, :, 1].astype(jnp.bfloat16)
    student_v = (proj_student[:, :, 2] + bias_qv[1]).astype(jnp.bfloat16)
    teacher_q = (proj_teacher[:, :, 0] + t_bias_qv[0]).astype(jnp.bfloat16)
    teacher_k = proj_teacher[:, :, 1].astype(jnp.bfloat16)
    teacher_v = (proj_teacher[:, :, 2] + t_bias_qv[1]).astype(jnp.bfloat16)
    student_queries = headed(student_q)
    teacher_queries = headed(teacher_q)
    query_pos = ctx_rank * local_len + jnp.arange(local_len, dtype=jnp.int32)
    key_tags = jnp.transpose(jnp.where(valid_mask > 0, segment_ids, -1))
    empty_state = (
        jnp.full((seq_count, local_heads, local_len), floor_score, jnp.float32),
        jnp.zeros((seq_count, local_heads, local_len), jnp.float32),
        jnp.zeros((seq_count, local_heads, local_len, HEAD_DIM), jnp.float32),
    )
    buffers = (
        jnp.zeros((full_len, seq_count, col_width), jnp.bfloat16),
        jnp.zeros((full_len, seq_count, col_width), jnp.bfloat16),
        jnp.zeros((full_len, seq_count), jnp.int32),
    )
    carry = (empty_state, empty_state, buffers)
    pieces = (
        lax.all_gather(student_k, "ctx", axis=0, tiled=True),
        lax.all_gather(student_v, "ctx", axis=0, tiled=True),
        lax.all_gather(teacher_k, "ctx", axis=0, tiled=True),
        lax.all_gather(teacher_v, "ctx", axis=0, tiled=True),
        lax.all_gather(key_tags, "ctx", axis=0, tiled=True),
    )
    start = jnp.int32(0)
    count = pieces[0].shape[0]
    block = key_block(count)

    def inner(states, index):
        offset = index * block
        parts = [lax.dynamic_slice_in_dim(piece, offset, block, 0) for piece in pieces]
        key_pos = offset + jnp.arange(block, dtype=jnp.int32)
        allowed = allowed_pairs(segment_ids, query_pos, parts[4], key_pos)
        states = (
            online_step(
                states[0], student_queries, headed(parts[0]), headed(parts[1]), allowed, scale
            ),
            online_step(
                states[1], teacher_queries, headed(parts[2]), headed(parts[3]), allowed, scale
            ),
        )
        return (states, None)

    states, _ = lax.scan(inner, (carry[0], carry[1]), jnp.arange(count // block, dtype=jnp.int32))
    kept = tuple(
        (
            lax.dynamic_update_slice_in_dim(buffer, piece, start, 0)
            for buffer, piece in zip(carry[2], (pieces[0], pieces[1], pieces[4]))
        )
    )
    student_state, teacher_state, kept = (states[0], states[1], kept)
    attended, log_total = finish(student_state)
    teacher_attended, _ = finish(teacher_state)
    attended_flat = attended.reshape(local_len, seq_count, col_width)
    ctx_ratio = jnp.tanh(attended_flat / clip_ctx)
    context = (clip_ctx * ctx_ratio).astype(jnp.bfloat16)
    teacher_context = teacher_attended.reshape(local_len, seq_count, col_width).astype(jnp.bfloat16)
    rows_student = context
    rows_teacher = teacher_context
    attn_both = lax.psum_scatter(
        jnp.concatenate(
            [
                jnp.einsum(
                    "tsh,dh->tsd", rows_student, full_out, preferred_element_type=jnp.float32
                ),
                jnp.einsum(
                    "tsh,dh->tsd", rows_teacher, teach_out, preferred_element_type=jnp.float32
                ),
            ],
            axis=-1,
        ).astype(jnp.bfloat16),
        "tp",
        scatter_dimension=0,
        tiled=True,
    ).astype(jnp.float32)
    attn_student = attn_both[..., :width] + row_params[0]
    attn_teacher = attn_both[..., width:] + t_rows[0]
    stream_rows = lax.dynamic_slice_in_dim(stream, tp_rank * share, share, 0)
    first_sum = stream_rows + attn_student
    h_one = layer_norm(first_sum, row_params[2], row_params[3])
    h_teacher = layer_norm(stream_rows + attn_teacher, t_rows[2], t_rows[3])
    h_full, h_teacher_full = (
        lax.all_gather(h_one.astype(jnp.bfloat16), "tp", axis=0, tiled=True),
        lax.all_gather(h_teacher.astype(jnp.bfloat16), "tp", axis=0, tiled=True),
    )
    upper = jnp.einsum("tsd,df->tsf", h_full, full_up, preferred_element_type=jnp.float32) + bias_up
    activated = exact_gelu(upper)
    hid_ratio = jnp.tanh(activated / clip_hidden)
    hidden = (clip_hidden * hid_ratio).astype(jnp.bfloat16)
    upper_teacher = (
        jnp.einsum("tsd,df->tsf", h_teacher_full, teach_up, preferred_element_type=jnp.float32)
        + t_bias_up
    )
    hidden_teacher = exact_gelu(upper_teacher).astype(jnp.bfloat16)
    rows_student = hidden
    rows_teacher = hidden_teacher
    ffn_both = lax.psum_scatter(
        jnp.concatenate(
            [
                jnp.einsum(
                    "tsf,df->tsd", rows_student, full_down, preferred_element_type=jnp.float32
                ),
                jnp.einsum(
                    "tsf,df->tsd", rows_teacher, teach_down, preferred_element_type=jnp.float32
                ),
            ],
            axis=-1,
        ).astype(jnp.bfloat16),
        "tp",
        scatter_dimension=0,
        tiled=True,
    ).astype(jnp.float32)
    ffn_student = ffn_both[..., :width] + row_params[1]
    ffn_teacher = ffn_both[..., width:] + t_rows[1]
    second_sum = h_one + ffn_student
    out = layer_norm(second_sum, row_params[4], row_params[5])
    teacher_out = layer_norm(h_teacher + ffn_teacher, t_rows[4], t_rows[5])
    layer_out = out.astype(jnp.bfloat16)
    valid_rows = jnp.transpose(
        lax.dynamic_slice_in_dim(valid_mask, tp_rank * share, share, 1)
    ).astype(jnp.float32)[..., None]
    difference = out - teacher_out
    grad_out_total = cotangent.astype(jnp.float32) + valid_rows * difference
    stat_terms = jnp.stack(
        [
            jnp.sum(valid_rows) + 0.0 * jnp.sum(stream_rows[:1, :1, :1]),
            jnp.sum(valid_rows * stream_rows * stream_rows),
            jnp.sum(valid_rows * attn_student * attn_student),
            jnp.sum(valid_rows * ffn_student * ffn_student),
            jnp.sum(valid_rows * difference * difference),
        ]
    )
    _, second_pull = jax.vjp(layer_norm, second_sum, row_params[4], row_params[5])
    d_second, d_gain_two, d_bias_two = second_pull(grad_out_total)
    d_ffn = d_second.astype(jnp.bfloat16)
    d_bias_down = jnp.sum(d_ffn.astype(jnp.float32), axis=(0, 1))
    d_ffn_full = lax.all_gather(d_ffn, "tp", axis=0, tiled=True)
    grad_bin_down = jnp.einsum(
        "tsd,tsf->df", d_ffn_full, hidden, preferred_element_type=jnp.float32
    )
    d_hidden = jnp.einsum("tsd,df->tsf", d_ffn_full, full_down, preferred_element_type=jnp.float32)
    d_hidden = d_hidden * (1.0 - hid_ratio * hid_ratio)
    _, gelu_pull = jax.vjp(exact_gelu, upper)
    d_upper = gelu_pull(d_hidden)[0].astype(jnp.bfloat16)
    d_bias_up = jnp.sum(d_upper.astype(jnp.float32), axis=(0, 1))
    grad_bin_up = jnp.einsum("tsd,tsf->df", h_full, d_upper, preferred_element_type=jnp.float32)
    rows = d_upper
    d_h_one = d_second + lax.psum_scatter(
        jnp.einsum("tsf,df->tsd", rows, full_up, preferred_element_type=jnp.float32).astype(
            jnp.bfloat16
        ),
        "tp",
        scatter_dimension=0,
        tiled=True,
    ).astype(jnp.float32)
    _, first_pull = jax.vjp(layer_norm, first_sum, row_params[2], row_params[3])
    d_first, d_gain_one, d_bias_one = first_pull(d_h_one)
    d_attn = d_first.astype(jnp.bfloat16)
    d_bias_out = jnp.sum(d_attn.astype(jnp.float32), axis=(0, 1))
    d_attn_full = lax.all_gather(d_attn, "tp", axis=0, tiled=True)
    grad_bin_out = jnp.einsum(
        "tsd,tsh->dh", d_attn_full, context, preferred_element_type=jnp.float32
    )
    d_context = jnp.einsum("tsd,dh->tsh", d_attn_full, full_out, preferred_element_type=jnp.float32)
    d_attended = (d_context * (1.0 - ctx_ratio * ctx_ratio)).astype(jnp.bfloat16)
    d_attended_heads = headed(d_attended)
    delta = jnp.transpose(
        jnp.sum(d_attended_heads.astype(jnp.float32) * attended, axis=-1), (1, 2, 0)
    )
    key_all, value_all, tag_all = kept
    back_block = key_block(full_len)

    def back_step(grad_q, index):
        offset = index * back_block
        keys = headed(lax.dynamic_slice_in_dim(key_all, offset, back_block, 0))
        values = headed(lax.dynamic_slice_in_dim(value_all, offset, back_block, 0))
        block_tags = lax.dynamic_slice_in_dim(tag_all, offset, back_block, 0)
        key_pos = offset + jnp.arange(back_block, dtype=jnp.int32)
        allowed = allowed_pairs(segment_ids, query_pos, block_tags, key_pos)
        current = grad_q
        scores = (
            jnp.einsum("tshe,kshe->shtk", student_queries, keys, preferred_element_type=jnp.float32)
            * scale
        )
        probs = jnp.where(allowed, jnp.exp(scores - log_total[..., None]), 0.0)
        d_probs = jnp.einsum(
            "tshe,kshe->shtk", d_attended_heads, values, preferred_element_type=jnp.float32
        )
        d_scores = (probs * (d_probs - delta[..., None])).astype(jnp.bfloat16)
        current = (
            current
            + jnp.einsum("shtk,kshe->shte", d_scores, keys, preferred_element_type=jnp.float32)
            * scale
        )
        grad_k = (
            jnp.einsum(
                "shtk,tshe->kshe", d_scores, student_queries, preferred_element_type=jnp.float32
            )
            * scale
        )
        grad_v = jnp.einsum(
            "shtk,tshe->kshe",
            probs.astype(jnp.bfloat16),
            d_attended_heads,
            preferred_element_type=jnp.float32,
        )
        joined = jnp.concatenate(
            [
                grad_k.reshape(back_block, seq_count, col_width),
                grad_v.reshape(back_block, seq_count, col_width),
            ],
            axis=-1,
        )
        return (current, joined)

    grad_q, key_terms = lax.scan(
        back_step,
        jnp.zeros((seq_count, local_heads, local_len, HEAD_DIM), jnp.float32),
        jnp.arange(full_len // back_block, dtype=jnp.int32),
    )
    key_terms = key_terms.reshape(full_len, seq_count, 2 * col_width)
    key_sums = lax.psum_scatter(
        key_terms.astype(jnp.bfloat16), "ctx", scatter_dimension=0, tiled=True
    ).astype(jnp.float32)
    grad_q_flat = jnp.transpose(grad_q, (2, 0, 1, 3)).reshape(local_len, seq_count, col_width)
    d_proj = jnp.stack(
        [grad_q_flat, key_sums[..., :col_width], key_sums[..., col_width:]], axis=2
    ).astype(jnp.bfloat16)
    d_bias_qv = jnp.stack(
        [
            jnp.sum(d_proj[:, :, 0].astype(jnp.float32), axis=(0, 1)),
            jnp.sum(d_proj[:, :, 2].astype(jnp.float32), axis=(0, 1)),
        ]
    )
    grad_bin_qkv = jnp.einsum("tsd,tskh->dkh", a_in, d_proj, preferred_element_type=jnp.float32)
    rows = d_proj
    through = lax.psum_scatter(
        jnp.einsum("tskh,dkh->tsd", rows, full_qkv, preferred_element_type=jnp.float32).astype(
            jnp.bfloat16
        ),
        "tp",
        scatter_dimension=0,
        tiled=True,
    ).astype(jnp.float32)
    input_grad = d_first + through * (jnp.abs(stream_rows) < clip_in).astype(jnp.float32)
    shards = (
        lax.psum_scatter(
            grad_bin_qkv.astype(jnp.bfloat16), "fsdp", scatter_dimension=0, tiled=True
        ).astype(jnp.float32),
        lax.psum_scatter(
            grad_bin_out.astype(jnp.bfloat16), "fsdp", scatter_dimension=0, tiled=True
        ).astype(jnp.float32),
        lax.psum_scatter(
            grad_bin_up.astype(jnp.bfloat16), "fsdp", scatter_dimension=0, tiled=True
        ).astype(jnp.float32),
        lax.psum_scatter(
            grad_bin_down.astype(jnp.bfloat16), "fsdp", scatter_dimension=0, tiled=True
        ).astype(jnp.float32),
    )
    summed = (
        lax.psum(shards[0].astype(jnp.bfloat16), "ctx").astype(jnp.float32),
        lax.psum(shards[1].astype(jnp.bfloat16), "ctx").astype(jnp.float32),
        lax.psum(shards[2].astype(jnp.bfloat16), "ctx").astype(jnp.float32),
        lax.psum(shards[3].astype(jnp.bfloat16), "ctx").astype(jnp.float32),
    )
    grad_qkv = straight(summed[0], latent_qkv, qkv_quant[0][None], qkv_quant[1][None])
    grad_out = straight(summed[1], latent_out, out_quant[0][:, None], out_quant[1][:, None])
    grad_up = straight(summed[2], latent_up, up_quant[0][None], up_quant[1][None])
    grad_down = straight(summed[3], latent_down, down_quant[0][:, None], down_quant[1][:, None])
    vector_grads = jnp.stack(
        [d_bias_out, d_bias_down, d_gain_one, d_bias_one, d_gain_two, d_bias_two]
    )
    placed_qv = lax.dynamic_update_slice_in_dim(
        jnp.zeros((2, width), jnp.float32), d_bias_qv, tp_rank * col_width, 1
    )
    placed_up = lax.dynamic_update_slice_in_dim(
        jnp.zeros((hidden_width * lax.axis_size("tp"),), jnp.float32),
        d_bias_up,
        tp_rank * hidden_width,
        0,
    )
    stat_sums, vector_sums, qv_sums, up_sums = lax.psum(
        (stat_terms, vector_grads, placed_qv, placed_up), ("fsdp", "ctx", "tp")
    )
    grad_rows = lax.dynamic_slice_in_dim(vector_sums, fsdp_rank * row_width, row_width, 1)
    grad_qv = lax.dynamic_slice_in_dim(qv_sums, tp_rank * col_width, col_width, 1)
    grad_bias_up = lax.dynamic_slice_in_dim(up_sums, tp_rank * hidden_width, hidden_width, 0)
    denom = stat_sums[0] * width
    statistics = jnp.stack(
        [
            jnp.sqrt(stat_sums[1] / denom),
            jnp.sqrt(stat_sums[2] / denom),
            jnp.sqrt(stat_sums[3] / denom),
            stat_sums[4] / denom,
        ]
    )
    return (
        layer_out,
        input_grad,
        grad_qkv,
        grad_out,
        grad_up,
        grad_down,
        grad_rows,
        grad_qv,
        grad_bias_up,
        statistics,
    )


def pick_body(mesh):
    sizes = dict(mesh.shape)
    if sizes["fsdp"] == 4 and sizes["tp"] == 4 and sizes["ctx"] == 2:
        return paired_body
    return general_body


def solution(mesh):
    return jax.shard_map(
        pick_body(mesh),
        mesh=mesh,
        in_specs=(
            P("ctx", "fsdp", None),
            P(("ctx", "tp"), "fsdp", None),
            P("fsdp", "ctx"),
            P("fsdp", "ctx"),
            P("fsdp", None, "tp"),
            P("fsdp", "tp"),
            P("fsdp", "tp"),
            P("fsdp", "tp"),
            P(None, None, "tp"),
            P(None, "tp"),
            P(None, "fsdp"),
            P(None, "fsdp"),
            P(None, "tp"),
            P("tp"),
            P(),
            P(),
            P("tp"),
            P("tp"),
            P("fsdp", None, "tp"),
            P("fsdp", "tp"),
            P("fsdp", "tp"),
            P("fsdp", "tp"),
            P(None, "tp"),
            P("tp"),
            P(),
        ),
        out_specs=(
            P(("ctx", "tp"), "fsdp", None),
            P(("ctx", "tp"), "fsdp", None),
            P("fsdp", None, "tp"),
            P("fsdp", "tp"),
            P("fsdp", "tp"),
            P("fsdp", "tp"),
            P(None, "fsdp"),
            P(None, "tp"),
            P("tp"),
            P(),
        ),
        check_vma=False,
    )
```

```python
import functools
import math

import jax
import jax.numpy as jnp
from jax import lax
from jax.experimental import pallas as pl
from jax.experimental.pallas import tpu as pltpu
from jax.sharding import PartitionSpec as P

HEAD_DIM = 64


epsilon = 1e-05
floor_score = -1e30


def binarize(latent, shift, scales):
    return (scales * jnp.sign(latent - shift)).astype(jnp.bfloat16)


def straight(summed, latent, shift, scales):
    inside = (jnp.abs(latent - shift) < 1.0).astype(jnp.float32)
    return summed * scales * inside


def layer_norm(stream, gains, biases):
    centred = stream - jnp.mean(stream, axis=-1, keepdims=True)
    spread = jnp.mean(centred * centred, axis=-1, keepdims=True)
    return centred * lax.rsqrt(spread + epsilon) * gains + biases


def exact_gelu(values):
    return jax.nn.gelu(values, approximate=False)


def key_block(count):
    return math.gcd(count, 512)


def headed(array):
    return array.reshape(array.shape[0], array.shape[1], array.shape[2] // HEAD_DIM, HEAD_DIM)


def allowed_pairs(query_seg, query_pos, key_tags, key_pos):
    same = query_seg[:, :, None] == jnp.transpose(key_tags)[:, None, :]
    diagonal = query_pos[:, None] == key_pos[None, :]
    return (same | diagonal[None])[:, None]


def online_step(state, queries, keys, values, allowed, scale):
    running, total, accum = state
    scores = (
        jnp.einsum("tshe,kshe->shtk", queries, keys, preferred_element_type=jnp.float32) * scale
    )
    scores = jnp.where(allowed, scores, floor_score)
    newest = jnp.maximum(running, jnp.max(scores, axis=-1))
    weights = jnp.where(allowed, jnp.exp(scores - newest[..., None]), 0.0)
    factor = jnp.exp(running - newest)
    total = total * factor + jnp.sum(weights, axis=-1)
    accum = accum * factor[..., None] + jnp.einsum(
        "shtk,kshe->shte", weights.astype(jnp.bfloat16), values, preferred_element_type=jnp.float32
    )
    return (newest, total, accum)


def finish(state):
    running, total, accum = state
    merged = accum / total[..., None]
    return (jnp.transpose(merged, (2, 0, 1, 3)), running + jnp.log(total))


WORK_FACTOR = 4
TOKEN = (8, 128)
ROOM = 8 * 2**20


def vmem_specs(count):
    return [pl.BlockSpec(memory_space=pltpu.VMEM)] * count


def vmem_room(inputs, outs, scratch):
    total = 0
    for array in (*inputs, *jax.tree.leaves(outs), *scratch):
        if not jnp.issubdtype(array.dtype, jnp.number):
            continue
        *lead, rows, lanes = (1, 1, *array.shape)
        size = jnp.dtype(array.dtype).itemsize
        tile = 8 * (4 // size)
        total += math.prod(lead) * size * (-(-rows // tile) * tile) * (-(-lanes // 128) * 128)
    return min(total + ROOM, 60 * 2**20)


def call_kernel(kernel, place, inputs, outs, scratch=(), flops=0, moved=0, exps=0, from_hbm=False):
    place, after = place if isinstance(place, tuple) else (place, ())

    def body(place_ref, *refs):
        kernel(place_ref, *refs[len(after) :])

    return pl.pallas_call(
        body,
        out_shape=outs,
        in_specs=[pl.BlockSpec(memory_space=pltpu.SMEM)]
        + [pl.BlockSpec(memory_space=pl.ANY)] * len(after)
        + ([pl.BlockSpec(memory_space=pltpu.HBM)] * len(inputs) if from_hbm else vmem_specs(len(inputs))),
        out_specs=jax.tree.map(lambda _: pl.BlockSpec(memory_space=pltpu.VMEM), outs),
        scratch_shapes=list(scratch),
        compiler_params=pltpu.CompilerParams(vmem_limit_bytes=vmem_room(inputs, outs, scratch)),
        cost_estimate=pl.CostEstimate(
            flops=WORK_FACTOR * flops, bytes_accessed=moved, transcendentals=exps
        ),
    )(place, *after, *inputs)


def shaped(shape, dtype):
    return jax.ShapeDtypeStruct(shape, dtype)


def gate_kernel(place_ref, token_ref):
    token_ref[...] = jnp.zeros_like(token_ref)


def gate(place, *arrays):
    return call_kernel(gate_kernel, (place, arrays), (), shaped(TOKEN, jnp.float32), flops=1, moved=1)


NT = (((1,), (1,)), ((), ()))


def dot_nt(left, right):
    return lax.dot_general(left, right, NT, preferred_element_type=jnp.float32)


def dot_nn(left, right):
    return jnp.dot(left, right, preferred_element_type=jnp.float32)


QUERY_BLOCK = 256


def place_projections(place_ref, pieces, target, first):
    size, cols = pieces[0].shape[1], target.shape[2]
    for kind in range(3):
        for distance, piece in zip((0, 2, 1, 3), pieces):
            start = pl.multiple_of((place_ref[0] ^ distance) * size, 64)
            target[kind, pl.ds(start, size), :] = piece[kind, :, first : first + cols]


def project_kernel(place_ref, own_ref, w0, w2, w1, w3, bias_ref, clip_in_ref, full_ref, a_ref, q_ref, token_ref):
    place_projections(place_ref, (w0, w2, w1, w3), full_ref, 0)
    clipped = jnp.clip(own_ref[...].astype(jnp.float32), -clip_in_ref[...], clip_in_ref[...])
    clipped = clipped.astype(jnp.bfloat16)
    a_ref[...] = clipped
    write_heads(clipped, full_ref, bias_ref, q_ref, 0)
    token_ref[...] = jnp.zeros_like(token_ref)


def write_heads(inputs, w_ref, bias_ref, target, base):
    rows = inputs.shape[0]
    for kind in range(3):
        values = dot_nn(inputs, w_ref[kind])
        if kind != 1:
            values = values + bias_ref[kind >> 1 : (kind >> 1) + 1, :]
        values = values.astype(jnp.bfloat16)
        if kind == 0:
            values = values * (HEAD_DIM**-0.5)
        for head in range(target.shape[1]):
            target[kind, head, base : base + rows, :] = values[:, head * HEAD_DIM : (head + 1) * HEAD_DIM]


def project_own(place, own, pieces, bias, clip_in):
    half, width = own.shape
    cols = pieces[0].shape[-1] // 2
    heads = cols // HEAD_DIM
    bf16 = jnp.bfloat16
    return call_kernel(
        project_kernel,
        place,
        (own, *pieces, bias, clip_in),
        (
            shaped((3, width, cols), bf16),
            shaped((half, width), bf16),
            shaped((3, heads, half, HEAD_DIM), bf16),
            shaped(TOKEN, jnp.float32),
        ),
        flops=1,
        moved=1,
    )


def unit_matrix():
    shape = (HEAD_DIM, HEAD_DIM)
    ones = lax.broadcasted_iota(jnp.int32, shape, 0) == lax.broadcasted_iota(jnp.int32, shape, 1)
    return ones.astype(jnp.bfloat16)


def block_window(row_ref, place_ref, blocks):
    mask = order_mask(place_ref)
    low, high = [], []
    for block in range(blocks):
        segment = row_ref[:, block * QUERY_BLOCK : (block + 1) * QUERY_BLOCK] >> 1
        low.append(jnp.min(segment))
        high.append(jnp.max(segment))
    windows = []
    for query in range(blocks):
        first, last = jnp.int32(blocks - 1), jnp.int32(0)
        for key in range(blocks):
            meets = (low[key] <= high[query]) & (high[key] >= low[query])
            at = key ^ mask
            first = jnp.where(meets, jnp.minimum(first, at), first)
            last = jnp.where(meets, jnp.maximum(last, at), last)
        windows.append((first, last - first + 1))
    return windows


def order_mask(place_ref):
    return 2 * place_ref[2] + (place_ref[1] >> 1)


def pick(values, index):
    chosen = values[0]
    for at in range(1, len(values)):
        chosen = jnp.where(index == at, values[at], chosen)
    return chosen


def pair_bias(col_ref, row_ref, query, key):
    size = QUERY_BLOCK
    code_col = col_ref[pl.ds(pl.multiple_of(key * size, size), size), :]
    code_row = row_ref[:, pl.ds(pl.multiple_of(query * size, size), size)]
    tags = jnp.where((code_col & 1) > 0, code_col >> 1, -1)
    apart = lax.broadcasted_iota(jnp.int32, (size, size), 0) - lax.broadcasted_iota(
        jnp.int32, (size, size), 1
    )
    allowed = (tags == (code_row >> 1)) | (apart == (query - key) * size)
    return jnp.where(allowed, 0.0, floor_score)


def each_count(windows, query, blocks, body):
    first = pick([w[0] for w in windows], query)
    count = pick([w[1] for w in windows], query)
    for fixed in range(1, blocks + 1):

        @pl.when(count == fixed)
        def _():
            body(first, fixed)


def attention_kernel(
    student, place_ref, other_ref, bias_ref, clip_in_ref, clip_ref, col_ref, row_ref, *refs
):
    if student:
        w_ref, part_ref, *c_refs = refs[:6]
        a_ref, rows_ref, qkv_ref, merged_ref, lse_ref, vt_ref, bias_at, score_ref, sum_ref = refs[6:]
    else:
        pieces, own_ref, c_refs, token_ref = refs[:4], refs[4], refs[5:9], refs[9]
        w_ref, qkv_ref, vt_ref, bias_at, score_ref, sum_ref = refs[10:]
        token_ref[...] = jnp.zeros_like(token_ref)
    half = qkv_ref.shape[2] // 2
    heads = qkv_ref.shape[1]
    cols = heads * HEAD_DIM
    size = QUERY_BLOCK
    blocks = 2 * half // size
    bf16, f32 = jnp.bfloat16, jnp.float32
    inputs = other_ref[0:half, :]
    if student:
        qkv_ref[:, :, 0:half, :] = part_ref[...]
        inputs = jnp.clip(inputs.astype(f32), -clip_in_ref[...], clip_in_ref[...]).astype(bf16)
        a_ref[...] = inputs
        rows_ref[...] = other_ref[0 : half // 4, :]
    else:
        place_projections(place_ref, pieces, w_ref, w_ref.shape[2])
        write_heads(own_ref[...], w_ref, bias_ref, qkv_ref, 0)
    write_heads(inputs, w_ref, bias_ref, qkv_ref, half)
    eye = unit_matrix()
    for head in range(heads):
        vt_ref[head] = dot_nt(eye, qkv_ref[2, head]).astype(bf16)
    windows = block_window(row_ref, place_ref, blocks)
    mask = order_mask(place_ref)
    sum_ref[...] = jnp.zeros_like(sum_ref)

    def one_query(query, carry):
        at = pl.multiple_of(query * size, size)

        def body(first, count):
            keys = [(first + step) ^ mask for step in range(count)]
            starts = [pl.multiple_of(key * size, size) for key in keys]
            for step in range(count):
                bias_at[step] = pair_bias(col_ref, row_ref, query, keys[step])
            for head in range(heads):
                queries = qkv_ref[0, head, pl.ds(at, size), :]
                top = None
                for step in range(count):
                    scores = bias_at[step] + dot_nt(
                        qkv_ref[1, head, pl.ds(starts[step], size), :], queries
                    )
                    score_ref[step] = scores
                    part = jnp.max(scores, axis=0, keepdims=True)
                    top = part if top is None else jnp.maximum(top, part)
                total, merged = 0.0, 0.0
                for step in range(count):
                    weights = jnp.exp(score_ref[step] - top)
                    total = total + jnp.sum(weights, axis=0, keepdims=True)
                    merged = merged + dot_nn(
                        vt_ref[head, :, pl.ds(starts[step], size)], weights.astype(bf16)
                    )
                sum_ref[head * HEAD_DIM : (head + 1) * HEAD_DIM, :] = merged * (1.0 / total)
                if student:
                    lse_ref[head : head + 1, pl.ds(at, size)] = top + jnp.log(total)

        each_count(windows, query, blocks, body)
        if student:
            merged_ref[:, pl.ds(at, size)] = sum_ref[0:cols, :]
        merged = jnp.transpose(sum_ref[...])[:, :cols]
        if student:
            merged = clip_ref[...] * jnp.tanh(merged / clip_ref[...])
        merged = merged.astype(bf16)
        share = size // 2
        for at in range(blocks):

            @pl.when(query == at)
            def _():
                lanes = slice((at >> 1) * cols, ((at >> 1) + 1) * cols)
                c_refs[2 * (at & 1)][:, lanes] = merged[:share]
                c_refs[2 * (at & 1) + 1][:, lanes] = merged[share:]

        return carry

    lax.fori_loop(0, blocks, one_query, 0)


def attention_forward(student, place, other, weights, parts, bias, clip_in, clip, code_col, code_row):
    width = other.shape[1]
    half = parts.shape[2] if student else parts.shape[0]
    cols = clip.shape[-1]
    heads = cols // HEAD_DIM
    count = 2 * half
    bf16, f32 = jnp.bfloat16, jnp.float32
    qkv = (3, heads, count, HEAD_DIM)
    c_shape = (shaped((half // 4, 2 * cols), bf16),) * 4
    scratch = (
        pltpu.VMEM((heads, HEAD_DIM, count), bf16),
        pltpu.VMEM((count // QUERY_BLOCK, QUERY_BLOCK, QUERY_BLOCK), f32),
        pltpu.VMEM((count // QUERY_BLOCK, QUERY_BLOCK, QUERY_BLOCK), f32),
        pltpu.VMEM((256, QUERY_BLOCK), f32),
    )
    if student:
        outs = (
            *c_shape,
            shaped((half, width), bf16),
            shaped((half // 4, width), bf16),
            shaped(qkv, bf16),
            shaped((cols, count), f32),
            shaped((8, count), f32),
        )
        inputs = (weights, parts)
    else:
        outs = (*c_shape, shaped(TOKEN, f32))
        scratch = (pltpu.VMEM((3, width, cols), bf16), pltpu.VMEM(qkv, bf16), *scratch)
        inputs = (*weights, parts)
    return call_kernel(
        functools.partial(attention_kernel, student),
        place,
        (other, bias, clip_in, clip, code_col, code_row, *inputs),
        outs,
        scratch,
        flops=2 * half * width * cols * 3 + 4 * count * count * cols,
        moved=6 * count * width,
        exps=heads * count * count,
    )


def attention_pull_kernel(
    place_ref,
    qkv_ref,
    clip_ref,
    merged_ref,
    lse_ref,
    col_ref,
    row_ref,
    d0_ref,
    d1_ref,
    d2_ref,
    d3_ref,
    w_ref,
    keep_ref,
    send_ref,
    dproj_ref,
    sums_ref,
    grad_ref,
    kt_ref,
    dk_ref,
    dv_ref,
    sum_ref,
    delta_ref,
    bias_at,
):
    _, heads, count, _ = qkv_ref.shape
    cols = heads * HEAD_DIM
    size = QUERY_BLOCK
    share = size // 2
    blocks = count // size
    bf16, f32 = jnp.bfloat16, jnp.float32
    eye = unit_matrix()
    for head in range(heads):
        kt_ref[head] = dot_nt(eye, qkv_ref[1, head]).astype(bf16)
    for distance, source in enumerate((d0_ref, d1_ref, d2_ref, d3_ref)):
        for part in range(2):
            at = part * (count // 2) + distance * share
            merged = merged_ref[:, at : at + share]
            wide = jnp.concatenate([merged, jnp.zeros((256 - cols, share), f32)], axis=0)
            ratio = jnp.tanh(jnp.transpose(wide)[:, :cols] / clip_ref[...])
            grad = (source[:, part * cols : (part + 1) * cols].astype(f32) * (1.0 - ratio * ratio)).astype(bf16)
            for head in range(heads):
                grad_ref[head, at : at + share, :] = grad[:, head * HEAD_DIM : (head + 1) * HEAD_DIM]
            wide = jnp.concatenate(
                [grad.astype(f32), jnp.zeros((share, 256 - cols), f32)], axis=1
            )
            turned = jnp.transpose(wide)[:cols] * merged
            for head in range(heads):
                delta_ref[head : head + 1, at : at + share] = jnp.sum(
                    turned[head * HEAD_DIM : (head + 1) * HEAD_DIM], axis=0, keepdims=True
                )
    dk_ref[...] = jnp.zeros_like(dk_ref)
    dv_ref[...] = jnp.zeros_like(dv_ref)
    windows = block_window(row_ref, place_ref, blocks)
    mask = order_mask(place_ref)
    sum_ref[...] = jnp.zeros_like(sum_ref)

    def one_query(query, carry):
        at = pl.multiple_of(query * size, size)

        def body(first, count):
            keys = [(first + step) ^ mask for step in range(count)]
            starts = [pl.multiple_of(key * size, size) for key in keys]
            for step in range(count):
                bias_at[step] = pair_bias(col_ref, row_ref, query, keys[step])
            for head in range(heads):
                queries = qkv_ref[0, head, pl.ds(at, size), :]
                grad = grad_ref[head, pl.ds(at, size), :]
                lse = lse_ref[head : head + 1, pl.ds(at, size)]
                delta = delta_ref[head : head + 1, pl.ds(at, size)]
                merged = 0.0
                for step in range(count):
                    rows = pl.ds(starts[step], size)
                    probs = jnp.exp(
                        dot_nt(qkv_ref[1, head, rows, :], queries) + (bias_at[step] - lse)
                    )
                    d_probs = dot_nt(qkv_ref[2, head, rows, :], grad)
                    d_scores = (probs * (d_probs - delta)).astype(bf16)
                    dv_ref[head, rows, :] += dot_nn(probs.astype(bf16), grad)
                    dk_ref[head, rows, :] += dot_nn(d_scores, queries)
                    merged = merged + dot_nn(kt_ref[head, :, rows], d_scores)
                sum_ref[head * HEAD_DIM : (head + 1) * HEAD_DIM, :] = merged

        each_count(windows, query, blocks, body)
        merged = jnp.transpose(sum_ref[...])[:, :cols] * (HEAD_DIM**-0.5)
        dproj_ref[0, pl.ds(at, size), :] = merged.astype(bf16)
        return carry

    lax.fori_loop(0, blocks, one_query, 0)
    for head in range(heads):
        lanes = slice(head * HEAD_DIM, (head + 1) * HEAD_DIM)
        dproj_ref[1, :, lanes] = dk_ref[head].astype(bf16)
        dproj_ref[2, :, lanes] = dv_ref[head].astype(bf16)
    sums_ref[0:1, :] = jnp.sum(dproj_ref[0].astype(f32), axis=0, keepdims=True)
    sums_ref[1:2, :] = jnp.sum(dproj_ref[2].astype(f32), axis=0, keepdims=True)
    for part in range(2):
        at = slice(part * (count // 2), (part + 1) * (count // 2))
        back = (
            dot_nt(dproj_ref[0, at, :], w_ref[0])
            + dot_nt(dproj_ref[1, at, :], w_ref[1])
            + dot_nt(dproj_ref[2, at, :], w_ref[2])
        ).astype(bf16)
        for distance in range(4):
            target = send_ref if distance & 1 else keep_ref
            target[distance >> 1, part] = back[distance * share : (distance + 1) * share]


def attention_backward(place, qkv, clip, merged, lse, code_col, code_row, grads, weights):
    _, heads, count, _ = qkv.shape
    cols = heads * HEAD_DIM
    width = weights.shape[1]
    bf16, f32 = jnp.bfloat16, jnp.float32
    return call_kernel(
        attention_pull_kernel,
        place,
        (qkv, clip, merged, lse, code_col, code_row, *grads, weights),
        (
            *(shaped((2, 2, count // 8, width), bf16),) * 2,
            shaped((3, count, cols), bf16),
            shaped((2, cols), f32),
        ),
        (
            pltpu.VMEM((heads, count, HEAD_DIM), bf16),
            pltpu.VMEM((heads, HEAD_DIM, count), bf16),
            pltpu.VMEM((heads, count, HEAD_DIM), f32),
            pltpu.VMEM((heads, count, HEAD_DIM), f32),
            pltpu.VMEM((256, QUERY_BLOCK), f32),
            pltpu.VMEM((8, count), f32),
            pltpu.VMEM((count // QUERY_BLOCK, QUERY_BLOCK, QUERY_BLOCK), f32),
        ),
        flops=2 * count * width * cols * 3 + 10 * count * count * cols,
        moved=8 * count * width,
        exps=heads * count * count,
    )


def unit_of(stream):
    mean = jnp.mean(stream, axis=-1, keepdims=True)
    centred = stream - mean
    scale = lax.rsqrt(jnp.mean(centred * centred, axis=-1, keepdims=True) + epsilon)
    return centred * scale, scale


def column_sum(value):
    return jnp.sum(value, axis=0, keepdims=True)


def dot_tn(left, right):
    return lax.dot_general(left, right, (((0,), (0,)), ((), ())), preferred_element_type=jnp.float32)


def out_norm_kernel(student, place_ref, *refs):
    if student:
        c_refs, pieces = refs[:4], refs[4:12]
        own_ref, other_ref, valid_ref, params_ref, cot_ref = refs[12:17]
        w_ref, unit_ref, scale_ref, low_ref, sums_ref, token_ref = refs[17:]
        token_ref[...] = jnp.zeros_like(token_ref)
    else:
        c_refs, w_ref = refs[:4], refs[4]
        own_ref, other_ref, valid_ref, params_ref = refs[5:9]
        wide_ref, low_ref, token_ref = refs[9:]
        token_ref[...] = jnp.zeros_like(token_ref)
    share = own_ref.shape[0]
    cols = c_refs[0].shape[1] // 2
    size = w_ref.shape[1] // 4
    total = None
    for r, source in enumerate(c_refs):
        if student:
            group = pieces[:4] if r % 2 == 0 else pieces[4:]
            for distance, piece in zip((0, 2, 1, 3), group):
                start = pl.multiple_of((place_ref[0] ^ distance) * size, 64)
                w_ref[r, pl.ds(start, size), :] = piece[r >> 1, 2 * size : 3 * size, :]
            weights = w_ref[r, :, 0:cols]
        else:
            weights = w_ref[r, :, cols : 2 * cols]
        context = jnp.concatenate([source[:, 0:cols], source[:, cols:]], axis=0)
        term = dot_nt(context, weights)
        total = term if total is None else total + term
    attn = total + params_ref[0:1, :]
    stream = jnp.concatenate([own_ref[...], other_ref[...]], axis=0).astype(jnp.float32)
    unit, scale = unit_of(stream + attn)
    wide = unit * params_ref[2:3, :] + params_ref[3:4, :]
    low_ref[0 : 2 * share, :] = wide.astype(jnp.bfloat16)
    if student:
        low_ref[2 * share :, :] = cot_ref[...]
        unit_ref[...] = unit
        scale_ref[...] = scale
        valid = valid_ref[...]
        sums_ref[0:1, :] = column_sum(valid * jnp.ones_like(stream))
        sums_ref[1:2, :] = column_sum(valid * stream * stream)
        sums_ref[2:3, :] = column_sum(valid * attn * attn)
    else:
        wide_ref[...] = wide


def out_norm(student, place, contexts, weights, own, other, valid, params, cot=()):
    share, width = own.shape
    rows = 2 * share
    cols = contexts[0].shape[-1] // 2
    f32, bf16 = jnp.float32, jnp.bfloat16
    if student:
        outs = (
            shaped((4, width, 2 * cols), bf16),
            shaped((rows, width), f32),
            shaped((rows, 1), f32),
            shaped((rows + share, width), bf16),
            shaped((3, width), f32),
            shaped(TOKEN, f32),
        )
    else:
        outs = (shaped((rows, width), f32), shaped((rows, width), bf16), shaped(TOKEN, f32))
    return call_kernel(
        functools.partial(out_norm_kernel, student),
        place,
        (*contexts, *(weights if student else (weights,)), own, other, valid, params, *cot),
        outs,
        flops=2 * rows * width * cols * 4,
        moved=12 * rows * width,
    )


def gelu_parts(values):
    cdf = 0.5 * (1.0 + lax.erf(values * (2.0**-0.5)))
    return values * cdf, cdf


def hidden_kernel(student, assemble, far, place_ref, h_ref, *refs):
    refs = list(refs)
    pieces = [refs.pop(0) for _ in range(8 if assemble else 1)]
    with_terms = student and assemble
    terms_ref = None if with_terms else refs.pop(0)
    w_ref = refs.pop(0) if assemble else pieces[0]
    if with_terms:
        terms_ref = refs.pop(0)
    if student:
        hid_ref, slope_ref = refs.pop(0), refs.pop(0)
    part_ref, token_ref = refs
    token_ref[...] = jnp.zeros_like(token_ref)
    bf16 = jnp.bfloat16
    total = None
    inputs = h_ref[0 : part_ref.shape[0], :]
    for r in range(4):
        if assemble:
            group = pieces[:4] if r % 2 == 0 else pieces[4:]
            size = w_ref.shape[2] // 4
            for mat in range(2):
                for distance, piece in zip((0, 2, 1, 3), group):
                    start = pl.multiple_of((place_ref[0] ^ distance) * size, 64)
                    w_ref[r, mat, pl.ds(start, size), :] = piece[r >> 1, mat * size : (mat + 1) * size, :]
        if with_terms:
            terms_ref[r] = group[0][r >> 1, 3 * size : 3 * size + 16, :]
        terms = terms_ref[r].astype(jnp.float32)
        base = 0 if student else 6
        bias = terms[base : base + 1] + terms[base + 1 : base + 2] + terms[base + 2 : base + 3]
        upper = dot_nn(inputs, w_ref[r, 0]) + bias
        active, cdf = gelu_parts(upper)
        if student:
            clip = terms[3:4] + terms[4:5] + terms[5:6]
            ratio = jnp.tanh(active / clip)
            pdf = jnp.exp(-0.5 * upper * upper) * ((2.0 * math.pi) ** -0.5)
            slope_ref[r] = ((1.0 - ratio * ratio) * (cdf + upper * pdf)).astype(bf16)
            hidden = (clip * ratio).astype(bf16)
            hid_ref[r] = hidden
        else:
            hidden = active.astype(bf16)
        term = dot_nt(hidden, w_ref[r, 1])
        total = term if total is None else total + term
    part_ref[...] = total.astype(part_ref.dtype)


def hidden_layer(student, far, place, h, rows, weights, terms=None):
    width = h.shape[-1]
    half = weights[0].shape[-1] if isinstance(weights, tuple) else weights.shape[-1]
    f32, bf16 = jnp.float32, jnp.bfloat16
    assemble = isinstance(weights, tuple)
    outs = []
    if assemble:
        outs.append(shaped((4, 2, width, half), bf16))
        if student:
            outs.append(shaped((4, 16, half), bf16))
    if student:
        outs += [shaped((4, rows, half), bf16)] * 2
    outs += [shaped((rows, width), bf16 if far else f32), shaped(TOKEN, f32)]
    inputs = (h, *(weights if assemble else (weights,))) + (() if terms is None else (terms,))
    return call_kernel(
        functools.partial(hidden_kernel, student, assemble, far),
        place,
        inputs,
        tuple(outs),
        flops=2 * rows * width * half * 8,
        moved=8 * width * half * 2 + 16 * rows * half,
        exps=(3 if student else 1) * rows * half * 4,
    )


def loss_kernel(
    place_ref, unit_ref, ffn_ref, got_ref, ht_ref, ffnt_ref, gott_ref, cot_ref, cot_other_ref, valid_ref, params_ref, t_ref,
    layer_ref, layer_other_ref, dz_ref, low_ref, sums_ref,
):
    share = cot_ref.shape[0]
    rows = 2 * share
    f32, bf16 = jnp.float32, jnp.bfloat16
    h_one = unit_ref[...] * params_ref[2:3, :] + params_ref[3:4, :]
    ffn = ffn_ref[...] + got_ref[...].astype(f32) + params_ref[1:2, :]
    unit, scale = unit_of(h_one + ffn)
    out = unit * params_ref[4:5, :] + params_ref[5:6, :]
    low = out.astype(bf16)
    layer_ref[...] = low[:share]
    layer_other_ref[...] = low[share:]
    t_unit, _ = unit_of(ht_ref[...] + ffnt_ref[...] + gott_ref[...].astype(f32) + t_ref[1:2, :])
    difference = out - (t_unit * t_ref[4:5, :] + t_ref[5:6, :])
    valid = valid_ref[...]
    gap = valid * difference
    arriving = jnp.concatenate([cot_ref[...], cot_other_ref[rows:, :]], axis=0).astype(f32)
    grad = arriving + gap
    inner = grad * params_ref[4:5, :]
    dz = scale * (
        inner
        - jnp.mean(inner, axis=-1, keepdims=True)
        - unit * jnp.mean(inner * unit, axis=-1, keepdims=True)
    )
    dz_ref[...] = dz
    dz_low = dz.astype(bf16)
    low_ref[...] = dz_low
    sums_ref[0:1, :] = column_sum(dz_low.astype(f32))
    sums_ref[1:2, :] = column_sum(grad * unit)
    sums_ref[2:3, :] = column_sum(grad)
    sums_ref[3:4, :] = column_sum(valid * ffn * ffn)
    sums_ref[4:5, :] = column_sum(gap * difference)


def loss_step(place, unit, ffn, got, ht, ffnt, gott, cot, cot_other, valid, params, t_rows):
    rows, width = unit.shape
    share = cot.shape[0]
    f32, bf16 = jnp.float32, jnp.bfloat16
    return call_kernel(
        loss_kernel,
        place,
        (unit, ffn, got, ht, ffnt, gott, cot, cot_other, valid, params, t_rows),
        (
            shaped((share, width), bf16),
            shaped((share, width), bf16),
            shaped((rows, width), f32),
            shaped((rows, width), bf16),
            shaped((5, width), f32),
        ),
        flops=60 * rows * width,
        moved=30 * rows * width,
    )


def hidden_pull_kernel(place_ref, grad_ref, w_ref, slope_ref, du_ref, part_ref, sums_ref):
    grad = grad_ref[0 : part_ref.shape[0], :]
    total = None
    for r in range(4):
        upper = (dot_nn(grad, w_ref[r, 1]) * slope_ref[r].astype(jnp.float32)).astype(jnp.bfloat16)
        du_ref[r] = upper
        sums_ref[r : r + 1, :] = column_sum(upper.astype(jnp.float32))
        term = dot_nt(upper, w_ref[r, 0])
        total = term if total is None else total + term
    part_ref[...] = total.astype(part_ref.dtype)


def hidden_pull(far, place, grad, weights, slope):
    width = grad.shape[-1]
    rows = slope.shape[1]
    half = slope.shape[-1]
    f32, bf16 = jnp.float32, jnp.bfloat16
    return call_kernel(
        hidden_pull_kernel,
        place,
        (grad, weights, slope),
        (shaped((4, rows, half), bf16), shaped((rows, width), bf16 if far else f32), shaped((4, half), f32)),
        flops=2 * rows * width * half * 8,
        moved=8 * width * half * 2 + 16 * rows * half,
    )


def hidden_grads_kernel(mat, place_ref, l0, l1, r0, r1, keep_ref, send_ref, full_ref):
    rows = r0.shape[1]
    left = jnp.transpose(jnp.concatenate([l0[0:rows, :], l1[0:rows, :]], axis=0))
    size = full_ref.shape[0] // 4
    for r in range(4):
        right = jnp.concatenate([r0[r], r1[r]], axis=0)
        full_ref[...] = dot_nn(left, right)
        for slot in range(2):
            for target, distance in ((keep_ref, 2 * slot), (send_ref, 2 * slot + 1)):
                start = pl.multiple_of((place_ref[0] ^ distance) * size, 64)
                target[slot, r] = full_ref[pl.ds(start, size), :].astype(jnp.bfloat16)


def hidden_grads(place, left, right):
    width = left[0].shape[-1]
    rows, half = right[0].shape[1:]
    out = shaped((2, 4, width // 4, half), jnp.bfloat16)
    return call_kernel(
        functools.partial(hidden_grads_kernel, 0),
        place,
        (*left, *right),
        (out, out),
        (pltpu.VMEM((width, half), jnp.float32),),
        flops=16 * rows * width * half * 4,
        moved=8 * width * half * 2,
    )


def first_pull_kernel(place_ref, dz_ref, part_ref, got_ref, unit_ref, scale_ref, params_ref, w_ref, first_ref, low_ref, sums_ref, *ctx_refs):
    f32, bf16 = jnp.float32, jnp.bfloat16
    grad = dz_ref[...] + part_ref[...] + got_ref[...].astype(f32)
    unit = unit_ref[...]
    inner = grad * params_ref[2:3, :]
    first = scale_ref[...] * (
        inner
        - jnp.mean(inner, axis=-1, keepdims=True)
        - unit * jnp.mean(inner * unit, axis=-1, keepdims=True)
    )
    first_ref[...] = first
    low = first.astype(bf16)
    low_ref[...] = low
    sums_ref[0:1, :] = column_sum(low.astype(f32))
    sums_ref[1:2, :] = column_sum(grad * unit)
    sums_ref[2:3, :] = column_sum(grad)
    share, cols = ctx_refs[0].shape[0], ctx_refs[0].shape[1] // 2
    for r in range(4):
        back = dot_nn(low, w_ref[r, :, 0:cols]).astype(bf16)
        ctx_refs[r][:, 0:cols] = back[:share]
        ctx_refs[r][:, cols:] = back[share:]


def first_pull(place, dz, part, got, unit, scale, params, weights):
    rows, width = dz.shape
    cols = weights.shape[-1] // 2
    f32, bf16 = jnp.float32, jnp.bfloat16
    return call_kernel(
        first_pull_kernel,
        place,
        (dz, part, got, unit, scale, params, weights),
        (
            shaped((rows, width), f32),
            shaped((rows, width), bf16),
            shaped((3, width), f32),
            *(shaped((rows // 2, 2 * cols), bf16),) * 4,
        ),
        flops=2 * rows * width * cols * 4,
        moved=20 * rows * width,
    )


def last_grads_kernel(place_ref, low_ref, c0, c1, c2, c3, a_ref, a_other_ref, d_ref, qv_ref, keep_ref, send_ref, full_ref):
    size, cols = full_ref.shape[0] // 4, full_ref.shape[1]
    half = a_ref.shape[0]
    low = jnp.transpose(low_ref[...])
    own, other = jnp.transpose(a_ref[...]), jnp.transpose(a_other_ref[...])
    spots = ((0, 0), (1, 0), (0, 1), (1, 1), (2, 0), (2, 1), (3, 0))
    for entry, (block, side) in enumerate(spots):
        if entry < 4:
            source = (c0, c1, c2, c3)[entry]
            context = jnp.concatenate([source[:, 0:cols], source[:, cols:]], axis=0)
            full_ref[...] = dot_nn(low, context)
        else:
            full_ref[...] = dot_nn(own, d_ref[entry - 4, 0:half, :]) + dot_nn(
                other, d_ref[entry - 4, half:, :]
            )
        for slot in range(2):
            for target, distance in ((keep_ref, 2 * slot), (send_ref, 2 * slot + 1)):
                start = pl.multiple_of((place_ref[0] ^ distance) * size, 64)
                target[slot, block * size : (block + 1) * size, side * cols : (side + 1) * cols] = (
                    full_ref[pl.ds(start, size), :].astype(jnp.bfloat16)
                )
    sums = jnp.concatenate([qv_ref[...], jnp.zeros((14, cols), jnp.float32)], axis=0)
    sums = jnp.concatenate([sums, jnp.zeros((16, cols), jnp.float32)], axis=1)
    nothing = jnp.zeros((size, cols), jnp.bfloat16)
    for slot in range(2):
        for target in (keep_ref, send_ref):
            target[slot, 3 * size : 4 * size, cols:] = nothing
            target[slot, 4 * size :, :] = sums.astype(jnp.bfloat16)


def last_grads(place, low, contexts, a_in, d_proj, d_bias_qv):
    rows, width = low.shape
    count = d_proj.shape[1]
    cols = d_proj.shape[-1]
    out = shaped((2, 4 * (width // 4) + 16, 2 * cols), jnp.bfloat16)
    return call_kernel(
        last_grads_kernel,
        place,
        (low, *contexts, *a_in, d_proj, d_bias_qv),
        (out, out),
        (pltpu.VMEM((width, cols), jnp.float32),),
        flops=2 * (4 * rows + 3 * count) * width * cols,
        moved=4 * count * width,
    )


def input_kernel(place_ref, first_ref, b0, b1, b2, own_ref, other_ref, clip_ref, mine_ref, other_out_ref):
    f32 = jnp.float32
    share = own_ref.shape[0]
    for part, (source, target) in enumerate(((own_ref, mine_ref), (other_ref, other_out_ref))):
        through = b0[0, part].astype(f32) + b1[0, part].astype(f32) + b2[part].astype(f32)
        inside = jnp.abs(source[...].astype(f32)) < clip_ref[...]
        first = first_ref[part * share : (part + 1) * share, :]
        target[...] = (first + jnp.where(inside, through, 0.0)).astype(target.dtype)


def input_rows(place, first, backs, own, other, clip_in):
    share, width = own.shape
    return call_kernel(
        input_kernel,
        place,
        (first, *backs, own, other, clip_in),
        (shaped((share, width), jnp.float32), shaped((share, width), jnp.bfloat16)),
        flops=10 * share * width,
        moved=20 * share * width,
    )


def vector_kernel(place_ref, third_ref, second_ref, first_ref, own_ref, far_ref, out_ref):
    half = own_ref.shape[1]
    out_ref[...] = jnp.zeros_like(out_ref)
    out_ref[0:3, :] = third_ref[...]
    out_ref[3:8, :] = second_ref[...]
    out_ref[8:11, :] = first_ref[...]
    for r in range(4):
        part = own_ref[r : r + 1, :] + far_ref[r : r + 1, :]
        nothing = jnp.zeros_like(part)
        left = jnp.where(place_ref[2] == 0, part, nothing)
        right = jnp.where(place_ref[2] == 0, nothing, part)
        out_ref[pl.ds(11 + (place_ref[1] ^ r), 1), :] = jnp.concatenate([left, right], axis=1)


def vector_rows(place, third, second, first, own, far):
    width = third.shape[1]
    return call_kernel(
        vector_kernel,
        place,
        (third, second, first, own, far),
        shaped((16, width), jnp.float32),
        flops=1,
        moved=1,
    )


def sign_of(value):
    return jnp.where(value > 0.0, 1.0, jnp.where(value < 0.0, -1.0, 0.0))


def piece_kernel(place_ref, *refs):
    sources, (piece_ref, teacher_ref), copies, sems = refs[:11], refs[11:13], refs[13:24], refs[24]
    moves = [
        pltpu.make_async_copy(source, target, sems.at[at])
        for at, (source, target) in enumerate(zip(sources, copies))
    ]
    for move in moves:
        move.start()
    for move in moves:
        move.wait()
    up_ref, down_ref, out_ref, t_out_ref, t_up_ref, t_down_ref, quant_ref, columns_ref, *rows = copies
    bf16, f32 = jnp.bfloat16, jnp.float32
    size, half = up_ref.shape[0], piece_ref.shape[1]
    lanes = pl.ds(pl.multiple_of(place_ref[2] * half, 128), half)
    quant = quant_ref[:, lanes]
    up = quant[1:2] * sign_of(up_ref[:, lanes] - quant[0:1])
    piece_ref[0:size, :] = up.astype(bf16)
    columns = columns_ref[...]
    down = columns[:, 3:4] * sign_of(down_ref[:, lanes] - columns[:, 2:3])
    piece_ref[size : 2 * size, :] = down.astype(bf16)
    out = columns[:, 1:2] * sign_of(out_ref[...] - columns[:, 0:1])
    piece_ref[2 * size : 3 * size, :] = jnp.concatenate([out.astype(bf16), t_out_ref[...]], axis=1)
    terms = []
    for row in rows:
        rest = row[:, lanes]
        for _ in range(3):
            term = rest.astype(bf16).astype(f32)
            terms.append(term)
            rest = rest - term
    terms = jnp.concatenate(terms + [jnp.zeros((7, half), f32)], axis=0)
    piece_ref[3 * size :, :] = terms.astype(bf16)
    teacher_ref[0:size, :] = t_up_ref[:, lanes]
    teacher_ref[size:, :] = t_down_ref[:, lanes]


def own_pieces(place, *sources):
    size, wide = sources[0].shape
    bf16 = jnp.bfloat16
    return call_kernel(
        piece_kernel,
        place,
        sources,
        (shaped((3 * size + 16, wide // 2), bf16), shaped((2 * size, wide // 2), bf16)),
        tuple(pltpu.VMEM(source.shape, source.dtype) for source in sources)
        + (pltpu.SemaphoreType.DMA((len(sources),)),),
        flops=1,
        moved=1,
        from_hbm=True,
    )


def swap_ctx(value):
    return lax.ppermute(value, "ctx", [(0, 1), (1, 0)])


def swap_core(value):
    return lax.ppermute(value, "fsdp", [(i, i ^ 1) for i in range(4)])


def swap_row(value):
    return lax.ppermute(value, "fsdp", [(i, i ^ 2) for i in range(4)])


def swap_tp(value, distance):
    return lax.ppermute(value, "tp", [(i, i ^ distance) for i in range(4)])


def fsdp_pieces(piece):
    far = swap_row(piece)
    return (piece, far, swap_core(piece), swap_core(far))


def exchange_tp(entries):
    return [entries[0]] + [swap_tp(entries[r], r) for r in (1, 2, 3)]


def three_terms(value):
    high = lax.reduce_precision(value, 8, 7)
    rest = value - high
    middle = lax.reduce_precision(rest, 8, 7)
    return [high.astype(jnp.bfloat16), middle.astype(jnp.bfloat16), (rest - middle).astype(jnp.bfloat16)]


def tie(values, *others):
    return lax.optimization_barrier((values, others))[0]


def once(place, *arrays):
    return (place, arrays)


def paired_body(
    tokens,
    cotangent,
    segment_ids,
    valid_mask,
    latent_qkv,
    latent_out,
    latent_up,
    latent_down,
    qkv_quant,
    up_quant,
    out_quant,
    down_quant,
    bias_qv,
    bias_up,
    row_params,
    clip_in,
    clip_ctx,
    clip_hidden,
    t_qkv,
    t_out,
    t_up,
    t_down,
    t_bias_qv,
    t_bias_up,
    t_rows,
):
    local_len, seq_count, width = tokens.shape
    share = cotangent.shape[0]
    col_width = latent_qkv.shape[2]
    hidden_width = latent_up.shape[1]
    half_hidden = hidden_width // 2
    row_width = latent_qkv.shape[0]
    tp_rank = lax.axis_index("tp")
    ctx_rank = lax.axis_index("ctx")
    fsdp_rank = lax.axis_index("fsdp")
    f32, bf16 = jnp.float32, jnp.bfloat16
    place = jnp.stack([fsdp_rank, tp_rank, ctx_rank]).astype(jnp.int32)

    def by_distance(value):
        pairs = value.reshape(2, 2, *value.shape[1:])
        pairs = jnp.where((tp_rank & 1) > 0, pairs[:, ::-1], pairs)
        pairs = jnp.where((tp_rank >> 1) > 0, pairs[::-1], pairs)
        return pairs.reshape(value.shape)

    def mine(value, axis):
        return lax.dynamic_index_in_dim(value, ctx_rank, axis, keepdims=False)

    def theirs(value, axis):
        return lax.dynamic_index_in_dim(value, 1 - ctx_rank, axis, keepdims=False)

    def half_of(weight):
        return jnp.where(ctx_rank == 0, weight[..., :half_hidden], weight[..., half_hidden:])

    def add(left, right):
        return left.astype(f32) + right.astype(f32)

    rows = 2 * share
    bin_up = binarize(latent_up, up_quant[0][None], up_quant[1][None])
    bin_down = binarize(latent_down, down_quant[0][:, None], down_quant[1][:, None])
    terms = [term for v in (bias_up, clip_hidden, t_bias_up) for term in three_terms(half_of(v))]
    vectors = jnp.pad(jnp.stack(terms), ((0, 16 - len(terms)), (0, 0)))
    bin_out = binarize(latent_out, out_quant[0][:, None], out_quant[1][:, None])
    piece = jnp.concatenate(
        [
            half_of(bin_up),
            half_of(bin_down),
            jnp.concatenate([bin_out, t_out], axis=1),
            vectors,
        ],
        axis=0,
    )
    piece_two = swap_tp(piece, 2)
    rows = 2 * share
    tokens_then, segment_then = tie((tokens, segment_ids), piece)
    relative = by_distance(tokens_then.reshape(4, share, seq_count, width))
    own = mine(relative, 2).reshape(local_len, width)
    code = by_distance(
        jnp.transpose(segment_then * 2 + (valid_mask > 0).astype(jnp.int32)).reshape(
            4, share, seq_count
        )
    )
    code_sent = jnp.pad(theirs(code, 2).reshape(1, local_len), ((0, 15), (0, width - local_len)))
    tokens_sent = jnp.concatenate(
        [theirs(relative, 2).reshape(local_len, width), code_sent.astype(bf16)], axis=0
    )
    other = swap_ctx(tokens_sent)
    latent_qkv_then, t_qkv = tie((latent_qkv, t_qkv), tokens_sent)
    bin_qkv = jnp.transpose(
        binarize(latent_qkv_then, qkv_quant[0][None], qkv_quant[1][None]), (1, 0, 2)
    )
    qkv_piece = jnp.concatenate([bin_qkv, jnp.transpose(t_qkv, (1, 0, 2))], axis=2)
    qkv_pieces = fsdp_pieces(qkv_piece)
    t_up, t_down = tie((t_up, t_down), qkv_piece)
    teacher_piece = jnp.concatenate([half_of(t_up), half_of(t_down)], axis=0)
    clip_in_row, clip_row = clip_in[None], clip_ctx[None]

    own_rows = own[:share]
    cot_own, cot_sent = mine(cotangent, 1), theirs(cotangent, 1)
    full_qkv, a_own, qkv_own, token = project_own(once(place, own_rows, cot_own, cot_sent), own, qkv_pieces, bias_qv, clip_in_row)
    other = tie(other, token)
    code_all = jnp.concatenate(
        [mine(code, 2).reshape(local_len), other[local_len, :local_len].astype(jnp.int32)]
    )
    code_col, code_row = code_all[:, None], code_all[None, :]
    valid = (
        jnp.concatenate([code_all[:share], code_all[local_len : local_len + share]]) & 1
    ).astype(f32)[:, None]
    even = jnp.stack([piece, tie(piece_two, token)])
    odd, even_row = swap_tp(even, 1), swap_row(even)
    *context, a_other, other_rows, qkv, merged, lse = attention_forward(
        True, once(place, even, token), other, full_qkv, qkv_own, bias_qv, clip_in_row,
        clip_row, code_col, code_row,
    )
    contexts = exchange_tp(context)
    odd, even_row = tie((odd, even_row), lse)
    even_cores = (swap_core(even), swap_core(even_row))
    odd_row = swap_row(odd)
    *teacher_context, token = attention_forward(
        False, once(place, lse, *even_cores), other, qkv_pieces, own,
        t_bias_qv, clip_in_row, clip_row, code_col, code_row,
    )
    token = gate(place, token, *contexts[1:])
    odd, odd_row, teacher_piece = tie((odd, odd_row, teacher_piece), token)
    teacher_two = swap_tp(teacher_piece, 2)
    pieces = (
        even, even_row, *even_cores,
        odd, odd_row, swap_core(odd), swap_core(odd_row),
    )
    out_full, unit, scale, h_low, first_sums, token = out_norm(
        True, once(place, token), contexts, pieces, own_rows, other_rows, valid, row_params,
        (cot_sent,),
    )
    h_far = swap_ctx(h_low)
    teacher_contexts = exchange_tp([teacher_context[0], *tie(teacher_context[1:], token)])
    hidden_full, terms, hid_own, slope_own, part_own, _ = hidden_layer(
        True, False, once(place, token), h_low, rows, pieces
    )
    teacher_even = jnp.stack([teacher_piece, tie(teacher_two, terms, *teacher_contexts[1:])])
    teacher_odd, teacher_even_row = swap_tp(teacher_even, 1), swap_row(teacher_even)
    h_teacher, ht_low, token = out_norm(
        False, once(place, part_own), teacher_contexts, out_full, own_rows, other_rows, valid, t_rows,
    )
    ht_far = swap_ctx(ht_low)
    hid_far, slope_far, part_far, token = hidden_layer(
        True, True, once(place, token), h_far, rows, hidden_full, terms
    )
    part_got = swap_ctx(part_far)
    teacher_odd = tie(teacher_odd, token)
    teacher_even_row = tie(teacher_even_row, token, ht_far)
    teacher_odd_row = swap_row(teacher_odd)
    teacher_hidden = (
        teacher_even, teacher_even_row, swap_core(teacher_even), swap_core(teacher_even_row),
        teacher_odd, teacher_odd_row, swap_core(teacher_odd), swap_core(teacher_odd_row),
    )
    teacher_full, t_part_far, _ = hidden_layer(
        False, True, once(place, token), ht_far, rows, teacher_hidden, terms
    )
    t_part_got = swap_ctx(t_part_far)
    t_part_own, _ = hidden_layer(
        False, False, once(place, t_part_far), ht_low, rows, teacher_full, terms
    )
    layer_own, layer_other, d_second, d_ffn, second_sums = loss_step(
        place, unit, part_own, part_got, h_teacher, t_part_own, t_part_got,
        cot_own, h_far, valid, row_params, t_rows,
    )

    def home(own_part, other_part):
        got = other_part.astype(own_part.dtype)
        first = jnp.where(ctx_rank == 0, own_part, got)
        second = jnp.where(ctx_rank == 0, got, own_part)
        return jnp.stack([first, second], axis=1)

    d_ffn_far = swap_ctx(d_ffn)
    du_own, d_part_own, du_sums_own = hidden_pull(False, place, d_ffn, hidden_full, slope_own)
    du_far, d_part_far, du_sums_far = hidden_pull(True, place, d_ffn_far, hidden_full, slope_far)
    d_part_got = swap_ctx(d_part_far)
    keep_down, send_down = hidden_grads(
        once(place, du_sums_far), (d_ffn, d_ffn_far), (hid_own, hid_far)
    )
    got_down = swap_core(send_down)
    leave_down = add(keep_down[1], got_down[1]).astype(bf16)
    d_first, d_attn, third_sums, *d_context = first_pull(
        once(place, send_down), d_second, d_part_own, d_part_got, unit, scale, row_params, out_full
    )
    d_contexts = exchange_tp(d_context)
    keep_up, send_up = hidden_grads(once(place, third_sums), (h_low, h_far), (du_own, du_far))
    got_up = swap_core(send_up)
    leave_up = add(keep_up[1], got_up[1]).astype(bf16)
    vector = vector_rows(place, third_sums, second_sums, first_sums, du_sums_own, du_sums_far)
    keep_back, send_back, d_proj, d_bias_qv = attention_backward(
        once(place, leave_down, leave_up, vector),
        qkv, clip_row, merged, lse, code_col, code_row, d_contexts, full_qkv,
    )
    got_back = swap_tp(send_back, 1)
    layer_out = home(layer_own, swap_ctx(tie(layer_other, d_bias_qv)))
    got_down_row, got_up_row = tie((swap_row(leave_down), swap_row(leave_up)), d_bias_qv)
    row_down = add(add(keep_down[0], got_down[0]), got_down_row)
    row_up = add(add(keep_up[0], got_up[0]), got_up_row)
    keep_last, send_last = last_grads(
        once(place, send_back, got_down_row, got_up_row),
        d_attn, contexts, (a_own, a_other), d_proj, d_bias_qv,
    )
    got_last, vector_got = swap_core(send_last), swap_core(tie(vector, send_last))
    got_back = tie(got_back, send_last)
    leave_back = add(keep_back[1], got_back[1]).astype(bf16)
    got_back_two = swap_tp(leave_back, 2)
    vector = tie(vector + vector_got, leave_back)
    vector_got = swap_ctx(vector)
    send_both = tie(jnp.stack([row_down[1::2], row_up[1::2]]).astype(bf16), leave_back)
    got_both = swap_tp(send_both, 1)
    leave_last = tie(add(keep_last[1], got_last[1]).astype(bf16), leave_back)
    got_last_row = swap_row(leave_last)
    vector = tie(vector + vector_got, leave_last)
    vector_got = swap_row(vector)
    entry = row_width
    row_last = add(add(keep_last[0], got_last[0]), got_last_row)
    send_one = row_last[entry : 2 * entry].astype(bf16)
    got_one = swap_tp(send_one, 1)
    leave_both = tie(
        jnp.stack([add(row_down[2], got_both[0, 1]), add(row_up[2], got_both[1, 1])]).astype(bf16), send_one, got_back_two
    )
    got_both_two = swap_tp(leave_both, 2)
    vector = tie(vector + vector_got, leave_both)
    vector_got = swap_tp(vector, 1)
    input_own, input_other = input_rows(
        once(place, leave_both), d_first, (keep_back, got_back, got_back_two), own_rows, other_rows, clip_in_row
    )
    input_grad = home(input_own, swap_ctx(input_other))
    out_two = add(row_last[0:entry], got_one)
    leave_two = out_two[:, col_width:].astype(bf16)
    got_two = swap_tp(leave_two, 2)
    low_both = add(
        jnp.stack([add(row_down[0], got_both[0, 0]), add(row_up[0], got_both[1, 0])]), got_both_two
    ).astype(bf16)
    low_out = add(out_two[:, :col_width], got_two)
    low_last = jnp.concatenate(
        [
            row_last[2 * entry : 3 * entry],
            jnp.concatenate([row_last[3 * entry : 4 * entry, :col_width], low_out], axis=1),
            row_last[4 * entry :],
        ],
        axis=0,
    ).astype(bf16)
    sum_last = add(low_last, swap_ctx(low_last))
    vector = tie(vector + vector_got, low_both)
    vector = vector + swap_tp(vector, 2)

    both_far = swap_ctx(low_both)
    grad_both = jnp.concatenate(
        [
            jnp.where(ctx_rank == 0, low_both, both_far),
            jnp.where(ctx_rank == 0, both_far, low_both),
        ],
        axis=-1,
    ).astype(f32)
    grad_up = straight(grad_both[1], latent_up, up_quant[0][None], up_quant[1][None])
    grad_down = straight(
        grad_both[0], latent_down, down_quant[0][:, None], down_quant[1][:, None]
    )
    grad_qkv = straight(
        jnp.stack(
            [
                sum_last[:entry, :col_width],
                sum_last[:entry, col_width:],
                sum_last[entry : 2 * entry, :col_width],
            ],
            axis=1,
        ),
        latent_qkv,
        qkv_quant[0][None],
        qkv_quant[1][None],
    )
    grad_out = straight(sum_last[entry : 2 * entry, col_width:], latent_out, out_quant[0][:, None], out_quant[1][:, None])
    grad_qv = sum_last[2 * entry : 2 * entry + 2, :col_width]
    vector_sums = jnp.concatenate([vector[0:1], vector[3:4], vector[1:3], vector[4:6]], axis=0)
    stat_sums = jnp.sum(vector[6:11], axis=-1)
    grad_rows = lax.dynamic_slice_in_dim(vector_sums, fsdp_rank * row_width, row_width, 1)
    grad_bias_up = lax.dynamic_index_in_dim(vector, 11 + tp_rank, 0, keepdims=False)
    denom = stat_sums[2]
    statistics = jnp.stack(
        [
            jnp.sqrt(stat_sums[3] / denom),
            jnp.sqrt(stat_sums[4] / denom),
            jnp.sqrt(stat_sums[0] / denom),
            stat_sums[1] / denom,
        ]
    )
    return (
        layer_out,
        input_grad,
        grad_qkv,
        grad_out,
        grad_up,
        grad_down,
        grad_rows,
        grad_qv,
        grad_bias_up,
        statistics,
    )


def general_body(
    tokens,
    cotangent,
    segment_ids,
    valid_mask,
    latent_qkv,
    latent_out,
    latent_up,
    latent_down,
    qkv_quant,
    up_quant,
    out_quant,
    down_quant,
    bias_qv,
    bias_up,
    row_params,
    clip_in,
    clip_ctx,
    clip_hidden,
    t_qkv,
    t_out,
    t_up,
    t_down,
    t_bias_qv,
    t_bias_up,
    t_rows,
):
    local_len, seq_count, width = tokens.shape
    share = cotangent.shape[0]
    col_width = latent_qkv.shape[2]
    hidden_width = latent_up.shape[1]
    row_width = latent_qkv.shape[0]
    local_heads = col_width // HEAD_DIM
    scale = HEAD_DIM ** (-0.5)
    tp_rank = lax.axis_index("tp")
    ctx_rank = lax.axis_index("ctx")
    fsdp_rank = lax.axis_index("fsdp")
    full_len = local_len * lax.axis_size("ctx")
    bin_qkv = binarize(latent_qkv, qkv_quant[0][None], qkv_quant[1][None])
    bin_out = binarize(latent_out, out_quant[0][:, None], out_quant[1][:, None])
    bin_up = binarize(latent_up, up_quant[0][None], up_quant[1][None])
    bin_down = binarize(latent_down, down_quant[0][:, None], down_quant[1][:, None])
    gathered = (
        lax.all_gather(bin_qkv, "fsdp", axis=0, tiled=True),
        lax.all_gather(bin_out, "fsdp", axis=0, tiled=True),
        lax.all_gather(bin_up, "fsdp", axis=0, tiled=True),
        lax.all_gather(bin_down, "fsdp", axis=0, tiled=True),
        lax.all_gather(t_qkv, "fsdp", axis=0, tiled=True),
        lax.all_gather(t_out, "fsdp", axis=0, tiled=True),
        lax.all_gather(t_up, "fsdp", axis=0, tiled=True),
        lax.all_gather(t_down, "fsdp", axis=0, tiled=True),
    )
    full_qkv, full_out, full_up, full_down, teach_qkv, teach_out, teach_up, teach_down = gathered
    stream = tokens.astype(jnp.float32)
    a_in = jnp.clip(stream, -clip_in, clip_in).astype(jnp.bfloat16)
    proj_student = jnp.einsum("tsd,dkh->tskh", a_in, full_qkv, preferred_element_type=jnp.float32)
    proj_teacher = jnp.einsum(
        "tsd,dkh->tskh", tokens, teach_qkv, preferred_element_type=jnp.float32
    )
    student_q = (proj_student[:, :, 0] + bias_qv[0]).astype(jnp.bfloat16)
    student_k = proj_student[:, :, 1].astype(jnp.bfloat16)
    student_v = (proj_student[:, :, 2] + bias_qv[1]).astype(jnp.bfloat16)
    teacher_q = (proj_teacher[:, :, 0] + t_bias_qv[0]).astype(jnp.bfloat16)
    teacher_k = proj_teacher[:, :, 1].astype(jnp.bfloat16)
    teacher_v = (proj_teacher[:, :, 2] + t_bias_qv[1]).astype(jnp.bfloat16)
    student_queries = headed(student_q)
    teacher_queries = headed(teacher_q)
    query_pos = ctx_rank * local_len + jnp.arange(local_len, dtype=jnp.int32)
    key_tags = jnp.transpose(jnp.where(valid_mask > 0, segment_ids, -1))
    empty_state = (
        jnp.full((seq_count, local_heads, local_len), floor_score, jnp.float32),
        jnp.zeros((seq_count, local_heads, local_len), jnp.float32),
        jnp.zeros((seq_count, local_heads, local_len, HEAD_DIM), jnp.float32),
    )
    buffers = (
        jnp.zeros((full_len, seq_count, col_width), jnp.bfloat16),
        jnp.zeros((full_len, seq_count, col_width), jnp.bfloat16),
        jnp.zeros((full_len, seq_count), jnp.int32),
    )
    carry = (empty_state, empty_state, buffers)
    pieces = (
        lax.all_gather(student_k, "ctx", axis=0, tiled=True),
        lax.all_gather(student_v, "ctx", axis=0, tiled=True),
        lax.all_gather(teacher_k, "ctx", axis=0, tiled=True),
        lax.all_gather(teacher_v, "ctx", axis=0, tiled=True),
        lax.all_gather(key_tags, "ctx", axis=0, tiled=True),
    )
    start = jnp.int32(0)
    count = pieces[0].shape[0]
    block = key_block(count)

    def inner(states, index):
        offset = index * block
        parts = [lax.dynamic_slice_in_dim(piece, offset, block, 0) for piece in pieces]
        key_pos = offset + jnp.arange(block, dtype=jnp.int32)
        allowed = allowed_pairs(segment_ids, query_pos, parts[4], key_pos)
        states = (
            online_step(
                states[0], student_queries, headed(parts[0]), headed(parts[1]), allowed, scale
            ),
            online_step(
                states[1], teacher_queries, headed(parts[2]), headed(parts[3]), allowed, scale
            ),
        )
        return (states, None)

    states, _ = lax.scan(inner, (carry[0], carry[1]), jnp.arange(count // block, dtype=jnp.int32))
    kept = tuple(
        (
            lax.dynamic_update_slice_in_dim(buffer, piece, start, 0)
            for buffer, piece in zip(carry[2], (pieces[0], pieces[1], pieces[4]))
        )
    )
    student_state, teacher_state, kept = (states[0], states[1], kept)
    attended, log_total = finish(student_state)
    teacher_attended, _ = finish(teacher_state)
    attended_flat = attended.reshape(local_len, seq_count, col_width)
    ctx_ratio = jnp.tanh(attended_flat / clip_ctx)
    context = (clip_ctx * ctx_ratio).astype(jnp.bfloat16)
    teacher_context = teacher_attended.reshape(local_len, seq_count, col_width).astype(jnp.bfloat16)
    rows_student = context
    rows_teacher = teacher_context
    attn_both = lax.psum_scatter(
        jnp.concatenate(
            [
                jnp.einsum(
                    "tsh,dh->tsd", rows_student, full_out, preferred_element_type=jnp.float32
                ),
                jnp.einsum(
                    "tsh,dh->tsd", rows_teacher, teach_out, preferred_element_type=jnp.float32
                ),
            ],
            axis=-1,
        ).astype(jnp.bfloat16),
        "tp",
        scatter_dimension=0,
        tiled=True,
    ).astype(jnp.float32)
    attn_student = attn_both[..., :width] + row_params[0]
    attn_teacher = attn_both[..., width:] + t_rows[0]
    stream_rows = lax.dynamic_slice_in_dim(stream, tp_rank * share, share, 0)
    first_sum = stream_rows + attn_student
    h_one = layer_norm(first_sum, row_params[2], row_params[3])
    h_teacher = layer_norm(stream_rows + attn_teacher, t_rows[2], t_rows[3])
    h_full, h_teacher_full = (
        lax.all_gather(h_one.astype(jnp.bfloat16), "tp", axis=0, tiled=True),
        lax.all_gather(h_teacher.astype(jnp.bfloat16), "tp", axis=0, tiled=True),
    )
    upper = jnp.einsum("tsd,df->tsf", h_full, full_up, preferred_element_type=jnp.float32) + bias_up
    activated = exact_gelu(upper)
    hid_ratio = jnp.tanh(activated / clip_hidden)
    hidden = (clip_hidden * hid_ratio).astype(jnp.bfloat16)
    upper_teacher = (
        jnp.einsum("tsd,df->tsf", h_teacher_full, teach_up, preferred_element_type=jnp.float32)
        + t_bias_up
    )
    hidden_teacher = exact_gelu(upper_teacher).astype(jnp.bfloat16)
    rows_student = hidden
    rows_teacher = hidden_teacher
    ffn_both = lax.psum_scatter(
        jnp.concatenate(
            [
                jnp.einsum(
                    "tsf,df->tsd", rows_student, full_down, preferred_element_type=jnp.float32
                ),
                jnp.einsum(
                    "tsf,df->tsd", rows_teacher, teach_down, preferred_element_type=jnp.float32
                ),
            ],
            axis=-1,
        ).astype(jnp.bfloat16),
        "tp",
        scatter_dimension=0,
        tiled=True,
    ).astype(jnp.float32)
    ffn_student = ffn_both[..., :width] + row_params[1]
    ffn_teacher = ffn_both[..., width:] + t_rows[1]
    second_sum = h_one + ffn_student
    out = layer_norm(second_sum, row_params[4], row_params[5])
    teacher_out = layer_norm(h_teacher + ffn_teacher, t_rows[4], t_rows[5])
    layer_out = out.astype(jnp.bfloat16)
    valid_rows = jnp.transpose(
        lax.dynamic_slice_in_dim(valid_mask, tp_rank * share, share, 1)
    ).astype(jnp.float32)[..., None]
    difference = out - teacher_out
    grad_out_total = cotangent.astype(jnp.float32) + valid_rows * difference
    stat_terms = jnp.stack(
        [
            jnp.sum(valid_rows) + 0.0 * jnp.sum(stream_rows[:1, :1, :1]),
            jnp.sum(valid_rows * stream_rows * stream_rows),
            jnp.sum(valid_rows * attn_student * attn_student),
            jnp.sum(valid_rows * ffn_student * ffn_student),
            jnp.sum(valid_rows * difference * difference),
        ]
    )
    _, second_pull = jax.vjp(layer_norm, second_sum, row_params[4], row_params[5])
    d_second, d_gain_two, d_bias_two = second_pull(grad_out_total)
    d_ffn = d_second.astype(jnp.bfloat16)
    d_bias_down = jnp.sum(d_ffn.astype(jnp.float32), axis=(0, 1))
    d_ffn_full = lax.all_gather(d_ffn, "tp", axis=0, tiled=True)
    grad_bin_down = jnp.einsum(
        "tsd,tsf->df", d_ffn_full, hidden, preferred_element_type=jnp.float32
    )
    d_hidden = jnp.einsum("tsd,df->tsf", d_ffn_full, full_down, preferred_element_type=jnp.float32)
    d_hidden = d_hidden * (1.0 - hid_ratio * hid_ratio)
    _, gelu_pull = jax.vjp(exact_gelu, upper)
    d_upper = gelu_pull(d_hidden)[0].astype(jnp.bfloat16)
    d_bias_up = jnp.sum(d_upper.astype(jnp.float32), axis=(0, 1))
    grad_bin_up = jnp.einsum("tsd,tsf->df", h_full, d_upper, preferred_element_type=jnp.float32)
    rows = d_upper
    d_h_one = d_second + lax.psum_scatter(
        jnp.einsum("tsf,df->tsd", rows, full_up, preferred_element_type=jnp.float32).astype(
            jnp.bfloat16
        ),
        "tp",
        scatter_dimension=0,
        tiled=True,
    ).astype(jnp.float32)
    _, first_pull = jax.vjp(layer_norm, first_sum, row_params[2], row_params[3])
    d_first, d_gain_one, d_bias_one = first_pull(d_h_one)
    d_attn = d_first.astype(jnp.bfloat16)
    d_bias_out = jnp.sum(d_attn.astype(jnp.float32), axis=(0, 1))
    d_attn_full = lax.all_gather(d_attn, "tp", axis=0, tiled=True)
    grad_bin_out = jnp.einsum(
        "tsd,tsh->dh", d_attn_full, context, preferred_element_type=jnp.float32
    )
    d_context = jnp.einsum("tsd,dh->tsh", d_attn_full, full_out, preferred_element_type=jnp.float32)
    d_attended = (d_context * (1.0 - ctx_ratio * ctx_ratio)).astype(jnp.bfloat16)
    d_attended_heads = headed(d_attended)
    delta = jnp.transpose(
        jnp.sum(d_attended_heads.astype(jnp.float32) * attended, axis=-1), (1, 2, 0)
    )
    key_all, value_all, tag_all = kept
    back_block = key_block(full_len)

    def back_step(grad_q, index):
        offset = index * back_block
        keys = headed(lax.dynamic_slice_in_dim(key_all, offset, back_block, 0))
        values = headed(lax.dynamic_slice_in_dim(value_all, offset, back_block, 0))
        block_tags = lax.dynamic_slice_in_dim(tag_all, offset, back_block, 0)
        key_pos = offset + jnp.arange(back_block, dtype=jnp.int32)
        allowed = allowed_pairs(segment_ids, query_pos, block_tags, key_pos)
        current = grad_q
        scores = (
            jnp.einsum("tshe,kshe->shtk", student_queries, keys, preferred_element_type=jnp.float32)
            * scale
        )
        probs = jnp.where(allowed, jnp.exp(scores - log_total[..., None]), 0.0)
        d_probs = jnp.einsum(
            "tshe,kshe->shtk", d_attended_heads, values, preferred_element_type=jnp.float32
        )
        d_scores = (probs * (d_probs - delta[..., None])).astype(jnp.bfloat16)
        current = (
            current
            + jnp.einsum("shtk,kshe->shte", d_scores, keys, preferred_element_type=jnp.float32)
            * scale
        )
        grad_k = (
            jnp.einsum(
                "shtk,tshe->kshe", d_scores, student_queries, preferred_element_type=jnp.float32
            )
            * scale
        )
        grad_v = jnp.einsum(
            "shtk,tshe->kshe",
            probs.astype(jnp.bfloat16),
            d_attended_heads,
            preferred_element_type=jnp.float32,
        )
        joined = jnp.concatenate(
            [
                grad_k.reshape(back_block, seq_count, col_width),
                grad_v.reshape(back_block, seq_count, col_width),
            ],
            axis=-1,
        )
        return (current, joined)

    grad_q, key_terms = lax.scan(
        back_step,
        jnp.zeros((seq_count, local_heads, local_len, HEAD_DIM), jnp.float32),
        jnp.arange(full_len // back_block, dtype=jnp.int32),
    )
    key_terms = key_terms.reshape(full_len, seq_count, 2 * col_width)
    key_sums = lax.psum_scatter(
        key_terms.astype(jnp.bfloat16), "ctx", scatter_dimension=0, tiled=True
    ).astype(jnp.float32)
    grad_q_flat = jnp.transpose(grad_q, (2, 0, 1, 3)).reshape(local_len, seq_count, col_width)
    d_proj = jnp.stack(
        [grad_q_flat, key_sums[..., :col_width], key_sums[..., col_width:]], axis=2
    ).astype(jnp.bfloat16)
    d_bias_qv = jnp.stack(
        [
            jnp.sum(d_proj[:, :, 0].astype(jnp.float32), axis=(0, 1)),
            jnp.sum(d_proj[:, :, 2].astype(jnp.float32), axis=(0, 1)),
        ]
    )
    grad_bin_qkv = jnp.einsum("tsd,tskh->dkh", a_in, d_proj, preferred_element_type=jnp.float32)
    rows = d_proj
    through = lax.psum_scatter(
        jnp.einsum("tskh,dkh->tsd", rows, full_qkv, preferred_element_type=jnp.float32).astype(
            jnp.bfloat16
        ),
        "tp",
        scatter_dimension=0,
        tiled=True,
    ).astype(jnp.float32)
    input_grad = d_first + through * (jnp.abs(stream_rows) < clip_in).astype(jnp.float32)
    shards = (
        lax.psum_scatter(
            grad_bin_qkv.astype(jnp.bfloat16), "fsdp", scatter_dimension=0, tiled=True
        ).astype(jnp.float32),
        lax.psum_scatter(
            grad_bin_out.astype(jnp.bfloat16), "fsdp", scatter_dimension=0, tiled=True
        ).astype(jnp.float32),
        lax.psum_scatter(
            grad_bin_up.astype(jnp.bfloat16), "fsdp", scatter_dimension=0, tiled=True
        ).astype(jnp.float32),
        lax.psum_scatter(
            grad_bin_down.astype(jnp.bfloat16), "fsdp", scatter_dimension=0, tiled=True
        ).astype(jnp.float32),
    )
    summed = (
        lax.psum(shards[0].astype(jnp.bfloat16), "ctx").astype(jnp.float32),
        lax.psum(shards[1].astype(jnp.bfloat16), "ctx").astype(jnp.float32),
        lax.psum(shards[2].astype(jnp.bfloat16), "ctx").astype(jnp.float32),
        lax.psum(shards[3].astype(jnp.bfloat16), "ctx").astype(jnp.float32),
    )
    grad_qkv = straight(summed[0], latent_qkv, qkv_quant[0][None], qkv_quant[1][None])
    grad_out = straight(summed[1], latent_out, out_quant[0][:, None], out_quant[1][:, None])
    grad_up = straight(summed[2], latent_up, up_quant[0][None], up_quant[1][None])
    grad_down = straight(summed[3], latent_down, down_quant[0][:, None], down_quant[1][:, None])
    vector_grads = jnp.stack(
        [d_bias_out, d_bias_down, d_gain_one, d_bias_one, d_gain_two, d_bias_two]
    )
    placed_qv = lax.dynamic_update_slice_in_dim(
        jnp.zeros((2, width), jnp.float32), d_bias_qv, tp_rank * col_width, 1
    )
    placed_up = lax.dynamic_update_slice_in_dim(
        jnp.zeros((hidden_width * lax.axis_size("tp"),), jnp.float32),
        d_bias_up,
        tp_rank * hidden_width,
        0,
    )
    stat_sums, vector_sums, qv_sums, up_sums = lax.psum(
        (stat_terms, vector_grads, placed_qv, placed_up), ("fsdp", "ctx", "tp")
    )
    grad_rows = lax.dynamic_slice_in_dim(vector_sums, fsdp_rank * row_width, row_width, 1)
    grad_qv = lax.dynamic_slice_in_dim(qv_sums, tp_rank * col_width, col_width, 1)
    grad_bias_up = lax.dynamic_slice_in_dim(up_sums, tp_rank * hidden_width, hidden_width, 0)
    denom = stat_sums[0] * width
    statistics = jnp.stack(
        [
            jnp.sqrt(stat_sums[1] / denom),
            jnp.sqrt(stat_sums[2] / denom),
            jnp.sqrt(stat_sums[3] / denom),
            stat_sums[4] / denom,
        ]
    )
    return (
        layer_out,
        input_grad,
        grad_qkv,
        grad_out,
        grad_up,
        grad_down,
        grad_rows,
        grad_qv,
        grad_bias_up,
        statistics,
    )


def pick_body(mesh):
    sizes = dict(mesh.shape)
    if sizes["fsdp"] == 4 and sizes["tp"] == 4 and sizes["ctx"] == 2:
        return paired_body
    return general_body


def solution(mesh):
    return jax.shard_map(
        pick_body(mesh),
        mesh=mesh,
        in_specs=(
            P("ctx", "fsdp", None),
            P(("ctx", "tp"), "fsdp", None),
            P("fsdp", "ctx"),
            P("fsdp", "ctx"),
            P("fsdp", None, "tp"),
            P("fsdp", "tp"),
            P("fsdp", "tp"),
            P("fsdp", "tp"),
            P(None, None, "tp"),
            P(None, "tp"),
            P(None, "fsdp"),
            P(None, "fsdp"),
            P(None, "tp"),
            P("tp"),
            P(),
            P(),
            P("tp"),
            P("tp"),
            P("fsdp", None, "tp"),
            P("fsdp", "tp"),
            P("fsdp", "tp"),
            P("fsdp", "tp"),
            P(None, "tp"),
            P("tp"),
            P(),
        ),
        out_specs=(
            P(("ctx", "tp"), "fsdp", None),
            P(("ctx", "tp"), "fsdp", None),
            P("fsdp", None, "tp"),
            P("fsdp", "tp"),
            P("fsdp", "tp"),
            P("fsdp", "tp"),
            P(None, "fsdp"),
            P(None, "tp"),
            P("tp"),
            P(),
        ),
        check_vma=False,
    )
```

```python
import functools
import math

import jax
import jax.numpy as jnp
from jax import lax
from jax.experimental import pallas as pl
from jax.experimental.pallas import tpu as pltpu
from jax.sharding import PartitionSpec as P

HEAD_DIM = 64


epsilon = 1e-05
floor_score = -1e30


def binarize(latent, shift, scales):
    return (scales * jnp.sign(latent - shift)).astype(jnp.bfloat16)


def straight(summed, latent, shift, scales):
    inside = (jnp.abs(latent - shift) < 1.0).astype(jnp.float32)
    return summed * scales * inside


def layer_norm(stream, gains, biases):
    centred = stream - jnp.mean(stream, axis=-1, keepdims=True)
    spread = jnp.mean(centred * centred, axis=-1, keepdims=True)
    return centred * lax.rsqrt(spread + epsilon) * gains + biases


def exact_gelu(values):
    return jax.nn.gelu(values, approximate=False)


def key_block(count):
    return math.gcd(count, 512)


def headed(array):
    return array.reshape(array.shape[0], array.shape[1], array.shape[2] // HEAD_DIM, HEAD_DIM)


def allowed_pairs(query_seg, query_pos, key_tags, key_pos):
    same = query_seg[:, :, None] == jnp.transpose(key_tags)[:, None, :]
    diagonal = query_pos[:, None] == key_pos[None, :]
    return (same | diagonal[None])[:, None]


def online_step(state, queries, keys, values, allowed, scale):
    running, total, accum = state
    scores = (
        jnp.einsum("tshe,kshe->shtk", queries, keys, preferred_element_type=jnp.float32) * scale
    )
    scores = jnp.where(allowed, scores, floor_score)
    newest = jnp.maximum(running, jnp.max(scores, axis=-1))
    weights = jnp.where(allowed, jnp.exp(scores - newest[..., None]), 0.0)
    factor = jnp.exp(running - newest)
    total = total * factor + jnp.sum(weights, axis=-1)
    accum = accum * factor[..., None] + jnp.einsum(
        "shtk,kshe->shte", weights.astype(jnp.bfloat16), values, preferred_element_type=jnp.float32
    )
    return (newest, total, accum)


def finish(state):
    running, total, accum = state
    merged = accum / total[..., None]
    return (jnp.transpose(merged, (2, 0, 1, 3)), running + jnp.log(total))


WORK_FACTOR = 4
TOKEN = (8, 128)
ROOM = 8 * 2**20


def vmem_specs(count):
    return [pl.BlockSpec(memory_space=pltpu.VMEM)] * count


def vmem_room(inputs, outs, scratch):
    total = 0
    for array in (*inputs, *jax.tree.leaves(outs), *scratch):
        if not jnp.issubdtype(array.dtype, jnp.number):
            continue
        *lead, rows, lanes = (1, 1, *array.shape)
        size = jnp.dtype(array.dtype).itemsize
        tile = 8 * (4 // size)
        total += math.prod(lead) * size * (-(-rows // tile) * tile) * (-(-lanes // 128) * 128)
    return min(total + ROOM, 60 * 2**20)


def call_kernel(kernel, place, inputs, outs, scratch=(), flops=0, moved=0, exps=0, from_hbm=False):
    place, after = place if isinstance(place, tuple) else (place, ())

    def body(place_ref, *refs):
        kernel(place_ref, *refs[len(after) :])

    return pl.pallas_call(
        body,
        out_shape=outs,
        in_specs=[pl.BlockSpec(memory_space=pltpu.SMEM)]
        + [pl.BlockSpec(memory_space=pl.ANY)] * len(after)
        + ([pl.BlockSpec(memory_space=pltpu.HBM)] * len(inputs) if from_hbm else vmem_specs(len(inputs))),
        out_specs=jax.tree.map(lambda _: pl.BlockSpec(memory_space=pltpu.VMEM), outs),
        scratch_shapes=list(scratch),
        compiler_params=pltpu.CompilerParams(vmem_limit_bytes=vmem_room(inputs, outs, scratch)),
        cost_estimate=pl.CostEstimate(
            flops=WORK_FACTOR * flops, bytes_accessed=moved, transcendentals=exps
        ),
    )(place, *after, *inputs)


def shaped(shape, dtype):
    return jax.ShapeDtypeStruct(shape, dtype)


def gate_kernel(place_ref, token_ref):
    token_ref[...] = jnp.zeros_like(token_ref)


def gate(place, *arrays):
    return call_kernel(gate_kernel, (place, arrays), (), shaped(TOKEN, jnp.float32), flops=1, moved=1)


NT = (((1,), (1,)), ((), ()))


def dot_nt(left, right):
    return lax.dot_general(left, right, NT, preferred_element_type=jnp.float32)


def dot_nn(left, right):
    return jnp.dot(left, right, preferred_element_type=jnp.float32)


QUERY_BLOCK = 256


def place_projections(place_ref, pieces, target, first):
    size, cols = pieces[0].shape[1], target.shape[2]
    for kind in range(3):
        for distance, piece in zip((0, 2, 1, 3), pieces):
            start = pl.multiple_of((place_ref[0] ^ distance) * size, 64)
            target[kind, pl.ds(start, size), :] = piece[kind, :, first : first + cols]


def project_kernel(place_ref, own_ref, w0, w2, w1, w3, bias_ref, clip_in_ref, full_ref, a_ref, q_ref, token_ref):
    place_projections(place_ref, (w0, w2, w1, w3), full_ref, 0)
    clipped = jnp.clip(own_ref[...].astype(jnp.float32), -clip_in_ref[...], clip_in_ref[...])
    clipped = clipped.astype(jnp.bfloat16)
    a_ref[...] = clipped
    write_heads(clipped, full_ref, bias_ref, q_ref, 0)
    token_ref[...] = jnp.zeros_like(token_ref)


def write_heads(inputs, w_ref, bias_ref, target, base):
    rows = inputs.shape[0]
    for kind in range(3):
        values = dot_nn(inputs, w_ref[kind])
        if kind != 1:
            values = values + bias_ref[kind >> 1 : (kind >> 1) + 1, :]
        values = values.astype(jnp.bfloat16)
        if kind == 0:
            values = values * (HEAD_DIM**-0.5)
        for head in range(target.shape[1]):
            target[kind, head, base : base + rows, :] = values[:, head * HEAD_DIM : (head + 1) * HEAD_DIM]


def project_own(place, own, pieces, bias, clip_in):
    half, width = own.shape
    cols = pieces[0].shape[-1] // 2
    heads = cols // HEAD_DIM
    bf16 = jnp.bfloat16
    return call_kernel(
        project_kernel,
        place,
        (own, *pieces, bias, clip_in),
        (
            shaped((3, width, cols), bf16),
            shaped((half, width), bf16),
            shaped((3, heads, half, HEAD_DIM), bf16),
            shaped(TOKEN, jnp.float32),
        ),
        flops=1,
        moved=1,
    )


def unit_matrix():
    shape = (HEAD_DIM, HEAD_DIM)
    ones = lax.broadcasted_iota(jnp.int32, shape, 0) == lax.broadcasted_iota(jnp.int32, shape, 1)
    return ones.astype(jnp.bfloat16)


def block_window(row_ref, place_ref, blocks):
    mask = order_mask(place_ref)
    low, high = [], []
    for block in range(blocks):
        segment = row_ref[:, block * QUERY_BLOCK : (block + 1) * QUERY_BLOCK] >> 1
        low.append(jnp.min(segment))
        high.append(jnp.max(segment))
    windows = []
    for query in range(blocks):
        first, last = jnp.int32(blocks - 1), jnp.int32(0)
        for key in range(blocks):
            meets = (low[key] <= high[query]) & (high[key] >= low[query])
            at = key ^ mask
            first = jnp.where(meets, jnp.minimum(first, at), first)
            last = jnp.where(meets, jnp.maximum(last, at), last)
        windows.append((first, last - first + 1))
    return windows


def order_mask(place_ref):
    return 2 * place_ref[2] + (place_ref[1] >> 1)


def pick(values, index):
    chosen = values[0]
    for at in range(1, len(values)):
        chosen = jnp.where(index == at, values[at], chosen)
    return chosen


def pair_bias(col_ref, row_ref, query, key):
    size = QUERY_BLOCK
    code_col = col_ref[pl.ds(pl.multiple_of(key * size, size), size), :]
    code_row = row_ref[:, pl.ds(pl.multiple_of(query * size, size), size)]
    tags = jnp.where((code_col & 1) > 0, code_col >> 1, -1)
    apart = lax.broadcasted_iota(jnp.int32, (size, size), 0) - lax.broadcasted_iota(
        jnp.int32, (size, size), 1
    )
    allowed = (tags == (code_row >> 1)) | (apart == (query - key) * size)
    return jnp.where(allowed, 0.0, floor_score)


def each_count(windows, query, blocks, body):
    first = pick([w[0] for w in windows], query)
    count = pick([w[1] for w in windows], query)
    for fixed in range(1, blocks + 1):

        @pl.when(count == fixed)
        def _():
            body(first, fixed)


def attention_kernel(
    student, place_ref, other_ref, bias_ref, clip_in_ref, clip_ref, col_ref, row_ref, *refs
):
    if student:
        w_ref, part_ref, *c_refs = refs[:6]
        a_ref, rows_ref, qkv_ref, merged_ref, lse_ref, vt_ref, bias_at, score_ref, sum_ref = refs[6:]
    else:
        pieces, own_ref, c_refs, token_ref = refs[:4], refs[4], refs[5:9], refs[9]
        w_ref, qkv_ref, vt_ref, bias_at, score_ref, sum_ref = refs[10:]
        token_ref[...] = jnp.zeros_like(token_ref)
    half = qkv_ref.shape[2] // 2
    heads = qkv_ref.shape[1]
    cols = heads * HEAD_DIM
    size = QUERY_BLOCK
    blocks = 2 * half // size
    bf16, f32 = jnp.bfloat16, jnp.float32
    inputs = other_ref[0:half, :]
    if student:
        qkv_ref[:, :, 0:half, :] = part_ref[...]
        inputs = jnp.clip(inputs.astype(f32), -clip_in_ref[...], clip_in_ref[...]).astype(bf16)
        a_ref[...] = inputs
        rows_ref[...] = other_ref[0 : half // 4, :]
    else:
        place_projections(place_ref, pieces, w_ref, w_ref.shape[2])
        write_heads(own_ref[...], w_ref, bias_ref, qkv_ref, 0)
    write_heads(inputs, w_ref, bias_ref, qkv_ref, half)
    eye = unit_matrix()
    for head in range(heads):
        vt_ref[head] = dot_nt(eye, qkv_ref[2, head]).astype(bf16)
    windows = block_window(row_ref, place_ref, blocks)
    mask = order_mask(place_ref)
    sum_ref[...] = jnp.zeros_like(sum_ref)

    def one_query(query, carry):
        at = pl.multiple_of(query * size, size)

        def body(first, count):
            keys = [(first + step) ^ mask for step in range(count)]
            starts = [pl.multiple_of(key * size, size) for key in keys]
            for step in range(count):
                bias_at[step] = pair_bias(col_ref, row_ref, query, keys[step])
            for head in range(heads):
                queries = qkv_ref[0, head, pl.ds(at, size), :]
                top = None
                for step in range(count):
                    scores = bias_at[step] + dot_nt(
                        qkv_ref[1, head, pl.ds(starts[step], size), :], queries
                    )
                    score_ref[step] = scores
                    part = jnp.max(scores, axis=0, keepdims=True)
                    top = part if top is None else jnp.maximum(top, part)
                total, merged = 0.0, 0.0
                for step in range(count):
                    weights = jnp.exp(score_ref[step] - top)
                    total = total + jnp.sum(weights, axis=0, keepdims=True)
                    merged = merged + dot_nn(
                        vt_ref[head, :, pl.ds(starts[step], size)], weights.astype(bf16)
                    )
                sum_ref[head * HEAD_DIM : (head + 1) * HEAD_DIM, :] = merged * (1.0 / total)
                if student:
                    lse_ref[head : head + 1, pl.ds(at, size)] = top + jnp.log(total)

        each_count(windows, query, blocks, body)
        if student:
            merged_ref[:, pl.ds(at, size)] = sum_ref[0:cols, :]
        merged = jnp.transpose(sum_ref[...])[:, :cols]
        if student:
            merged = clip_ref[...] * jnp.tanh(merged / clip_ref[...])
        merged = merged.astype(bf16)
        share = size // 2
        for at in range(blocks):

            @pl.when(query == at)
            def _():
                lanes = slice((at >> 1) * cols, ((at >> 1) + 1) * cols)
                c_refs[2 * (at & 1)][:, lanes] = merged[:share]
                c_refs[2 * (at & 1) + 1][:, lanes] = merged[share:]

        return carry

    lax.fori_loop(0, blocks, one_query, 0)


def attention_forward(student, place, other, weights, parts, bias, clip_in, clip, code_col, code_row):
    width = other.shape[1]
    half = parts.shape[2] if student else parts.shape[0]
    cols = clip.shape[-1]
    heads = cols // HEAD_DIM
    count = 2 * half
    bf16, f32 = jnp.bfloat16, jnp.float32
    qkv = (3, heads, count, HEAD_DIM)
    c_shape = (shaped((half // 4, 2 * cols), bf16),) * 4
    scratch = (
        pltpu.VMEM((heads, HEAD_DIM, count), bf16),
        pltpu.VMEM((count // QUERY_BLOCK, QUERY_BLOCK, QUERY_BLOCK), f32),
        pltpu.VMEM((count // QUERY_BLOCK, QUERY_BLOCK, QUERY_BLOCK), f32),
        pltpu.VMEM((256, QUERY_BLOCK), f32),
    )
    if student:
        outs = (
            *c_shape,
            shaped((half, width), bf16),
            shaped((half // 4, width), bf16),
            shaped(qkv, bf16),
            shaped((cols, count), f32),
            shaped((8, count), f32),
        )
        inputs = (weights, parts)
    else:
        outs = (*c_shape, shaped(TOKEN, f32))
        scratch = (pltpu.VMEM((3, width, cols), bf16), pltpu.VMEM(qkv, bf16), *scratch)
        inputs = (*weights, parts)
    return call_kernel(
        functools.partial(attention_kernel, student),
        place,
        (other, bias, clip_in, clip, code_col, code_row, *inputs),
        outs,
        scratch,
        flops=2 * half * width * cols * 3 + 4 * count * count * cols,
        moved=6 * count * width,
        exps=heads * count * count,
    )


def attention_pull_kernel(
    place_ref,
    qkv_ref,
    clip_ref,
    merged_ref,
    lse_ref,
    col_ref,
    row_ref,
    d0_ref,
    d1_ref,
    d2_ref,
    d3_ref,
    w_ref,
    keep_ref,
    send_ref,
    dproj_ref,
    sums_ref,
    grad_ref,
    kt_ref,
    dk_ref,
    dv_ref,
    sum_ref,
    delta_ref,
    bias_at,
):
    _, heads, count, _ = qkv_ref.shape
    cols = heads * HEAD_DIM
    size = QUERY_BLOCK
    share = size // 2
    blocks = count // size
    bf16, f32 = jnp.bfloat16, jnp.float32
    eye = unit_matrix()
    for head in range(heads):
        kt_ref[head] = dot_nt(eye, qkv_ref[1, head]).astype(bf16)
    for distance, source in enumerate((d0_ref, d1_ref, d2_ref, d3_ref)):
        for part in range(2):
            at = part * (count // 2) + distance * share
            merged = merged_ref[:, at : at + share]
            wide = jnp.concatenate([merged, jnp.zeros((256 - cols, share), f32)], axis=0)
            ratio = jnp.tanh(jnp.transpose(wide)[:, :cols] / clip_ref[...])
            grad = (source[:, part * cols : (part + 1) * cols].astype(f32) * (1.0 - ratio * ratio)).astype(bf16)
            for head in range(heads):
                grad_ref[head, at : at + share, :] = grad[:, head * HEAD_DIM : (head + 1) * HEAD_DIM]
            wide = jnp.concatenate(
                [grad.astype(f32), jnp.zeros((share, 256 - cols), f32)], axis=1
            )
            turned = jnp.transpose(wide)[:cols] * merged
            for head in range(heads):
                delta_ref[head : head + 1, at : at + share] = jnp.sum(
                    turned[head * HEAD_DIM : (head + 1) * HEAD_DIM], axis=0, keepdims=True
                )
    dk_ref[...] = jnp.zeros_like(dk_ref)
    dv_ref[...] = jnp.zeros_like(dv_ref)
    windows = block_window(row_ref, place_ref, blocks)
    mask = order_mask(place_ref)
    sum_ref[...] = jnp.zeros_like(sum_ref)

    def one_query(query, carry):
        at = pl.multiple_of(query * size, size)

        def body(first, count):
            keys = [(first + step) ^ mask for step in range(count)]
            starts = [pl.multiple_of(key * size, size) for key in keys]
            for step in range(count):
                bias_at[step] = pair_bias(col_ref, row_ref, query, keys[step])
            for head in range(heads):
                queries = qkv_ref[0, head, pl.ds(at, size), :]
                grad = grad_ref[head, pl.ds(at, size), :]
                lse = lse_ref[head : head + 1, pl.ds(at, size)]
                delta = delta_ref[head : head + 1, pl.ds(at, size)]
                merged = 0.0
                for step in range(count):
                    rows = pl.ds(starts[step], size)
                    probs = jnp.exp(
                        dot_nt(qkv_ref[1, head, rows, :], queries) + (bias_at[step] - lse)
                    )
                    d_probs = dot_nt(qkv_ref[2, head, rows, :], grad)
                    d_scores = (probs * (d_probs - delta)).astype(bf16)
                    dv_ref[head, rows, :] += dot_nn(probs.astype(bf16), grad)
                    dk_ref[head, rows, :] += dot_nn(d_scores, queries)
                    merged = merged + dot_nn(kt_ref[head, :, rows], d_scores)
                sum_ref[head * HEAD_DIM : (head + 1) * HEAD_DIM, :] = merged

        each_count(windows, query, blocks, body)
        merged = jnp.transpose(sum_ref[...])[:, :cols] * (HEAD_DIM**-0.5)
        dproj_ref[0, pl.ds(at, size), :] = merged.astype(bf16)
        return carry

    lax.fori_loop(0, blocks, one_query, 0)
    for head in range(heads):
        lanes = slice(head * HEAD_DIM, (head + 1) * HEAD_DIM)
        dproj_ref[1, :, lanes] = dk_ref[head].astype(bf16)
        dproj_ref[2, :, lanes] = dv_ref[head].astype(bf16)
    sums_ref[0:1, :] = jnp.sum(dproj_ref[0].astype(f32), axis=0, keepdims=True)
    sums_ref[1:2, :] = jnp.sum(dproj_ref[2].astype(f32), axis=0, keepdims=True)
    for part in range(2):
        at = slice(part * (count // 2), (part + 1) * (count // 2))
        back = (
            dot_nt(dproj_ref[0, at, :], w_ref[0])
            + dot_nt(dproj_ref[1, at, :], w_ref[1])
            + dot_nt(dproj_ref[2, at, :], w_ref[2])
        ).astype(bf16)
        for distance in range(4):
            target = send_ref if distance & 1 else keep_ref
            target[distance >> 1, part] = back[distance * share : (distance + 1) * share]


def attention_backward(place, qkv, clip, merged, lse, code_col, code_row, grads, weights):
    _, heads, count, _ = qkv.shape
    cols = heads * HEAD_DIM
    width = weights.shape[1]
    bf16, f32 = jnp.bfloat16, jnp.float32
    return call_kernel(
        attention_pull_kernel,
        place,
        (qkv, clip, merged, lse, code_col, code_row, *grads, weights),
        (
            *(shaped((2, 2, count // 8, width), bf16),) * 2,
            shaped((3, count, cols), bf16),
            shaped((2, cols), f32),
        ),
        (
            pltpu.VMEM((heads, count, HEAD_DIM), bf16),
            pltpu.VMEM((heads, HEAD_DIM, count), bf16),
            pltpu.VMEM((heads, count, HEAD_DIM), f32),
            pltpu.VMEM((heads, count, HEAD_DIM), f32),
            pltpu.VMEM((256, QUERY_BLOCK), f32),
            pltpu.VMEM((8, count), f32),
            pltpu.VMEM((count // QUERY_BLOCK, QUERY_BLOCK, QUERY_BLOCK), f32),
        ),
        flops=2 * count * width * cols * 3 + 10 * count * count * cols,
        moved=8 * count * width,
        exps=heads * count * count,
    )


def unit_of(stream):
    mean = jnp.mean(stream, axis=-1, keepdims=True)
    centred = stream - mean
    scale = lax.rsqrt(jnp.mean(centred * centred, axis=-1, keepdims=True) + epsilon)
    return centred * scale, scale


def column_sum(value):
    return jnp.sum(value, axis=0, keepdims=True)


def dot_tn(left, right):
    return lax.dot_general(left, right, (((0,), (0,)), ((), ())), preferred_element_type=jnp.float32)


def out_norm_kernel(student, place_ref, *refs):
    if student:
        c_refs, pieces = refs[:4], refs[4:12]
        own_ref, other_ref, valid_ref, params_ref, cot_ref = refs[12:17]
        w_ref, unit_ref, scale_ref, low_ref, sums_ref, token_ref = refs[17:]
        token_ref[...] = jnp.zeros_like(token_ref)
    else:
        c_refs, w_ref = refs[:4], refs[4]
        own_ref, other_ref, valid_ref, params_ref = refs[5:9]
        wide_ref, low_ref, token_ref = refs[9:]
        token_ref[...] = jnp.zeros_like(token_ref)
    share = own_ref.shape[0]
    cols = c_refs[0].shape[1] // 2
    size = w_ref.shape[1] // 4
    total = None
    for r, source in enumerate(c_refs):
        if student:
            group = pieces[:4] if r % 2 == 0 else pieces[4:]
            for distance, piece in zip((0, 2, 1, 3), group):
                start = pl.multiple_of((place_ref[0] ^ distance) * size, 64)
                w_ref[r, pl.ds(start, size), :] = piece[r >> 1, 2 * size : 3 * size, :]
            weights = w_ref[r, :, 0:cols]
        else:
            weights = w_ref[r, :, cols : 2 * cols]
        context = jnp.concatenate([source[:, 0:cols], source[:, cols:]], axis=0)
        term = dot_nt(context, weights)
        total = term if total is None else total + term
    attn = total + params_ref[0:1, :]
    stream = jnp.concatenate([own_ref[...], other_ref[...]], axis=0).astype(jnp.float32)
    unit, scale = unit_of(stream + attn)
    wide = unit * params_ref[2:3, :] + params_ref[3:4, :]
    low_ref[0 : 2 * share, :] = wide.astype(jnp.bfloat16)
    if student:
        low_ref[2 * share :, :] = cot_ref[...]
        unit_ref[...] = unit
        scale_ref[...] = scale
        valid = valid_ref[...]
        sums_ref[0:1, :] = column_sum(valid * jnp.ones_like(stream))
        sums_ref[1:2, :] = column_sum(valid * stream * stream)
        sums_ref[2:3, :] = column_sum(valid * attn * attn)
    else:
        wide_ref[...] = wide


def out_norm(student, place, contexts, weights, own, other, valid, params, cot=()):
    share, width = own.shape
    rows = 2 * share
    cols = contexts[0].shape[-1] // 2
    f32, bf16 = jnp.float32, jnp.bfloat16
    if student:
        outs = (
            shaped((4, width, 2 * cols), bf16),
            shaped((rows, width), f32),
            shaped((rows, 1), f32),
            shaped((rows + share, width), bf16),
            shaped((3, width), f32),
            shaped(TOKEN, f32),
        )
    else:
        outs = (shaped((rows, width), f32), shaped((rows, width), bf16), shaped(TOKEN, f32))
    return call_kernel(
        functools.partial(out_norm_kernel, student),
        place,
        (*contexts, *(weights if student else (weights,)), own, other, valid, params, *cot),
        outs,
        flops=2 * rows * width * cols * 4,
        moved=12 * rows * width,
    )


def gelu_parts(values):
    cdf = 0.5 * (1.0 + lax.erf(values * (2.0**-0.5)))
    return values * cdf, cdf


def hidden_kernel(student, assemble, far, place_ref, h_ref, *refs):
    refs = list(refs)
    pieces = [refs.pop(0) for _ in range(8 if assemble else 1)]
    with_terms = student and assemble
    terms_ref = None if with_terms else refs.pop(0)
    w_ref = refs.pop(0) if assemble else pieces[0]
    if with_terms:
        terms_ref = refs.pop(0)
    if student:
        hid_ref, slope_ref = refs.pop(0), refs.pop(0)
    part_ref, token_ref = refs
    token_ref[...] = jnp.zeros_like(token_ref)
    bf16 = jnp.bfloat16
    total = None
    inputs = h_ref[0 : part_ref.shape[0], :]
    for r in range(4):
        if assemble:
            group = pieces[:4] if r % 2 == 0 else pieces[4:]
            size = w_ref.shape[2] // 4
            for mat in range(2):
                for distance, piece in zip((0, 2, 1, 3), group):
                    start = pl.multiple_of((place_ref[0] ^ distance) * size, 64)
                    w_ref[r, mat, pl.ds(start, size), :] = piece[r >> 1, mat * size : (mat + 1) * size, :]
        if with_terms:
            terms_ref[r] = group[0][r >> 1, 3 * size : 3 * size + 16, :]
        terms = terms_ref[r].astype(jnp.float32)
        base = 0 if student else 6
        bias = terms[base : base + 1] + terms[base + 1 : base + 2] + terms[base + 2 : base + 3]
        upper = dot_nn(inputs, w_ref[r, 0]) + bias
        active, cdf = gelu_parts(upper)
        if student:
            clip = terms[3:4] + terms[4:5] + terms[5:6]
            ratio = jnp.tanh(active / clip)
            pdf = jnp.exp(-0.5 * upper * upper) * ((2.0 * math.pi) ** -0.5)
            slope_ref[r] = ((1.0 - ratio * ratio) * (cdf + upper * pdf)).astype(bf16)
            hidden = (clip * ratio).astype(bf16)
            hid_ref[r] = hidden
        else:
            hidden = active.astype(bf16)
        term = dot_nt(hidden, w_ref[r, 1])
        total = term if total is None else total + term
    part_ref[...] = total.astype(part_ref.dtype)


def hidden_layer(student, far, place, h, rows, weights, terms=None):
    width = h.shape[-1]
    half = weights[0].shape[-1] if isinstance(weights, tuple) else weights.shape[-1]
    f32, bf16 = jnp.float32, jnp.bfloat16
    assemble = isinstance(weights, tuple)
    outs = []
    if assemble:
        outs.append(shaped((4, 2, width, half), bf16))
        if student:
            outs.append(shaped((4, 16, half), bf16))
    if student:
        outs += [shaped((4, rows, half), bf16)] * 2
    outs += [shaped((rows, width), bf16 if far else f32), shaped(TOKEN, f32)]
    inputs = (h, *(weights if assemble else (weights,))) + (() if terms is None else (terms,))
    return call_kernel(
        functools.partial(hidden_kernel, student, assemble, far),
        place,
        inputs,
        tuple(outs),
        flops=2 * rows * width * half * 8,
        moved=8 * width * half * 2 + 16 * rows * half,
        exps=(3 if student else 1) * rows * half * 4,
    )


def loss_kernel(
    place_ref, unit_ref, ffn_ref, got_ref, ht_ref, ffnt_ref, gott_ref, cot_ref, cot_other_ref, valid_ref, params_ref, t_ref,
    layer_ref, layer_other_ref, dz_ref, low_ref, sums_ref,
):
    share = cot_ref.shape[0]
    rows = 2 * share
    f32, bf16 = jnp.float32, jnp.bfloat16
    h_one = unit_ref[...] * params_ref[2:3, :] + params_ref[3:4, :]
    ffn = ffn_ref[...] + got_ref[...].astype(f32) + params_ref[1:2, :]
    unit, scale = unit_of(h_one + ffn)
    out = unit * params_ref[4:5, :] + params_ref[5:6, :]
    low = out.astype(bf16)
    layer_ref[...] = low[:share]
    layer_other_ref[...] = low[share:]
    t_unit, _ = unit_of(ht_ref[...] + ffnt_ref[...] + gott_ref[...].astype(f32) + t_ref[1:2, :])
    difference = out - (t_unit * t_ref[4:5, :] + t_ref[5:6, :])
    valid = valid_ref[...]
    gap = valid * difference
    arriving = jnp.concatenate([cot_ref[...], cot_other_ref[rows:, :]], axis=0).astype(f32)
    grad = arriving + gap
    inner = grad * params_ref[4:5, :]
    dz = scale * (
        inner
        - jnp.mean(inner, axis=-1, keepdims=True)
        - unit * jnp.mean(inner * unit, axis=-1, keepdims=True)
    )
    dz_ref[...] = dz
    dz_low = dz.astype(bf16)
    low_ref[...] = dz_low
    sums_ref[0:1, :] = column_sum(dz_low.astype(f32))
    sums_ref[1:2, :] = column_sum(grad * unit)
    sums_ref[2:3, :] = column_sum(grad)
    sums_ref[3:4, :] = column_sum(valid * ffn * ffn)
    sums_ref[4:5, :] = column_sum(gap * difference)


def loss_step(place, unit, ffn, got, ht, ffnt, gott, cot, cot_other, valid, params, t_rows):
    rows, width = unit.shape
    share = cot.shape[0]
    f32, bf16 = jnp.float32, jnp.bfloat16
    return call_kernel(
        loss_kernel,
        place,
        (unit, ffn, got, ht, ffnt, gott, cot, cot_other, valid, params, t_rows),
        (
            shaped((share, width), bf16),
            shaped((share, width), bf16),
            shaped((rows, width), f32),
            shaped((rows, width), bf16),
            shaped((5, width), f32),
        ),
        flops=60 * rows * width,
        moved=30 * rows * width,
    )


def hidden_pull_kernel(place_ref, grad_ref, w_ref, slope_ref, du_ref, part_ref, sums_ref):
    grad = grad_ref[0 : part_ref.shape[0], :]
    total = None
    for r in range(4):
        upper = (dot_nn(grad, w_ref[r, 1]) * slope_ref[r].astype(jnp.float32)).astype(jnp.bfloat16)
        du_ref[r] = upper
        sums_ref[r : r + 1, :] = column_sum(upper.astype(jnp.float32))
        term = dot_nt(upper, w_ref[r, 0])
        total = term if total is None else total + term
    part_ref[...] = total.astype(part_ref.dtype)


def hidden_pull(far, place, grad, weights, slope):
    width = grad.shape[-1]
    rows = slope.shape[1]
    half = slope.shape[-1]
    f32, bf16 = jnp.float32, jnp.bfloat16
    return call_kernel(
        hidden_pull_kernel,
        place,
        (grad, weights, slope),
        (shaped((4, rows, half), bf16), shaped((rows, width), bf16 if far else f32), shaped((4, half), f32)),
        flops=2 * rows * width * half * 8,
        moved=8 * width * half * 2 + 16 * rows * half,
    )


def hidden_grads_kernel(mat, place_ref, l0, l1, r0, r1, keep_ref, send_ref, full_ref):
    rows = r0.shape[1]
    left = jnp.transpose(jnp.concatenate([l0[0:rows, :], l1[0:rows, :]], axis=0))
    size = full_ref.shape[0] // 4
    for r in range(4):
        right = jnp.concatenate([r0[r], r1[r]], axis=0)
        full_ref[...] = dot_nn(left, right)
        for slot in range(2):
            for target, distance in ((keep_ref, 2 * slot), (send_ref, 2 * slot + 1)):
                start = pl.multiple_of((place_ref[0] ^ distance) * size, 64)
                target[slot, r] = full_ref[pl.ds(start, size), :].astype(jnp.bfloat16)


def hidden_grads(place, left, right):
    width = left[0].shape[-1]
    rows, half = right[0].shape[1:]
    out = shaped((2, 4, width // 4, half), jnp.bfloat16)
    return call_kernel(
        functools.partial(hidden_grads_kernel, 0),
        place,
        (*left, *right),
        (out, out),
        (pltpu.VMEM((width, half), jnp.float32),),
        flops=16 * rows * width * half * 4,
        moved=8 * width * half * 2,
    )


def first_pull_kernel(place_ref, dz_ref, part_ref, got_ref, unit_ref, scale_ref, params_ref, w_ref, first_ref, low_ref, sums_ref, *ctx_refs):
    f32, bf16 = jnp.float32, jnp.bfloat16
    grad = dz_ref[...] + part_ref[...] + got_ref[...].astype(f32)
    unit = unit_ref[...]
    inner = grad * params_ref[2:3, :]
    first = scale_ref[...] * (
        inner
        - jnp.mean(inner, axis=-1, keepdims=True)
        - unit * jnp.mean(inner * unit, axis=-1, keepdims=True)
    )
    first_ref[...] = first
    low = first.astype(bf16)
    low_ref[...] = low
    sums_ref[0:1, :] = column_sum(low.astype(f32))
    sums_ref[1:2, :] = column_sum(grad * unit)
    sums_ref[2:3, :] = column_sum(grad)
    share, cols = ctx_refs[0].shape[0], ctx_refs[0].shape[1] // 2
    for r in range(4):
        back = dot_nn(low, w_ref[r, :, 0:cols]).astype(bf16)
        ctx_refs[r][:, 0:cols] = back[:share]
        ctx_refs[r][:, cols:] = back[share:]


def first_pull(place, dz, part, got, unit, scale, params, weights):
    rows, width = dz.shape
    cols = weights.shape[-1] // 2
    f32, bf16 = jnp.float32, jnp.bfloat16
    return call_kernel(
        first_pull_kernel,
        place,
        (dz, part, got, unit, scale, params, weights),
        (
            shaped((rows, width), f32),
            shaped((rows, width), bf16),
            shaped((3, width), f32),
            *(shaped((rows // 2, 2 * cols), bf16),) * 4,
        ),
        flops=2 * rows * width * cols * 4,
        moved=20 * rows * width,
    )


def last_grads_kernel(place_ref, low_ref, c0, c1, c2, c3, a_ref, a_other_ref, d_ref, qv_ref, keep_ref, send_ref, full_ref):
    size, cols = full_ref.shape[0] // 4, full_ref.shape[1]
    half = a_ref.shape[0]
    low = jnp.transpose(low_ref[...])
    own, other = jnp.transpose(a_ref[...]), jnp.transpose(a_other_ref[...])
    spots = ((0, 0), (1, 0), (0, 1), (1, 1), (2, 0), (2, 1), (3, 0))
    for entry, (block, side) in enumerate(spots):
        if entry < 4:
            source = (c0, c1, c2, c3)[entry]
            context = jnp.concatenate([source[:, 0:cols], source[:, cols:]], axis=0)
            full_ref[...] = dot_nn(low, context)
        else:
            full_ref[...] = dot_nn(own, d_ref[entry - 4, 0:half, :]) + dot_nn(
                other, d_ref[entry - 4, half:, :]
            )
        for slot in range(2):
            for target, distance in ((keep_ref, 2 * slot), (send_ref, 2 * slot + 1)):
                start = pl.multiple_of((place_ref[0] ^ distance) * size, 64)
                target[slot, block * size : (block + 1) * size, side * cols : (side + 1) * cols] = (
                    full_ref[pl.ds(start, size), :].astype(jnp.bfloat16)
                )
    sums = jnp.concatenate([qv_ref[...], jnp.zeros((14, cols), jnp.float32)], axis=0)
    sums = jnp.concatenate([sums, jnp.zeros((16, cols), jnp.float32)], axis=1)
    nothing = jnp.zeros((size, cols), jnp.bfloat16)
    for slot in range(2):
        for target in (keep_ref, send_ref):
            target[slot, 3 * size : 4 * size, cols:] = nothing
            target[slot, 4 * size :, :] = sums.astype(jnp.bfloat16)


def last_grads(place, low, contexts, a_in, d_proj, d_bias_qv):
    rows, width = low.shape
    count = d_proj.shape[1]
    cols = d_proj.shape[-1]
    out = shaped((2, 4 * (width // 4) + 16, 2 * cols), jnp.bfloat16)
    return call_kernel(
        last_grads_kernel,
        place,
        (low, *contexts, *a_in, d_proj, d_bias_qv),
        (out, out),
        (pltpu.VMEM((width, cols), jnp.float32),),
        flops=2 * (4 * rows + 3 * count) * width * cols,
        moved=4 * count * width,
    )


def input_kernel(place_ref, first_ref, b0, b1, b2, own_ref, other_ref, clip_ref, mine_ref, other_out_ref):
    f32 = jnp.float32
    share = own_ref.shape[0]
    for part, (source, target) in enumerate(((own_ref, mine_ref), (other_ref, other_out_ref))):
        through = b0[0, part].astype(f32) + b1[0, part].astype(f32) + b2[part].astype(f32)
        inside = jnp.abs(source[...].astype(f32)) < clip_ref[...]
        first = first_ref[part * share : (part + 1) * share, :]
        target[...] = (first + jnp.where(inside, through, 0.0)).astype(target.dtype)


def input_rows(place, first, backs, own, other, clip_in):
    share, width = own.shape
    return call_kernel(
        input_kernel,
        place,
        (first, *backs, own, other, clip_in),
        (shaped((share, width), jnp.float32), shaped((share, width), jnp.bfloat16)),
        flops=10 * share * width,
        moved=20 * share * width,
    )


def vector_kernel(place_ref, third_ref, second_ref, first_ref, own_ref, far_ref, out_ref):
    half = own_ref.shape[1]
    out_ref[...] = jnp.zeros_like(out_ref)
    out_ref[0:3, :] = third_ref[...]
    out_ref[3:8, :] = second_ref[...]
    out_ref[8:11, :] = first_ref[...]
    for r in range(4):
        part = own_ref[r : r + 1, :] + far_ref[r : r + 1, :]
        nothing = jnp.zeros_like(part)
        left = jnp.where(place_ref[2] == 0, part, nothing)
        right = jnp.where(place_ref[2] == 0, nothing, part)
        out_ref[pl.ds(11 + (place_ref[1] ^ r), 1), :] = jnp.concatenate([left, right], axis=1)


def vector_rows(place, third, second, first, own, far):
    width = third.shape[1]
    return call_kernel(
        vector_kernel,
        place,
        (third, second, first, own, far),
        shaped((16, width), jnp.float32),
        flops=1,
        moved=1,
    )


def sign_of(value):
    return jnp.where(value > 0.0, 1.0, jnp.where(value < 0.0, -1.0, 0.0))


def piece_kernel(place_ref, *refs):
    sources, (piece_ref, teacher_ref), copies, sems = refs[:11], refs[11:13], refs[13:24], refs[24]
    moves = [
        pltpu.make_async_copy(source, target, sems.at[at])
        for at, (source, target) in enumerate(zip(sources, copies))
    ]
    for move in moves:
        move.start()
    for move in moves:
        move.wait()
    up_ref, down_ref, out_ref, t_out_ref, t_up_ref, t_down_ref, quant_ref, columns_ref, *rows = copies
    bf16, f32 = jnp.bfloat16, jnp.float32
    size, half = up_ref.shape[0], piece_ref.shape[1]
    lanes = pl.ds(pl.multiple_of(place_ref[2] * half, 128), half)
    quant = quant_ref[:, lanes]
    up = quant[1:2] * sign_of(up_ref[:, lanes] - quant[0:1])
    piece_ref[0:size, :] = up.astype(bf16)
    columns = columns_ref[...]
    down = columns[:, 3:4] * sign_of(down_ref[:, lanes] - columns[:, 2:3])
    piece_ref[size : 2 * size, :] = down.astype(bf16)
    out = columns[:, 1:2] * sign_of(out_ref[...] - columns[:, 0:1])
    piece_ref[2 * size : 3 * size, :] = jnp.concatenate([out.astype(bf16), t_out_ref[...]], axis=1)
    terms = []
    for row in rows:
        rest = row[:, lanes]
        for _ in range(3):
            term = rest.astype(bf16).astype(f32)
            terms.append(term)
            rest = rest - term
    terms = jnp.concatenate(terms + [jnp.zeros((7, half), f32)], axis=0)
    piece_ref[3 * size :, :] = terms.astype(bf16)
    teacher_ref[0:size, :] = t_up_ref[:, lanes]
    teacher_ref[size:, :] = t_down_ref[:, lanes]


def own_pieces(place, *sources):
    size, wide = sources[0].shape
    bf16 = jnp.bfloat16
    return call_kernel(
        piece_kernel,
        place,
        sources,
        (shaped((3 * size + 16, wide // 2), bf16), shaped((2 * size, wide // 2), bf16)),
        tuple(pltpu.VMEM(source.shape, source.dtype) for source in sources)
        + (pltpu.SemaphoreType.DMA((len(sources),)),),
        flops=1,
        moved=1,
        from_hbm=True,
    )


def finish_kernel(place_ref, vector_ref, got_ref, rows_ref, up_ref, stat_ref):
    total = vector_ref[...] + got_ref[...]
    ordered = jnp.concatenate([total[0:1], total[3:4], total[1:3], total[4:6]], axis=0)
    size = rows_ref.shape[1]
    part = ordered[:, 0:size]
    for index in range(1, 4):
        part = jnp.where(place_ref[0] == index, ordered[:, index * size : (index + 1) * size], part)
    rows_ref[...] = part
    up = total[11:12]
    for index in range(1, 4):
        up = jnp.where(place_ref[1] == index, total[11 + index : 12 + index], up)
    up_ref[...] = up
    sums = jnp.sum(total[6:11], axis=-1, keepdims=True)
    means = sums / sums[2:3]
    lane = lax.broadcasted_iota(jnp.int32, stat_ref.shape, 1)
    stat_ref[...] = jnp.where(
        lane == 0,
        jnp.sqrt(means[3:4]),
        jnp.where(lane == 1, jnp.sqrt(means[4:5]), jnp.where(lane == 2, jnp.sqrt(means[0:1]), means[1:2])),
    )


def finish_vectors(place, vector, got):
    width = vector.shape[1]
    f32 = jnp.float32
    return call_kernel(
        finish_kernel,
        place,
        (vector, got),
        (shaped((6, width // 4), f32), shaped((1, width), f32), shaped((1, 128), f32)),
        flops=1,
        moved=1,
    )


def swap_ctx(value):
    return lax.ppermute(value, "ctx", [(0, 1), (1, 0)])


def swap_core(value):
    return lax.ppermute(value, "fsdp", [(i, i ^ 1) for i in range(4)])


def swap_row(value):
    return lax.ppermute(value, "fsdp", [(i, i ^ 2) for i in range(4)])


def swap_tp(value, distance):
    return lax.ppermute(value, "tp", [(i, i ^ distance) for i in range(4)])


def fsdp_pieces(piece):
    far = swap_row(piece)
    return (piece, far, swap_core(piece), swap_core(far))


def exchange_tp(entries):
    return [entries[0]] + [swap_tp(entries[r], r) for r in (1, 2, 3)]


def three_terms(value):
    high = lax.reduce_precision(value, 8, 7)
    rest = value - high
    middle = lax.reduce_precision(rest, 8, 7)
    return [high.astype(jnp.bfloat16), middle.astype(jnp.bfloat16), (rest - middle).astype(jnp.bfloat16)]


def tie(values, *others):
    return lax.optimization_barrier((values, others))[0]


def once(place, *arrays):
    return (place, arrays)


def paired_body(
    tokens,
    cotangent,
    segment_ids,
    valid_mask,
    latent_qkv,
    latent_out,
    latent_up,
    latent_down,
    qkv_quant,
    up_quant,
    out_quant,
    down_quant,
    bias_qv,
    bias_up,
    row_params,
    clip_in,
    clip_ctx,
    clip_hidden,
    t_qkv,
    t_out,
    t_up,
    t_down,
    t_bias_qv,
    t_bias_up,
    t_rows,
):
    local_len, seq_count, width = tokens.shape
    share = cotangent.shape[0]
    col_width = latent_qkv.shape[2]
    hidden_width = latent_up.shape[1]
    half_hidden = hidden_width // 2
    row_width = latent_qkv.shape[0]
    tp_rank = lax.axis_index("tp")
    ctx_rank = lax.axis_index("ctx")
    fsdp_rank = lax.axis_index("fsdp")
    f32, bf16 = jnp.float32, jnp.bfloat16
    place = jnp.stack([fsdp_rank, tp_rank, ctx_rank]).astype(jnp.int32)

    def by_distance(value):
        pairs = value.reshape(2, 2, *value.shape[1:])
        pairs = jnp.where((tp_rank & 1) > 0, pairs[:, ::-1], pairs)
        pairs = jnp.where((tp_rank >> 1) > 0, pairs[::-1], pairs)
        return pairs.reshape(value.shape)

    def mine(value, axis):
        return lax.dynamic_index_in_dim(value, ctx_rank, axis, keepdims=False)

    def theirs(value, axis):
        return lax.dynamic_index_in_dim(value, 1 - ctx_rank, axis, keepdims=False)

    def half_of(weight):
        return jnp.where(ctx_rank == 0, weight[..., :half_hidden], weight[..., half_hidden:])

    def add(left, right):
        return left.astype(f32) + right.astype(f32)

    rows = 2 * share
    bin_up = binarize(latent_up, up_quant[0][None], up_quant[1][None])
    bin_down = binarize(latent_down, down_quant[0][:, None], down_quant[1][:, None])
    terms = [term for v in (bias_up, clip_hidden, t_bias_up) for term in three_terms(half_of(v))]
    vectors = jnp.pad(jnp.stack(terms), ((0, 16 - len(terms)), (0, 0)))
    bin_out = binarize(latent_out, out_quant[0][:, None], out_quant[1][:, None])
    piece = jnp.concatenate(
        [
            half_of(bin_up),
            half_of(bin_down),
            jnp.concatenate([bin_out, t_out], axis=1),
            vectors,
        ],
        axis=0,
    )
    piece_two = swap_tp(piece, 2)
    rows = 2 * share
    tokens_then, segment_then = tie((tokens, segment_ids), piece)
    relative = by_distance(tokens_then.reshape(4, share, seq_count, width))
    own = mine(relative, 2).reshape(local_len, width)
    code = by_distance(
        jnp.transpose(segment_then * 2 + (valid_mask > 0).astype(jnp.int32)).reshape(
            4, share, seq_count
        )
    )
    code_sent = jnp.pad(theirs(code, 2).reshape(1, local_len), ((0, 15), (0, width - local_len)))
    tokens_sent = jnp.concatenate(
        [theirs(relative, 2).reshape(local_len, width), code_sent.astype(bf16)], axis=0
    )
    other = swap_ctx(tokens_sent)
    latent_qkv_then, t_qkv = tie((latent_qkv, t_qkv), tokens_sent)
    bin_qkv = jnp.transpose(
        binarize(latent_qkv_then, qkv_quant[0][None], qkv_quant[1][None]), (1, 0, 2)
    )
    qkv_piece = jnp.concatenate([bin_qkv, jnp.transpose(t_qkv, (1, 0, 2))], axis=2)
    qkv_pieces = fsdp_pieces(qkv_piece)
    t_up, t_down = tie((t_up, t_down), qkv_piece)
    teacher_piece = jnp.concatenate([half_of(t_up), half_of(t_down)], axis=0)
    clip_in_row, clip_row = clip_in[None], clip_ctx[None]

    own_rows = own[:share]
    cot_own, cot_sent = mine(cotangent, 1), theirs(cotangent, 1)
    full_qkv, a_own, qkv_own, token = project_own(once(place, own_rows, cot_own, cot_sent), own, qkv_pieces, bias_qv, clip_in_row)
    other = tie(other, token)
    code_all = jnp.concatenate(
        [mine(code, 2).reshape(local_len), other[local_len, :local_len].astype(jnp.int32)]
    )
    code_col, code_row = code_all[:, None], code_all[None, :]
    valid = (
        jnp.concatenate([code_all[:share], code_all[local_len : local_len + share]]) & 1
    ).astype(f32)[:, None]
    even = jnp.stack([piece, tie(piece_two, token)])
    odd, even_row = swap_tp(even, 1), swap_row(even)
    *context, a_other, other_rows, qkv, merged, lse = attention_forward(
        True, once(place, even, token), other, full_qkv, qkv_own, bias_qv, clip_in_row,
        clip_row, code_col, code_row,
    )
    contexts = exchange_tp(context)
    odd, even_row = tie((odd, even_row), lse)
    even_cores = (swap_core(even), swap_core(even_row))
    odd_row = swap_row(odd)
    *teacher_context, token = attention_forward(
        False, once(place, lse, *even_cores), other, qkv_pieces, own,
        t_bias_qv, clip_in_row, clip_row, code_col, code_row,
    )
    token = gate(place, token, *contexts[1:])
    odd, odd_row, teacher_piece = tie((odd, odd_row, teacher_piece), token)
    teacher_two = swap_tp(teacher_piece, 2)
    pieces = (
        even, even_row, *even_cores,
        odd, odd_row, swap_core(odd), swap_core(odd_row),
    )
    out_full, unit, scale, h_low, first_sums, token = out_norm(
        True, once(place, token), contexts, pieces, own_rows, other_rows, valid, row_params,
        (cot_sent,),
    )
    h_far = swap_ctx(h_low)
    teacher_contexts = exchange_tp([teacher_context[0], *tie(teacher_context[1:], token)])
    hidden_full, terms, hid_own, slope_own, part_own, _ = hidden_layer(
        True, False, once(place, token), h_low, rows, pieces
    )
    teacher_even = jnp.stack([teacher_piece, tie(teacher_two, terms, *teacher_contexts[1:])])
    teacher_odd, teacher_even_row = swap_tp(teacher_even, 1), swap_row(teacher_even)
    h_teacher, ht_low, token = out_norm(
        False, once(place, part_own), teacher_contexts, out_full, own_rows, other_rows, valid, t_rows,
    )
    ht_far = swap_ctx(ht_low)
    hid_far, slope_far, part_far, token = hidden_layer(
        True, True, once(place, token), h_far, rows, hidden_full, terms
    )
    part_got = swap_ctx(part_far)
    teacher_odd = tie(teacher_odd, token)
    teacher_even_row = tie(teacher_even_row, token, ht_far)
    teacher_odd_row = swap_row(teacher_odd)
    teacher_hidden = (
        teacher_even, teacher_even_row, swap_core(teacher_even), swap_core(teacher_even_row),
        teacher_odd, teacher_odd_row, swap_core(teacher_odd), swap_core(teacher_odd_row),
    )
    teacher_full, t_part_far, _ = hidden_layer(
        False, True, once(place, token), ht_far, rows, teacher_hidden, terms
    )
    t_part_got = swap_ctx(t_part_far)
    t_part_own, _ = hidden_layer(
        False, False, once(place, t_part_far), ht_low, rows, teacher_full, terms
    )
    layer_own, layer_other, d_second, d_ffn, second_sums = loss_step(
        place, unit, part_own, part_got, h_teacher, t_part_own, t_part_got,
        cot_own, h_far, valid, row_params, t_rows,
    )

    def home(own_part, other_part):
        got = other_part.astype(own_part.dtype)
        first = jnp.where(ctx_rank == 0, own_part, got)
        second = jnp.where(ctx_rank == 0, got, own_part)
        return jnp.stack([first, second], axis=1)

    d_ffn_far = swap_ctx(d_ffn)
    du_own, d_part_own, du_sums_own = hidden_pull(False, place, d_ffn, hidden_full, slope_own)
    du_far, d_part_far, du_sums_far = hidden_pull(True, place, d_ffn_far, hidden_full, slope_far)
    d_part_got = swap_ctx(d_part_far)
    keep_down, send_down = hidden_grads(
        once(place, du_sums_far), (d_ffn, d_ffn_far), (hid_own, hid_far)
    )
    got_down = swap_core(send_down)
    leave_down = add(keep_down[1], got_down[1]).astype(bf16)
    d_first, d_attn, third_sums, *d_context = first_pull(
        once(place, send_down), d_second, d_part_own, d_part_got, unit, scale, row_params, out_full
    )
    d_contexts = exchange_tp(d_context)
    keep_up, send_up = hidden_grads(once(place, third_sums), (h_low, h_far), (du_own, du_far))
    got_up = swap_core(send_up)
    leave_up = add(keep_up[1], got_up[1]).astype(bf16)
    vector = vector_rows(place, third_sums, second_sums, first_sums, du_sums_own, du_sums_far)
    keep_back, send_back, d_proj, d_bias_qv = attention_backward(
        once(place, leave_down, leave_up, vector),
        qkv, clip_row, merged, lse, code_col, code_row, d_contexts, full_qkv,
    )
    got_back = swap_tp(send_back, 1)
    got_down_row = tie(swap_row(leave_down), d_bias_qv)
    got_up_row = tie(swap_row(leave_up), d_bias_qv)
    row_down = add(add(keep_down[0], got_down[0]), got_down_row)
    row_up = add(add(keep_up[0], got_up[0]), got_up_row)
    keep_last, send_last = last_grads(
        once(place, send_back, got_down_row),
        d_attn, contexts, (a_own, a_other), d_proj, d_bias_qv,
    )
    got_last, vector_got = swap_core(send_last), swap_core(tie(vector, send_last))
    got_back = tie(got_back, send_last)
    leave_back = add(keep_back[1], got_back[1]).astype(bf16)
    got_back_two = swap_tp(leave_back, 2)
    layer_out = home(layer_own, swap_ctx(tie(layer_other, leave_back)))
    vector = tie(vector + vector_got, leave_back)
    vector_got = swap_ctx(vector)
    send_both = tie(jnp.stack([row_down[1::2], row_up[1::2]]).astype(bf16), leave_back)
    got_both = swap_tp(send_both, 1)
    leave_last = tie(add(keep_last[1], got_last[1]).astype(bf16), leave_back)
    got_last_row = swap_row(leave_last)
    vector = tie(vector + vector_got, leave_last)
    vector_got = swap_row(vector)
    entry = row_width
    row_last = add(add(keep_last[0], got_last[0]), got_last_row)
    send_one = row_last[entry : 2 * entry].astype(bf16)
    got_one = swap_tp(send_one, 1)
    leave_both = tie(
        jnp.stack([add(row_down[2], got_both[0, 1]), add(row_up[2], got_both[1, 1])]).astype(bf16), send_one
    )
    got_both_two = swap_tp(leave_both, 2)
    vector = tie(vector + vector_got, leave_both)
    vector_got = swap_tp(vector, 1)
    input_own, input_other = input_rows(
        once(place, leave_both), d_first, (keep_back, got_back, got_back_two), own_rows, other_rows, clip_in_row
    )
    input_grad = home(input_own, swap_ctx(input_other))
    out_two = add(row_last[0:entry], got_one)
    leave_two = out_two[:, col_width:].astype(bf16)
    got_two = swap_tp(leave_two, 2)
    low_both = add(
        jnp.stack([add(row_down[0], got_both[0, 0]), add(row_up[0], got_both[1, 0])]), got_both_two
    ).astype(bf16)
    low_out = add(out_two[:, :col_width], got_two)
    low_last = jnp.concatenate(
        [
            row_last[2 * entry : 3 * entry],
            jnp.concatenate([row_last[3 * entry : 4 * entry, :col_width], low_out], axis=1),
            row_last[4 * entry :],
        ],
        axis=0,
    ).astype(bf16)
    sum_last = add(low_last, swap_ctx(low_last))
    vector = tie(vector + vector_got, low_both)
    grad_rows, grad_up_bias, statistics = finish_vectors(place, vector, swap_tp(vector, 2))

    both_far = swap_ctx(low_both)
    grad_both = jnp.concatenate(
        [
            jnp.where(ctx_rank == 0, low_both, both_far),
            jnp.where(ctx_rank == 0, both_far, low_both),
        ],
        axis=-1,
    ).astype(f32)
    grad_up = straight(grad_both[1], latent_up, up_quant[0][None], up_quant[1][None])
    grad_down = straight(
        grad_both[0], latent_down, down_quant[0][:, None], down_quant[1][:, None]
    )
    grad_qkv = straight(
        jnp.stack(
            [
                sum_last[:entry, :col_width],
                sum_last[:entry, col_width:],
                sum_last[entry : 2 * entry, :col_width],
            ],
            axis=1,
        ),
        latent_qkv,
        qkv_quant[0][None],
        qkv_quant[1][None],
    )
    grad_out = straight(sum_last[entry : 2 * entry, col_width:], latent_out, out_quant[0][:, None], out_quant[1][:, None])
    grad_qv = sum_last[2 * entry : 2 * entry + 2, :col_width]
    grad_bias_up, statistics = grad_up_bias[0], statistics[0, :4]
    return (
        layer_out,
        input_grad,
        grad_qkv,
        grad_out,
        grad_up,
        grad_down,
        grad_rows,
        grad_qv,
        grad_bias_up,
        statistics,
    )


def general_body(
    tokens,
    cotangent,
    segment_ids,
    valid_mask,
    latent_qkv,
    latent_out,
    latent_up,
    latent_down,
    qkv_quant,
    up_quant,
    out_quant,
    down_quant,
    bias_qv,
    bias_up,
    row_params,
    clip_in,
    clip_ctx,
    clip_hidden,
    t_qkv,
    t_out,
    t_up,
    t_down,
    t_bias_qv,
    t_bias_up,
    t_rows,
):
    local_len, seq_count, width = tokens.shape
    share = cotangent.shape[0]
    col_width = latent_qkv.shape[2]
    hidden_width = latent_up.shape[1]
    row_width = latent_qkv.shape[0]
    local_heads = col_width // HEAD_DIM
    scale = HEAD_DIM ** (-0.5)
    tp_rank = lax.axis_index("tp")
    ctx_rank = lax.axis_index("ctx")
    fsdp_rank = lax.axis_index("fsdp")
    full_len = local_len * lax.axis_size("ctx")
    bin_qkv = binarize(latent_qkv, qkv_quant[0][None], qkv_quant[1][None])
    bin_out = binarize(latent_out, out_quant[0][:, None], out_quant[1][:, None])
    bin_up = binarize(latent_up, up_quant[0][None], up_quant[1][None])
    bin_down = binarize(latent_down, down_quant[0][:, None], down_quant[1][:, None])
    gathered = (
        lax.all_gather(bin_qkv, "fsdp", axis=0, tiled=True),
        lax.all_gather(bin_out, "fsdp", axis=0, tiled=True),
        lax.all_gather(bin_up, "fsdp", axis=0, tiled=True),
        lax.all_gather(bin_down, "fsdp", axis=0, tiled=True),
        lax.all_gather(t_qkv, "fsdp", axis=0, tiled=True),
        lax.all_gather(t_out, "fsdp", axis=0, tiled=True),
        lax.all_gather(t_up, "fsdp", axis=0, tiled=True),
        lax.all_gather(t_down, "fsdp", axis=0, tiled=True),
    )
    full_qkv, full_out, full_up, full_down, teach_qkv, teach_out, teach_up, teach_down = gathered
    stream = tokens.astype(jnp.float32)
    a_in = jnp.clip(stream, -clip_in, clip_in).astype(jnp.bfloat16)
    proj_student = jnp.einsum("tsd,dkh->tskh", a_in, full_qkv, preferred_element_type=jnp.float32)
    proj_teacher = jnp.einsum(
        "tsd,dkh->tskh", tokens, teach_qkv, preferred_element_type=jnp.float32
    )
    student_q = (proj_student[:, :, 0] + bias_qv[0]).astype(jnp.bfloat16)
    student_k = proj_student[:, :, 1].astype(jnp.bfloat16)
    student_v = (proj_student[:, :, 2] + bias_qv[1]).astype(jnp.bfloat16)
    teacher_q = (proj_teacher[:, :, 0] + t_bias_qv[0]).astype(jnp.bfloat16)
    teacher_k = proj_teacher[:, :, 1].astype(jnp.bfloat16)
    teacher_v = (proj_teacher[:, :, 2] + t_bias_qv[1]).astype(jnp.bfloat16)
    student_queries = headed(student_q)
    teacher_queries = headed(teacher_q)
    query_pos = ctx_rank * local_len + jnp.arange(local_len, dtype=jnp.int32)
    key_tags = jnp.transpose(jnp.where(valid_mask > 0, segment_ids, -1))
    empty_state = (
        jnp.full((seq_count, local_heads, local_len), floor_score, jnp.float32),
        jnp.zeros((seq_count, local_heads, local_len), jnp.float32),
        jnp.zeros((seq_count, local_heads, local_len, HEAD_DIM), jnp.float32),
    )
    buffers = (
        jnp.zeros((full_len, seq_count, col_width), jnp.bfloat16),
        jnp.zeros((full_len, seq_count, col_width), jnp.bfloat16),
        jnp.zeros((full_len, seq_count), jnp.int32),
    )
    carry = (empty_state, empty_state, buffers)
    pieces = (
        lax.all_gather(student_k, "ctx", axis=0, tiled=True),
        lax.all_gather(student_v, "ctx", axis=0, tiled=True),
        lax.all_gather(teacher_k, "ctx", axis=0, tiled=True),
        lax.all_gather(teacher_v, "ctx", axis=0, tiled=True),
        lax.all_gather(key_tags, "ctx", axis=0, tiled=True),
    )
    start = jnp.int32(0)
    count = pieces[0].shape[0]
    block = key_block(count)

    def inner(states, index):
        offset = index * block
        parts = [lax.dynamic_slice_in_dim(piece, offset, block, 0) for piece in pieces]
        key_pos = offset + jnp.arange(block, dtype=jnp.int32)
        allowed = allowed_pairs(segment_ids, query_pos, parts[4], key_pos)
        states = (
            online_step(
                states[0], student_queries, headed(parts[0]), headed(parts[1]), allowed, scale
            ),
            online_step(
                states[1], teacher_queries, headed(parts[2]), headed(parts[3]), allowed, scale
            ),
        )
        return (states, None)

    states, _ = lax.scan(inner, (carry[0], carry[1]), jnp.arange(count // block, dtype=jnp.int32))
    kept = tuple(
        (
            lax.dynamic_update_slice_in_dim(buffer, piece, start, 0)
            for buffer, piece in zip(carry[2], (pieces[0], pieces[1], pieces[4]))
        )
    )
    student_state, teacher_state, kept = (states[0], states[1], kept)
    attended, log_total = finish(student_state)
    teacher_attended, _ = finish(teacher_state)
    attended_flat = attended.reshape(local_len, seq_count, col_width)
    ctx_ratio = jnp.tanh(attended_flat / clip_ctx)
    context = (clip_ctx * ctx_ratio).astype(jnp.bfloat16)
    teacher_context = teacher_attended.reshape(local_len, seq_count, col_width).astype(jnp.bfloat16)
    rows_student = context
    rows_teacher = teacher_context
    attn_both = lax.psum_scatter(
        jnp.concatenate(
            [
                jnp.einsum(
                    "tsh,dh->tsd", rows_student, full_out, preferred_element_type=jnp.float32
                ),
                jnp.einsum(
                    "tsh,dh->tsd", rows_teacher, teach_out, preferred_element_type=jnp.float32
                ),
            ],
            axis=-1,
        ).astype(jnp.bfloat16),
        "tp",
        scatter_dimension=0,
        tiled=True,
    ).astype(jnp.float32)
    attn_student = attn_both[..., :width] + row_params[0]
    attn_teacher = attn_both[..., width:] + t_rows[0]
    stream_rows = lax.dynamic_slice_in_dim(stream, tp_rank * share, share, 0)
    first_sum = stream_rows + attn_student
    h_one = layer_norm(first_sum, row_params[2], row_params[3])
    h_teacher = layer_norm(stream_rows + attn_teacher, t_rows[2], t_rows[3])
    h_full, h_teacher_full = (
        lax.all_gather(h_one.astype(jnp.bfloat16), "tp", axis=0, tiled=True),
        lax.all_gather(h_teacher.astype(jnp.bfloat16), "tp", axis=0, tiled=True),
    )
    upper = jnp.einsum("tsd,df->tsf", h_full, full_up, preferred_element_type=jnp.float32) + bias_up
    activated = exact_gelu(upper)
    hid_ratio = jnp.tanh(activated / clip_hidden)
    hidden = (clip_hidden * hid_ratio).astype(jnp.bfloat16)
    upper_teacher = (
        jnp.einsum("tsd,df->tsf", h_teacher_full, teach_up, preferred_element_type=jnp.float32)
        + t_bias_up
    )
    hidden_teacher = exact_gelu(upper_teacher).astype(jnp.bfloat16)
    rows_student = hidden
    rows_teacher = hidden_teacher
    ffn_both = lax.psum_scatter(
        jnp.concatenate(
            [
                jnp.einsum(
                    "tsf,df->tsd", rows_student, full_down, preferred_element_type=jnp.float32
                ),
                jnp.einsum(
                    "tsf,df->tsd", rows_teacher, teach_down, preferred_element_type=jnp.float32
                ),
            ],
            axis=-1,
        ).astype(jnp.bfloat16),
        "tp",
        scatter_dimension=0,
        tiled=True,
    ).astype(jnp.float32)
    ffn_student = ffn_both[..., :width] + row_params[1]
    ffn_teacher = ffn_both[..., width:] + t_rows[1]
    second_sum = h_one + ffn_student
    out = layer_norm(second_sum, row_params[4], row_params[5])
    teacher_out = layer_norm(h_teacher + ffn_teacher, t_rows[4], t_rows[5])
    layer_out = out.astype(jnp.bfloat16)
    valid_rows = jnp.transpose(
        lax.dynamic_slice_in_dim(valid_mask, tp_rank * share, share, 1)
    ).astype(jnp.float32)[..., None]
    difference = out - teacher_out
    grad_out_total = cotangent.astype(jnp.float32) + valid_rows * difference
    stat_terms = jnp.stack(
        [
            jnp.sum(valid_rows) + 0.0 * jnp.sum(stream_rows[:1, :1, :1]),
            jnp.sum(valid_rows * stream_rows * stream_rows),
            jnp.sum(valid_rows * attn_student * attn_student),
            jnp.sum(valid_rows * ffn_student * ffn_student),
            jnp.sum(valid_rows * difference * difference),
        ]
    )
    _, second_pull = jax.vjp(layer_norm, second_sum, row_params[4], row_params[5])
    d_second, d_gain_two, d_bias_two = second_pull(grad_out_total)
    d_ffn = d_second.astype(jnp.bfloat16)
    d_bias_down = jnp.sum(d_ffn.astype(jnp.float32), axis=(0, 1))
    d_ffn_full = lax.all_gather(d_ffn, "tp", axis=0, tiled=True)
    grad_bin_down = jnp.einsum(
        "tsd,tsf->df", d_ffn_full, hidden, preferred_element_type=jnp.float32
    )
    d_hidden = jnp.einsum("tsd,df->tsf", d_ffn_full, full_down, preferred_element_type=jnp.float32)
    d_hidden = d_hidden * (1.0 - hid_ratio * hid_ratio)
    _, gelu_pull = jax.vjp(exact_gelu, upper)
    d_upper = gelu_pull(d_hidden)[0].astype(jnp.bfloat16)
    d_bias_up = jnp.sum(d_upper.astype(jnp.float32), axis=(0, 1))
    grad_bin_up = jnp.einsum("tsd,tsf->df", h_full, d_upper, preferred_element_type=jnp.float32)
    rows = d_upper
    d_h_one = d_second + lax.psum_scatter(
        jnp.einsum("tsf,df->tsd", rows, full_up, preferred_element_type=jnp.float32).astype(
            jnp.bfloat16
        ),
        "tp",
        scatter_dimension=0,
        tiled=True,
    ).astype(jnp.float32)
    _, first_pull = jax.vjp(layer_norm, first_sum, row_params[2], row_params[3])
    d_first, d_gain_one, d_bias_one = first_pull(d_h_one)
    d_attn = d_first.astype(jnp.bfloat16)
    d_bias_out = jnp.sum(d_attn.astype(jnp.float32), axis=(0, 1))
    d_attn_full = lax.all_gather(d_attn, "tp", axis=0, tiled=True)
    grad_bin_out = jnp.einsum(
        "tsd,tsh->dh", d_attn_full, context, preferred_element_type=jnp.float32
    )
    d_context = jnp.einsum("tsd,dh->tsh", d_attn_full, full_out, preferred_element_type=jnp.float32)
    d_attended = (d_context * (1.0 - ctx_ratio * ctx_ratio)).astype(jnp.bfloat16)
    d_attended_heads = headed(d_attended)
    delta = jnp.transpose(
        jnp.sum(d_attended_heads.astype(jnp.float32) * attended, axis=-1), (1, 2, 0)
    )
    key_all, value_all, tag_all = kept
    back_block = key_block(full_len)

    def back_step(grad_q, index):
        offset = index * back_block
        keys = headed(lax.dynamic_slice_in_dim(key_all, offset, back_block, 0))
        values = headed(lax.dynamic_slice_in_dim(value_all, offset, back_block, 0))
        block_tags = lax.dynamic_slice_in_dim(tag_all, offset, back_block, 0)
        key_pos = offset + jnp.arange(back_block, dtype=jnp.int32)
        allowed = allowed_pairs(segment_ids, query_pos, block_tags, key_pos)
        current = grad_q
        scores = (
            jnp.einsum("tshe,kshe->shtk", student_queries, keys, preferred_element_type=jnp.float32)
            * scale
        )
        probs = jnp.where(allowed, jnp.exp(scores - log_total[..., None]), 0.0)
        d_probs = jnp.einsum(
            "tshe,kshe->shtk", d_attended_heads, values, preferred_element_type=jnp.float32
        )
        d_scores = (probs * (d_probs - delta[..., None])).astype(jnp.bfloat16)
        current = (
            current
            + jnp.einsum("shtk,kshe->shte", d_scores, keys, preferred_element_type=jnp.float32)
            * scale
        )
        grad_k = (
            jnp.einsum(
                "shtk,tshe->kshe", d_scores, student_queries, preferred_element_type=jnp.float32
            )
            * scale
        )
        grad_v = jnp.einsum(
            "shtk,tshe->kshe",
            probs.astype(jnp.bfloat16),
            d_attended_heads,
            preferred_element_type=jnp.float32,
        )
        joined = jnp.concatenate(
            [
                grad_k.reshape(back_block, seq_count, col_width),
                grad_v.reshape(back_block, seq_count, col_width),
            ],
            axis=-1,
        )
        return (current, joined)

    grad_q, key_terms = lax.scan(
        back_step,
        jnp.zeros((seq_count, local_heads, local_len, HEAD_DIM), jnp.float32),
        jnp.arange(full_len // back_block, dtype=jnp.int32),
    )
    key_terms = key_terms.reshape(full_len, seq_count, 2 * col_width)
    key_sums = lax.psum_scatter(
        key_terms.astype(jnp.bfloat16), "ctx", scatter_dimension=0, tiled=True
    ).astype(jnp.float32)
    grad_q_flat = jnp.transpose(grad_q, (2, 0, 1, 3)).reshape(local_len, seq_count, col_width)
    d_proj = jnp.stack(
        [grad_q_flat, key_sums[..., :col_width], key_sums[..., col_width:]], axis=2
    ).astype(jnp.bfloat16)
    d_bias_qv = jnp.stack(
        [
            jnp.sum(d_proj[:, :, 0].astype(jnp.float32), axis=(0, 1)),
            jnp.sum(d_proj[:, :, 2].astype(jnp.float32), axis=(0, 1)),
        ]
    )
    grad_bin_qkv = jnp.einsum("tsd,tskh->dkh", a_in, d_proj, preferred_element_type=jnp.float32)
    rows = d_proj
    through = lax.psum_scatter(
        jnp.einsum("tskh,dkh->tsd", rows, full_qkv, preferred_element_type=jnp.float32).astype(
            jnp.bfloat16
        ),
        "tp",
        scatter_dimension=0,
        tiled=True,
    ).astype(jnp.float32)
    input_grad = d_first + through * (jnp.abs(stream_rows) < clip_in).astype(jnp.float32)
    shards = (
        lax.psum_scatter(
            grad_bin_qkv.astype(jnp.bfloat16), "fsdp", scatter_dimension=0, tiled=True
        ).astype(jnp.float32),
        lax.psum_scatter(
            grad_bin_out.astype(jnp.bfloat16), "fsdp", scatter_dimension=0, tiled=True
        ).astype(jnp.float32),
        lax.psum_scatter(
            grad_bin_up.astype(jnp.bfloat16), "fsdp", scatter_dimension=0, tiled=True
        ).astype(jnp.float32),
        lax.psum_scatter(
            grad_bin_down.astype(jnp.bfloat16), "fsdp", scatter_dimension=0, tiled=True
        ).astype(jnp.float32),
    )
    summed = (
        lax.psum(shards[0].astype(jnp.bfloat16), "ctx").astype(jnp.float32),
        lax.psum(shards[1].astype(jnp.bfloat16), "ctx").astype(jnp.float32),
        lax.psum(shards[2].astype(jnp.bfloat16), "ctx").astype(jnp.float32),
        lax.psum(shards[3].astype(jnp.bfloat16), "ctx").astype(jnp.float32),
    )
    grad_qkv = straight(summed[0], latent_qkv, qkv_quant[0][None], qkv_quant[1][None])
    grad_out = straight(summed[1], latent_out, out_quant[0][:, None], out_quant[1][:, None])
    grad_up = straight(summed[2], latent_up, up_quant[0][None], up_quant[1][None])
    grad_down = straight(summed[3], latent_down, down_quant[0][:, None], down_quant[1][:, None])
    vector_grads = jnp.stack(
        [d_bias_out, d_bias_down, d_gain_one, d_bias_one, d_gain_two, d_bias_two]
    )
    placed_qv = lax.dynamic_update_slice_in_dim(
        jnp.zeros((2, width), jnp.float32), d_bias_qv, tp_rank * col_width, 1
    )
    placed_up = lax.dynamic_update_slice_in_dim(
        jnp.zeros((hidden_width * lax.axis_size("tp"),), jnp.float32),
        d_bias_up,
        tp_rank * hidden_width,
        0,
    )
    stat_sums, vector_sums, qv_sums, up_sums = lax.psum(
        (stat_terms, vector_grads, placed_qv, placed_up), ("fsdp", "ctx", "tp")
    )
    grad_rows = lax.dynamic_slice_in_dim(vector_sums, fsdp_rank * row_width, row_width, 1)
    grad_qv = lax.dynamic_slice_in_dim(qv_sums, tp_rank * col_width, col_width, 1)
    grad_bias_up = lax.dynamic_slice_in_dim(up_sums, tp_rank * hidden_width, hidden_width, 0)
    denom = stat_sums[0] * width
    statistics = jnp.stack(
        [
            jnp.sqrt(stat_sums[1] / denom),
            jnp.sqrt(stat_sums[2] / denom),
            jnp.sqrt(stat_sums[3] / denom),
            stat_sums[4] / denom,
        ]
    )
    return (
        layer_out,
        input_grad,
        grad_qkv,
        grad_out,
        grad_up,
        grad_down,
        grad_rows,
        grad_qv,
        grad_bias_up,
        statistics,
    )


def pick_body(mesh):
    sizes = dict(mesh.shape)
    if sizes["fsdp"] == 4 and sizes["tp"] == 4 and sizes["ctx"] == 2:
        return paired_body
    return general_body


def solution(mesh):
    return jax.shard_map(
        pick_body(mesh),
        mesh=mesh,
        in_specs=(
            P("ctx", "fsdp", None),
            P(("ctx", "tp"), "fsdp", None),
            P("fsdp", "ctx"),
            P("fsdp", "ctx"),
            P("fsdp", None, "tp"),
            P("fsdp", "tp"),
            P("fsdp", "tp"),
            P("fsdp", "tp"),
            P(None, None, "tp"),
            P(None, "tp"),
            P(None, "fsdp"),
            P(None, "fsdp"),
            P(None, "tp"),
            P("tp"),
            P(),
            P(),
            P("tp"),
            P("tp"),
            P("fsdp", None, "tp"),
            P("fsdp", "tp"),
            P("fsdp", "tp"),
            P("fsdp", "tp"),
            P(None, "tp"),
            P("tp"),
            P(),
        ),
        out_specs=(
            P(("ctx", "tp"), "fsdp", None),
            P(("ctx", "tp"), "fsdp", None),
            P("fsdp", None, "tp"),
            P("fsdp", "tp"),
            P("fsdp", "tp"),
            P("fsdp", "tp"),
            P(None, "fsdp"),
            P(None, "tp"),
            P("tp"),
            P(),
        ),
        check_vma=False,
    )
```

```python
import functools
import math

import jax
import jax.numpy as jnp
from jax import lax
from jax.experimental import pallas as pl
from jax.experimental.pallas import tpu as pltpu
from jax.sharding import PartitionSpec as P

HEAD_DIM = 64


epsilon = 1e-05
floor_score = -1e30


def binarize(latent, shift, scales):
    return (scales * jnp.sign(latent - shift)).astype(jnp.bfloat16)


def straight(summed, latent, shift, scales):
    inside = (jnp.abs(latent - shift) < 1.0).astype(jnp.float32)
    return summed * scales * inside


def layer_norm(stream, gains, biases):
    centred = stream - jnp.mean(stream, axis=-1, keepdims=True)
    spread = jnp.mean(centred * centred, axis=-1, keepdims=True)
    return centred * lax.rsqrt(spread + epsilon) * gains + biases


def exact_gelu(values):
    return jax.nn.gelu(values, approximate=False)


def key_block(count):
    return math.gcd(count, 512)


def headed(array):
    return array.reshape(array.shape[0], array.shape[1], array.shape[2] // HEAD_DIM, HEAD_DIM)


def allowed_pairs(query_seg, query_pos, key_tags, key_pos):
    same = query_seg[:, :, None] == jnp.transpose(key_tags)[:, None, :]
    diagonal = query_pos[:, None] == key_pos[None, :]
    return (same | diagonal[None])[:, None]


def online_step(state, queries, keys, values, allowed, scale):
    running, total, accum = state
    scores = (
        jnp.einsum("tshe,kshe->shtk", queries, keys, preferred_element_type=jnp.float32) * scale
    )
    scores = jnp.where(allowed, scores, floor_score)
    newest = jnp.maximum(running, jnp.max(scores, axis=-1))
    weights = jnp.where(allowed, jnp.exp(scores - newest[..., None]), 0.0)
    factor = jnp.exp(running - newest)
    total = total * factor + jnp.sum(weights, axis=-1)
    accum = accum * factor[..., None] + jnp.einsum(
        "shtk,kshe->shte", weights.astype(jnp.bfloat16), values, preferred_element_type=jnp.float32
    )
    return (newest, total, accum)


def finish(state):
    running, total, accum = state
    merged = accum / total[..., None]
    return (jnp.transpose(merged, (2, 0, 1, 3)), running + jnp.log(total))


WORK_FACTOR = 4
TOKEN = (8, 128)
ROOM = 8 * 2**20


def vmem_specs(count):
    return [pl.BlockSpec(memory_space=pltpu.VMEM)] * count


def vmem_room(inputs, outs, scratch):
    total = 0
    for array in (*inputs, *jax.tree.leaves(outs), *scratch):
        if not jnp.issubdtype(array.dtype, jnp.number):
            continue
        *lead, rows, lanes = (1, 1, *array.shape)
        size = jnp.dtype(array.dtype).itemsize
        tile = 8 * (4 // size)
        total += math.prod(lead) * size * (-(-rows // tile) * tile) * (-(-lanes // 128) * 128)
    return min(total + ROOM, 60 * 2**20)


def call_kernel(kernel, place, inputs, outs, scratch=(), flops=0, moved=0, exps=0, from_hbm=False):
    place, after = place if isinstance(place, tuple) else (place, ())

    def body(place_ref, *refs):
        kernel(place_ref, *refs[len(after) :])

    return pl.pallas_call(
        body,
        out_shape=outs,
        in_specs=[pl.BlockSpec(memory_space=pltpu.SMEM)]
        + [pl.BlockSpec(memory_space=pl.ANY)] * len(after)
        + ([pl.BlockSpec(memory_space=pltpu.HBM)] * len(inputs) if from_hbm else vmem_specs(len(inputs))),
        out_specs=jax.tree.map(lambda _: pl.BlockSpec(memory_space=pltpu.VMEM), outs),
        scratch_shapes=list(scratch),
        compiler_params=pltpu.CompilerParams(vmem_limit_bytes=vmem_room(inputs, outs, scratch)),
        cost_estimate=pl.CostEstimate(
            flops=WORK_FACTOR * flops, bytes_accessed=moved, transcendentals=exps
        ),
    )(place, *after, *inputs)


def shaped(shape, dtype):
    return jax.ShapeDtypeStruct(shape, dtype)


def gate_kernel(place_ref, token_ref):
    token_ref[...] = jnp.zeros_like(token_ref)


def gate(place, *arrays):
    return call_kernel(gate_kernel, (place, arrays), (), shaped(TOKEN, jnp.float32), flops=1, moved=1)


NT = (((1,), (1,)), ((), ()))


def dot_nt(left, right):
    return lax.dot_general(left, right, NT, preferred_element_type=jnp.float32)


def dot_nn(left, right):
    return jnp.dot(left, right, preferred_element_type=jnp.float32)


QUERY_BLOCK = 256


def place_projections(place_ref, pieces, target, first):
    size, cols = pieces[0].shape[1], target.shape[2]
    for kind in range(3):
        for distance, piece in zip((0, 2, 1, 3), pieces):
            start = pl.multiple_of((place_ref[0] ^ distance) * size, 64)
            target[kind, pl.ds(start, size), :] = piece[kind, :, first : first + cols]


def project_kernel(place_ref, own_ref, w0, w2, w1, w3, bias_ref, clip_in_ref, full_ref, a_ref, q_ref, token_ref):
    place_projections(place_ref, (w0, w2, w1, w3), full_ref, 0)
    clipped = jnp.clip(own_ref[...].astype(jnp.float32), -clip_in_ref[...], clip_in_ref[...])
    clipped = clipped.astype(jnp.bfloat16)
    a_ref[...] = clipped
    write_heads(clipped, full_ref, bias_ref, q_ref, 0)
    token_ref[...] = jnp.zeros_like(token_ref)


def write_heads(inputs, w_ref, bias_ref, target, base):
    rows = inputs.shape[0]
    for kind in range(3):
        values = dot_nn(inputs, w_ref[kind])
        if kind != 1:
            values = values + bias_ref[kind >> 1 : (kind >> 1) + 1, :]
        values = values.astype(jnp.bfloat16)
        if kind == 0:
            values = values * (HEAD_DIM**-0.5)
        for head in range(target.shape[1]):
            target[kind, head, base : base + rows, :] = values[:, head * HEAD_DIM : (head + 1) * HEAD_DIM]


def project_own(place, own, pieces, bias, clip_in):
    half, width = own.shape
    cols = pieces[0].shape[-1] // 2
    heads = cols // HEAD_DIM
    bf16 = jnp.bfloat16
    return call_kernel(
        project_kernel,
        place,
        (own, *pieces, bias, clip_in),
        (
            shaped((3, width, cols), bf16),
            shaped((half, width), bf16),
            shaped((3, heads, half, HEAD_DIM), bf16),
            shaped(TOKEN, jnp.float32),
        ),
        flops=1,
        moved=1,
    )


def unit_matrix():
    shape = (HEAD_DIM, HEAD_DIM)
    ones = lax.broadcasted_iota(jnp.int32, shape, 0) == lax.broadcasted_iota(jnp.int32, shape, 1)
    return ones.astype(jnp.bfloat16)


def block_window(row_ref, place_ref, blocks):
    mask = order_mask(place_ref)
    low, high = [], []
    for block in range(blocks):
        segment = row_ref[:, block * QUERY_BLOCK : (block + 1) * QUERY_BLOCK] >> 1
        low.append(jnp.min(segment))
        high.append(jnp.max(segment))
    windows = []
    for query in range(blocks):
        first, last = jnp.int32(blocks - 1), jnp.int32(0)
        for key in range(blocks):
            meets = (low[key] <= high[query]) & (high[key] >= low[query])
            at = key ^ mask
            first = jnp.where(meets, jnp.minimum(first, at), first)
            last = jnp.where(meets, jnp.maximum(last, at), last)
        windows.append((first, last - first + 1))
    return windows


def order_mask(place_ref):
    return 2 * place_ref[2] + (place_ref[1] >> 1)


def pick(values, index):
    chosen = values[0]
    for at in range(1, len(values)):
        chosen = jnp.where(index == at, values[at], chosen)
    return chosen


def pair_bias(col_ref, row_ref, query, key):
    size = QUERY_BLOCK
    code_col = col_ref[pl.ds(pl.multiple_of(key * size, size), size), :]
    code_row = row_ref[:, pl.ds(pl.multiple_of(query * size, size), size)]
    tags = jnp.where((code_col & 1) > 0, code_col >> 1, -1)
    apart = lax.broadcasted_iota(jnp.int32, (size, size), 0) - lax.broadcasted_iota(
        jnp.int32, (size, size), 1
    )
    allowed = (tags == (code_row >> 1)) | (apart == (query - key) * size)
    return jnp.where(allowed, 0.0, floor_score)


def each_count(windows, query, blocks, body):
    first = pick([w[0] for w in windows], query)
    count = pick([w[1] for w in windows], query)
    for fixed in range(1, blocks + 1):

        @pl.when(count == fixed)
        def _():
            body(first, fixed)


def attention_kernel(
    student, place_ref, other_ref, bias_ref, clip_in_ref, clip_ref, col_ref, row_ref, *refs
):
    if student:
        w_ref, part_ref, *c_refs = refs[:6]
        a_ref, rows_ref, qkv_ref, merged_ref, lse_ref, vt_ref, bias_at, score_ref, sum_ref = refs[6:]
    else:
        pieces, own_ref, c_refs, token_ref = refs[:4], refs[4], refs[5:9], refs[9]
        w_ref, qkv_ref, vt_ref, bias_at, score_ref, sum_ref = refs[10:]
        token_ref[...] = jnp.zeros_like(token_ref)
    half = qkv_ref.shape[2] // 2
    heads = qkv_ref.shape[1]
    cols = heads * HEAD_DIM
    size = QUERY_BLOCK
    blocks = 2 * half // size
    bf16, f32 = jnp.bfloat16, jnp.float32
    inputs = other_ref[0:half, :]
    if student:
        qkv_ref[:, :, 0:half, :] = part_ref[...]
        inputs = jnp.clip(inputs.astype(f32), -clip_in_ref[...], clip_in_ref[...]).astype(bf16)
        a_ref[...] = inputs
        rows_ref[...] = other_ref[0 : half // 4, :]
    else:
        place_projections(place_ref, pieces, w_ref, w_ref.shape[2])
        write_heads(own_ref[...], w_ref, bias_ref, qkv_ref, 0)
    write_heads(inputs, w_ref, bias_ref, qkv_ref, half)
    eye = unit_matrix()
    for head in range(heads):
        vt_ref[head] = dot_nt(eye, qkv_ref[2, head]).astype(bf16)
    windows = block_window(row_ref, place_ref, blocks)
    mask = order_mask(place_ref)
    sum_ref[...] = jnp.zeros_like(sum_ref)

    def one_query(query, carry):
        at = pl.multiple_of(query * size, size)

        def body(first, count):
            keys = [(first + step) ^ mask for step in range(count)]
            starts = [pl.multiple_of(key * size, size) for key in keys]
            for step in range(count):
                bias_at[step] = pair_bias(col_ref, row_ref, query, keys[step])
            for head in range(heads):
                queries = qkv_ref[0, head, pl.ds(at, size), :]
                top = None
                for step in range(count):
                    scores = bias_at[step] + dot_nt(
                        qkv_ref[1, head, pl.ds(starts[step], size), :], queries
                    )
                    score_ref[step] = scores
                    part = jnp.max(scores, axis=0, keepdims=True)
                    top = part if top is None else jnp.maximum(top, part)
                total, merged = 0.0, 0.0
                for step in range(count):
                    weights = jnp.exp(score_ref[step] - top)
                    total = total + jnp.sum(weights, axis=0, keepdims=True)
                    merged = merged + dot_nn(
                        vt_ref[head, :, pl.ds(starts[step], size)], weights.astype(bf16)
                    )
                sum_ref[head * HEAD_DIM : (head + 1) * HEAD_DIM, :] = merged * (1.0 / total)
                if student:
                    lse_ref[head : head + 1, pl.ds(at, size)] = top + jnp.log(total)

        each_count(windows, query, blocks, body)
        if student:
            merged_ref[:, pl.ds(at, size)] = sum_ref[0:cols, :]
        merged = jnp.transpose(sum_ref[...])[:, :cols]
        if student:
            merged = clip_ref[...] * jnp.tanh(merged / clip_ref[...])
        merged = merged.astype(bf16)
        share = size // 2
        for at in range(blocks):

            @pl.when(query == at)
            def _():
                lanes = slice((at >> 1) * cols, ((at >> 1) + 1) * cols)
                c_refs[2 * (at & 1)][:, lanes] = merged[:share]
                c_refs[2 * (at & 1) + 1][:, lanes] = merged[share:]

        return carry

    lax.fori_loop(0, blocks, one_query, 0)


def attention_forward(student, place, other, weights, parts, bias, clip_in, clip, code_col, code_row):
    width = other.shape[1]
    half = parts.shape[2] if student else parts.shape[0]
    cols = clip.shape[-1]
    heads = cols // HEAD_DIM
    count = 2 * half
    bf16, f32 = jnp.bfloat16, jnp.float32
    qkv = (3, heads, count, HEAD_DIM)
    c_shape = (shaped((half // 4, 2 * cols), bf16),) * 4
    scratch = (
        pltpu.VMEM((heads, HEAD_DIM, count), bf16),
        pltpu.VMEM((count // QUERY_BLOCK, QUERY_BLOCK, QUERY_BLOCK), f32),
        pltpu.VMEM((count // QUERY_BLOCK, QUERY_BLOCK, QUERY_BLOCK), f32),
        pltpu.VMEM((256, QUERY_BLOCK), f32),
    )
    if student:
        outs = (
            *c_shape,
            shaped((half, width), bf16),
            shaped((half // 4, width), bf16),
            shaped(qkv, bf16),
            shaped((cols, count), f32),
            shaped((8, count), f32),
        )
        inputs = (weights, parts)
    else:
        outs = (*c_shape, shaped(TOKEN, f32))
        scratch = (pltpu.VMEM((3, width, cols), bf16), pltpu.VMEM(qkv, bf16), *scratch)
        inputs = (*weights, parts)
    return call_kernel(
        functools.partial(attention_kernel, student),
        place,
        (other, bias, clip_in, clip, code_col, code_row, *inputs),
        outs,
        scratch,
        flops=2 * half * width * cols * 3 + 4 * count * count * cols,
        moved=6 * count * width,
        exps=heads * count * count,
    )


def attention_pull_kernel(
    place_ref,
    qkv_ref,
    clip_ref,
    merged_ref,
    lse_ref,
    col_ref,
    row_ref,
    d0_ref,
    d1_ref,
    d2_ref,
    d3_ref,
    w_ref,
    keep_ref,
    send_ref,
    dproj_ref,
    sums_ref,
    grad_ref,
    kt_ref,
    dk_ref,
    dv_ref,
    sum_ref,
    delta_ref,
    bias_at,
):
    _, heads, count, _ = qkv_ref.shape
    cols = heads * HEAD_DIM
    size = QUERY_BLOCK
    share = size // 2
    blocks = count // size
    bf16, f32 = jnp.bfloat16, jnp.float32
    eye = unit_matrix()
    for head in range(heads):
        kt_ref[head] = dot_nt(eye, qkv_ref[1, head]).astype(bf16)
    for distance, source in enumerate((d0_ref, d1_ref, d2_ref, d3_ref)):
        for part in range(2):
            at = part * (count // 2) + distance * share
            merged = merged_ref[:, at : at + share]
            wide = jnp.concatenate([merged, jnp.zeros((256 - cols, share), f32)], axis=0)
            ratio = jnp.tanh(jnp.transpose(wide)[:, :cols] / clip_ref[...])
            grad = (source[:, part * cols : (part + 1) * cols].astype(f32) * (1.0 - ratio * ratio)).astype(bf16)
            for head in range(heads):
                grad_ref[head, at : at + share, :] = grad[:, head * HEAD_DIM : (head + 1) * HEAD_DIM]
            wide = jnp.concatenate(
                [grad.astype(f32), jnp.zeros((share, 256 - cols), f32)], axis=1
            )
            turned = jnp.transpose(wide)[:cols] * merged
            for head in range(heads):
                delta_ref[head : head + 1, at : at + share] = jnp.sum(
                    turned[head * HEAD_DIM : (head + 1) * HEAD_DIM], axis=0, keepdims=True
                )
    dk_ref[...] = jnp.zeros_like(dk_ref)
    dv_ref[...] = jnp.zeros_like(dv_ref)
    windows = block_window(row_ref, place_ref, blocks)
    mask = order_mask(place_ref)
    sum_ref[...] = jnp.zeros_like(sum_ref)

    def one_query(query, carry):
        at = pl.multiple_of(query * size, size)

        def body(first, count):
            keys = [(first + step) ^ mask for step in range(count)]
            starts = [pl.multiple_of(key * size, size) for key in keys]
            for step in range(count):
                bias_at[step] = pair_bias(col_ref, row_ref, query, keys[step])
            for head in range(heads):
                queries = qkv_ref[0, head, pl.ds(at, size), :]
                grad = grad_ref[head, pl.ds(at, size), :]
                lse = lse_ref[head : head + 1, pl.ds(at, size)]
                delta = delta_ref[head : head + 1, pl.ds(at, size)]
                merged = 0.0
                for step in range(count):
                    rows = pl.ds(starts[step], size)
                    probs = jnp.exp(
                        dot_nt(qkv_ref[1, head, rows, :], queries) + (bias_at[step] - lse)
                    )
                    d_probs = dot_nt(qkv_ref[2, head, rows, :], grad)
                    d_scores = (probs * (d_probs - delta)).astype(bf16)
                    dv_ref[head, rows, :] += dot_nn(probs.astype(bf16), grad)
                    dk_ref[head, rows, :] += dot_nn(d_scores, queries)
                    merged = merged + dot_nn(kt_ref[head, :, rows], d_scores)
                sum_ref[head * HEAD_DIM : (head + 1) * HEAD_DIM, :] = merged

        each_count(windows, query, blocks, body)
        merged = jnp.transpose(sum_ref[...])[:, :cols] * (HEAD_DIM**-0.5)
        dproj_ref[0, pl.ds(at, size), :] = merged.astype(bf16)
        return carry

    lax.fori_loop(0, blocks, one_query, 0)
    for head in range(heads):
        lanes = slice(head * HEAD_DIM, (head + 1) * HEAD_DIM)
        dproj_ref[1, :, lanes] = dk_ref[head].astype(bf16)
        dproj_ref[2, :, lanes] = dv_ref[head].astype(bf16)
    sums_ref[0:1, :] = jnp.sum(dproj_ref[0].astype(f32), axis=0, keepdims=True)
    sums_ref[1:2, :] = jnp.sum(dproj_ref[2].astype(f32), axis=0, keepdims=True)
    for part in range(2):
        at = slice(part * (count // 2), (part + 1) * (count // 2))
        back = (
            dot_nt(dproj_ref[0, at, :], w_ref[0])
            + dot_nt(dproj_ref[1, at, :], w_ref[1])
            + dot_nt(dproj_ref[2, at, :], w_ref[2])
        ).astype(bf16)
        for distance in range(4):
            target = send_ref if distance & 1 else keep_ref
            target[distance >> 1, part] = back[distance * share : (distance + 1) * share]


def attention_backward(place, qkv, clip, merged, lse, code_col, code_row, grads, weights):
    _, heads, count, _ = qkv.shape
    cols = heads * HEAD_DIM
    width = weights.shape[1]
    bf16, f32 = jnp.bfloat16, jnp.float32
    return call_kernel(
        attention_pull_kernel,
        place,
        (qkv, clip, merged, lse, code_col, code_row, *grads, weights),
        (
            *(shaped((2, 2, count // 8, width), bf16),) * 2,
            shaped((3, count, cols), bf16),
            shaped((2, cols), f32),
        ),
        (
            pltpu.VMEM((heads, count, HEAD_DIM), bf16),
            pltpu.VMEM((heads, HEAD_DIM, count), bf16),
            pltpu.VMEM((heads, count, HEAD_DIM), f32),
            pltpu.VMEM((heads, count, HEAD_DIM), f32),
            pltpu.VMEM((256, QUERY_BLOCK), f32),
            pltpu.VMEM((8, count), f32),
            pltpu.VMEM((count // QUERY_BLOCK, QUERY_BLOCK, QUERY_BLOCK), f32),
        ),
        flops=2 * count * width * cols * 3 + 10 * count * count * cols,
        moved=8 * count * width,
        exps=heads * count * count,
    )


def unit_of(stream):
    mean = jnp.mean(stream, axis=-1, keepdims=True)
    centred = stream - mean
    scale = lax.rsqrt(jnp.mean(centred * centred, axis=-1, keepdims=True) + epsilon)
    return centred * scale, scale


def column_sum(value):
    return jnp.sum(value, axis=0, keepdims=True)


def dot_tn(left, right):
    return lax.dot_general(left, right, (((0,), (0,)), ((), ())), preferred_element_type=jnp.float32)


def out_norm_kernel(student, place_ref, *refs):
    if student:
        c_refs, pieces = refs[:4], refs[4:12]
        own_ref, other_ref, valid_ref, params_ref, cot_ref = refs[12:17]
        w_ref, unit_ref, scale_ref, low_ref, sums_ref, token_ref = refs[17:]
        token_ref[...] = jnp.zeros_like(token_ref)
    else:
        c_refs, w_ref = refs[:4], refs[4]
        own_ref, other_ref, valid_ref, params_ref = refs[5:9]
        wide_ref, low_ref, token_ref = refs[9:]
        token_ref[...] = jnp.zeros_like(token_ref)
    share = own_ref.shape[0]
    cols = c_refs[0].shape[1] // 2
    size = w_ref.shape[1] // 4
    total = None
    for r, source in enumerate(c_refs):
        if student:
            group = pieces[:4] if r % 2 == 0 else pieces[4:]
            for distance, piece in zip((0, 2, 1, 3), group):
                start = pl.multiple_of((place_ref[0] ^ distance) * size, 64)
                w_ref[r, pl.ds(start, size), :] = piece[r >> 1, 2 * size : 3 * size, :]
            weights = w_ref[r, :, 0:cols]
        else:
            weights = w_ref[r, :, cols : 2 * cols]
        context = jnp.concatenate([source[:, 0:cols], source[:, cols:]], axis=0)
        term = dot_nt(context, weights)
        total = term if total is None else total + term
    attn = total + params_ref[0:1, :]
    stream = jnp.concatenate([own_ref[...], other_ref[...]], axis=0).astype(jnp.float32)
    unit, scale = unit_of(stream + attn)
    wide = unit * params_ref[2:3, :] + params_ref[3:4, :]
    low_ref[0 : 2 * share, :] = wide.astype(jnp.bfloat16)
    if student:
        low_ref[2 * share :, :] = cot_ref[...]
        unit_ref[...] = unit
        scale_ref[...] = scale
        valid = valid_ref[...]
        sums_ref[0:1, :] = column_sum(valid * jnp.ones_like(stream))
        sums_ref[1:2, :] = column_sum(valid * stream * stream)
        sums_ref[2:3, :] = column_sum(valid * attn * attn)
    else:
        wide_ref[...] = wide


def out_norm(student, place, contexts, weights, own, other, valid, params, cot=()):
    share, width = own.shape
    rows = 2 * share
    cols = contexts[0].shape[-1] // 2
    f32, bf16 = jnp.float32, jnp.bfloat16
    if student:
        outs = (
            shaped((4, width, 2 * cols), bf16),
            shaped((rows, width), f32),
            shaped((rows, 1), f32),
            shaped((rows + share, width), bf16),
            shaped((3, width), f32),
            shaped(TOKEN, f32),
        )
    else:
        outs = (shaped((rows, width), f32), shaped((rows, width), bf16), shaped(TOKEN, f32))
    return call_kernel(
        functools.partial(out_norm_kernel, student),
        place,
        (*contexts, *(weights if student else (weights,)), own, other, valid, params, *cot),
        outs,
        flops=2 * rows * width * cols * 4,
        moved=12 * rows * width,
    )


def gelu_parts(values):
    cdf = 0.5 * (1.0 + lax.erf(values * (2.0**-0.5)))
    return values * cdf, cdf


def hidden_kernel(student, assemble, far, place_ref, h_ref, *refs):
    refs = list(refs)
    pieces = [refs.pop(0) for _ in range(8 if assemble else 1)]
    with_terms = student and assemble
    terms_ref = None if with_terms else refs.pop(0)
    w_ref = refs.pop(0) if assemble else pieces[0]
    if with_terms:
        terms_ref = refs.pop(0)
    if student:
        hid_ref, slope_ref = refs.pop(0), refs.pop(0)
    part_ref, token_ref = refs
    token_ref[...] = jnp.zeros_like(token_ref)
    bf16 = jnp.bfloat16
    total = None
    inputs = h_ref[0 : part_ref.shape[0], :]
    for r in range(4):
        if assemble:
            group = pieces[:4] if r % 2 == 0 else pieces[4:]
            size = w_ref.shape[2] // 4
            for mat in range(2):
                for distance, piece in zip((0, 2, 1, 3), group):
                    start = pl.multiple_of((place_ref[0] ^ distance) * size, 64)
                    w_ref[r, mat, pl.ds(start, size), :] = piece[r >> 1, mat * size : (mat + 1) * size, :]
        if with_terms:
            terms_ref[r] = group[0][r >> 1, 3 * size : 3 * size + 16, :]
        terms = terms_ref[r].astype(jnp.float32)
        base = 0 if student else 6
        bias = terms[base : base + 1] + terms[base + 1 : base + 2] + terms[base + 2 : base + 3]
        upper = dot_nn(inputs, w_ref[r, 0]) + bias
        active, cdf = gelu_parts(upper)
        if student:
            clip = terms[3:4] + terms[4:5] + terms[5:6]
            ratio = jnp.tanh(active / clip)
            pdf = jnp.exp(-0.5 * upper * upper) * ((2.0 * math.pi) ** -0.5)
            slope_ref[r] = ((1.0 - ratio * ratio) * (cdf + upper * pdf)).astype(bf16)
            hidden = (clip * ratio).astype(bf16)
            hid_ref[r] = hidden
        else:
            hidden = active.astype(bf16)
        term = dot_nt(hidden, w_ref[r, 1])
        total = term if total is None else total + term
    part_ref[...] = total.astype(part_ref.dtype)


def hidden_layer(student, far, place, h, rows, weights, terms=None):
    width = h.shape[-1]
    half = weights[0].shape[-1] if isinstance(weights, tuple) else weights.shape[-1]
    f32, bf16 = jnp.float32, jnp.bfloat16
    assemble = isinstance(weights, tuple)
    outs = []
    if assemble:
        outs.append(shaped((4, 2, width, half), bf16))
        if student:
            outs.append(shaped((4, 16, half), bf16))
    if student:
        outs += [shaped((4, rows, half), bf16)] * 2
    outs += [shaped((rows, width), bf16 if far else f32), shaped(TOKEN, f32)]
    inputs = (h, *(weights if assemble else (weights,))) + (() if terms is None else (terms,))
    return call_kernel(
        functools.partial(hidden_kernel, student, assemble, far),
        place,
        inputs,
        tuple(outs),
        flops=2 * rows * width * half * 8,
        moved=8 * width * half * 2 + 16 * rows * half,
        exps=(3 if student else 1) * rows * half * 4,
    )


def loss_kernel(
    place_ref, unit_ref, ffn_ref, got_ref, ht_ref, ffnt_ref, gott_ref, cot_ref, cot_other_ref, valid_ref, params_ref, t_ref,
    layer_ref, layer_other_ref, dz_ref, low_ref, sums_ref,
):
    share = cot_ref.shape[0]
    rows = 2 * share
    f32, bf16 = jnp.float32, jnp.bfloat16
    h_one = unit_ref[...] * params_ref[2:3, :] + params_ref[3:4, :]
    ffn = ffn_ref[...] + got_ref[...].astype(f32) + params_ref[1:2, :]
    unit, scale = unit_of(h_one + ffn)
    out = unit * params_ref[4:5, :] + params_ref[5:6, :]
    low = out.astype(bf16)
    layer_ref[...] = low[:share]
    layer_other_ref[...] = low[share:]
    t_unit, _ = unit_of(ht_ref[...] + ffnt_ref[...] + gott_ref[...].astype(f32) + t_ref[1:2, :])
    difference = out - (t_unit * t_ref[4:5, :] + t_ref[5:6, :])
    valid = valid_ref[...]
    gap = valid * difference
    arriving = jnp.concatenate([cot_ref[...], cot_other_ref[rows:, :]], axis=0).astype(f32)
    grad = arriving + gap
    inner = grad * params_ref[4:5, :]
    dz = scale * (
        inner
        - jnp.mean(inner, axis=-1, keepdims=True)
        - unit * jnp.mean(inner * unit, axis=-1, keepdims=True)
    )
    dz_ref[...] = dz
    dz_low = dz.astype(bf16)
    low_ref[...] = dz_low
    sums_ref[0:1, :] = column_sum(dz_low.astype(f32))
    sums_ref[1:2, :] = column_sum(grad * unit)
    sums_ref[2:3, :] = column_sum(grad)
    sums_ref[3:4, :] = column_sum(valid * ffn * ffn)
    sums_ref[4:5, :] = column_sum(gap * difference)


def loss_step(place, unit, ffn, got, ht, ffnt, gott, cot, cot_other, valid, params, t_rows):
    rows, width = unit.shape
    share = cot.shape[0]
    f32, bf16 = jnp.float32, jnp.bfloat16
    return call_kernel(
        loss_kernel,
        place,
        (unit, ffn, got, ht, ffnt, gott, cot, cot_other, valid, params, t_rows),
        (
            shaped((share, width), bf16),
            shaped((share, width), bf16),
            shaped((rows, width), f32),
            shaped((rows, width), bf16),
            shaped((5, width), f32),
        ),
        flops=60 * rows * width,
        moved=30 * rows * width,
    )


def hidden_pull_kernel(place_ref, grad_ref, w_ref, slope_ref, du_ref, part_ref, sums_ref):
    grad = grad_ref[0 : part_ref.shape[0], :]
    total = None
    for r in range(4):
        upper = (dot_nn(grad, w_ref[r, 1]) * slope_ref[r].astype(jnp.float32)).astype(jnp.bfloat16)
        du_ref[r] = upper
        sums_ref[r : r + 1, :] = column_sum(upper.astype(jnp.float32))
        term = dot_nt(upper, w_ref[r, 0])
        total = term if total is None else total + term
    part_ref[...] = total.astype(part_ref.dtype)


def hidden_pull(far, place, grad, weights, slope):
    width = grad.shape[-1]
    rows = slope.shape[1]
    half = slope.shape[-1]
    f32, bf16 = jnp.float32, jnp.bfloat16
    return call_kernel(
        hidden_pull_kernel,
        place,
        (grad, weights, slope),
        (shaped((4, rows, half), bf16), shaped((rows, width), bf16 if far else f32), shaped((4, half), f32)),
        flops=2 * rows * width * half * 8,
        moved=8 * width * half * 2 + 16 * rows * half,
    )


def hidden_grads_kernel(mat, place_ref, l0, l1, r0, r1, keep_ref, send_ref, full_ref):
    rows = r0.shape[1]
    left = jnp.transpose(jnp.concatenate([l0[0:rows, :], l1[0:rows, :]], axis=0))
    size = full_ref.shape[0] // 4
    for r in range(4):
        right = jnp.concatenate([r0[r], r1[r]], axis=0)
        full_ref[...] = dot_nn(left, right)
        for slot in range(2):
            for target, distance in ((keep_ref, 2 * slot), (send_ref, 2 * slot + 1)):
                start = pl.multiple_of((place_ref[0] ^ distance) * size, 64)
                target[slot, r] = full_ref[pl.ds(start, size), :].astype(jnp.bfloat16)


def hidden_grads(place, left, right):
    width = left[0].shape[-1]
    rows, half = right[0].shape[1:]
    out = shaped((2, 4, width // 4, half), jnp.bfloat16)
    return call_kernel(
        functools.partial(hidden_grads_kernel, 0),
        place,
        (*left, *right),
        (out, out),
        (pltpu.VMEM((width, half), jnp.float32),),
        flops=16 * rows * width * half * 4,
        moved=8 * width * half * 2,
    )


def first_pull_kernel(place_ref, dz_ref, part_ref, got_ref, unit_ref, scale_ref, params_ref, w_ref, first_ref, low_ref, sums_ref, *ctx_refs):
    f32, bf16 = jnp.float32, jnp.bfloat16
    grad = dz_ref[...] + part_ref[...] + got_ref[...].astype(f32)
    unit = unit_ref[...]
    inner = grad * params_ref[2:3, :]
    first = scale_ref[...] * (
        inner
        - jnp.mean(inner, axis=-1, keepdims=True)
        - unit * jnp.mean(inner * unit, axis=-1, keepdims=True)
    )
    first_ref[...] = first
    low = first.astype(bf16)
    low_ref[...] = low
    sums_ref[0:1, :] = column_sum(low.astype(f32))
    sums_ref[1:2, :] = column_sum(grad * unit)
    sums_ref[2:3, :] = column_sum(grad)
    share, cols = ctx_refs[0].shape[0], ctx_refs[0].shape[1] // 2
    for r in range(4):
        back = dot_nn(low, w_ref[r, :, 0:cols]).astype(bf16)
        ctx_refs[r][:, 0:cols] = back[:share]
        ctx_refs[r][:, cols:] = back[share:]


def first_pull(place, dz, part, got, unit, scale, params, weights):
    rows, width = dz.shape
    cols = weights.shape[-1] // 2
    f32, bf16 = jnp.float32, jnp.bfloat16
    return call_kernel(
        first_pull_kernel,
        place,
        (dz, part, got, unit, scale, params, weights),
        (
            shaped((rows, width), f32),
            shaped((rows, width), bf16),
            shaped((3, width), f32),
            *(shaped((rows // 2, 2 * cols), bf16),) * 4,
        ),
        flops=2 * rows * width * cols * 4,
        moved=20 * rows * width,
    )


def last_grads_kernel(place_ref, low_ref, c0, c1, c2, c3, a_ref, a_other_ref, d_ref, qv_ref, keep_ref, send_ref, full_ref):
    size, cols = full_ref.shape[0] // 4, full_ref.shape[1]
    half = a_ref.shape[0]
    low = jnp.transpose(low_ref[...])
    own, other = jnp.transpose(a_ref[...]), jnp.transpose(a_other_ref[...])
    spots = ((0, 0), (1, 0), (0, 1), (1, 1), (2, 0), (2, 1), (3, 0))
    for entry, (block, side) in enumerate(spots):
        if entry < 4:
            source = (c0, c1, c2, c3)[entry]
            context = jnp.concatenate([source[:, 0:cols], source[:, cols:]], axis=0)
            full_ref[...] = dot_nn(low, context)
        else:
            full_ref[...] = dot_nn(own, d_ref[entry - 4, 0:half, :]) + dot_nn(
                other, d_ref[entry - 4, half:, :]
            )
        for slot in range(2):
            for target, distance in ((keep_ref, 2 * slot), (send_ref, 2 * slot + 1)):
                start = pl.multiple_of((place_ref[0] ^ distance) * size, 64)
                target[slot, block * size : (block + 1) * size, side * cols : (side + 1) * cols] = (
                    full_ref[pl.ds(start, size), :].astype(jnp.bfloat16)
                )
    sums = jnp.concatenate([qv_ref[...], jnp.zeros((14, cols), jnp.float32)], axis=0)
    sums = jnp.concatenate([sums, jnp.zeros((16, cols), jnp.float32)], axis=1)
    nothing = jnp.zeros((size, cols), jnp.bfloat16)
    for slot in range(2):
        for target in (keep_ref, send_ref):
            target[slot, 3 * size : 4 * size, cols:] = nothing
            target[slot, 4 * size :, :] = sums.astype(jnp.bfloat16)


def last_grads(place, low, contexts, a_in, d_proj, d_bias_qv):
    rows, width = low.shape
    count = d_proj.shape[1]
    cols = d_proj.shape[-1]
    out = shaped((2, 4 * (width // 4) + 16, 2 * cols), jnp.bfloat16)
    return call_kernel(
        last_grads_kernel,
        place,
        (low, *contexts, *a_in, d_proj, d_bias_qv),
        (out, out),
        (pltpu.VMEM((width, cols), jnp.float32),),
        flops=2 * (4 * rows + 3 * count) * width * cols,
        moved=4 * count * width,
    )


def input_kernel(place_ref, first_ref, b0, b1, b2, own_ref, other_ref, clip_ref, mine_ref, other_out_ref):
    f32 = jnp.float32
    share = own_ref.shape[0]
    for part, (source, target) in enumerate(((own_ref, mine_ref), (other_ref, other_out_ref))):
        through = b0[0, part].astype(f32) + b1[0, part].astype(f32) + b2[part].astype(f32)
        inside = jnp.abs(source[...].astype(f32)) < clip_ref[...]
        first = first_ref[part * share : (part + 1) * share, :]
        target[...] = (first + jnp.where(inside, through, 0.0)).astype(target.dtype)


def input_rows(place, first, backs, own, other, clip_in):
    share, width = own.shape
    return call_kernel(
        input_kernel,
        place,
        (first, *backs, own, other, clip_in),
        (shaped((share, width), jnp.float32), shaped((share, width), jnp.bfloat16)),
        flops=10 * share * width,
        moved=20 * share * width,
    )


def vector_kernel(place_ref, third_ref, second_ref, first_ref, own_ref, far_ref, out_ref):
    half = own_ref.shape[1]
    out_ref[...] = jnp.zeros_like(out_ref)
    out_ref[0:3, :] = third_ref[...]
    out_ref[3:8, :] = second_ref[...]
    out_ref[8:11, :] = first_ref[...]
    for r in range(4):
        part = own_ref[r : r + 1, :] + far_ref[r : r + 1, :]
        nothing = jnp.zeros_like(part)
        left = jnp.where(place_ref[2] == 0, part, nothing)
        right = jnp.where(place_ref[2] == 0, nothing, part)
        out_ref[pl.ds(11 + (place_ref[1] ^ r), 1), :] = jnp.concatenate([left, right], axis=1)


def vector_rows(place, third, second, first, own, far):
    width = third.shape[1]
    return call_kernel(
        vector_kernel,
        place,
        (third, second, first, own, far),
        shaped((16, width), jnp.float32),
        flops=1,
        moved=1,
    )


def sign_of(value):
    return jnp.where(value > 0.0, 1.0, jnp.where(value < 0.0, -1.0, 0.0))


def piece_kernel(place_ref, *refs):
    sources, (piece_ref, teacher_ref), copies, sems = refs[:11], refs[11:13], refs[13:24], refs[24]
    moves = [
        pltpu.make_async_copy(source, target, sems.at[at])
        for at, (source, target) in enumerate(zip(sources, copies))
    ]
    for move in moves:
        move.start()
    for move in moves:
        move.wait()
    up_ref, down_ref, out_ref, t_out_ref, t_up_ref, t_down_ref, quant_ref, columns_ref, *rows = copies
    bf16, f32 = jnp.bfloat16, jnp.float32
    size, half = up_ref.shape[0], piece_ref.shape[1]
    lanes = pl.ds(pl.multiple_of(place_ref[2] * half, 128), half)
    quant = quant_ref[:, lanes]
    up = quant[1:2] * sign_of(up_ref[:, lanes] - quant[0:1])
    piece_ref[0:size, :] = up.astype(bf16)
    columns = columns_ref[...]
    down = columns[:, 3:4] * sign_of(down_ref[:, lanes] - columns[:, 2:3])
    piece_ref[size : 2 * size, :] = down.astype(bf16)
    out = columns[:, 1:2] * sign_of(out_ref[...] - columns[:, 0:1])
    piece_ref[2 * size : 3 * size, :] = jnp.concatenate([out.astype(bf16), t_out_ref[...]], axis=1)
    terms = []
    for row in rows:
        rest = row[:, lanes]
        for _ in range(3):
            term = rest.astype(bf16).astype(f32)
            terms.append(term)
            rest = rest - term
    terms = jnp.concatenate(terms + [jnp.zeros((7, half), f32)], axis=0)
    piece_ref[3 * size :, :] = terms.astype(bf16)
    teacher_ref[0:size, :] = t_up_ref[:, lanes]
    teacher_ref[size:, :] = t_down_ref[:, lanes]


def own_pieces(place, *sources):
    size, wide = sources[0].shape
    bf16 = jnp.bfloat16
    return call_kernel(
        piece_kernel,
        place,
        sources,
        (shaped((3 * size + 16, wide // 2), bf16), shaped((2 * size, wide // 2), bf16)),
        tuple(pltpu.VMEM(source.shape, source.dtype) for source in sources)
        + (pltpu.SemaphoreType.DMA((len(sources),)),),
        flops=1,
        moved=1,
        from_hbm=True,
    )


def finish_kernel(place_ref, vector_ref, got_ref, rows_ref, up_ref, stat_ref):
    total = vector_ref[...] + got_ref[...]
    ordered = jnp.concatenate([total[0:1], total[3:4], total[1:3], total[4:6]], axis=0)
    size = rows_ref.shape[1]
    part = ordered[:, 0:size]
    for index in range(1, 4):
        part = jnp.where(place_ref[0] == index, ordered[:, index * size : (index + 1) * size], part)
    rows_ref[...] = part
    up = total[11:12]
    for index in range(1, 4):
        up = jnp.where(place_ref[1] == index, total[11 + index : 12 + index], up)
    up_ref[...] = up
    sums = jnp.sum(total[6:11], axis=-1, keepdims=True)
    means = sums / sums[2:3]
    lane = lax.broadcasted_iota(jnp.int32, stat_ref.shape, 1)
    stat_ref[...] = jnp.where(
        lane == 0,
        jnp.sqrt(means[3:4]),
        jnp.where(lane == 1, jnp.sqrt(means[4:5]), jnp.where(lane == 2, jnp.sqrt(means[0:1]), means[1:2])),
    )


def finish_vectors(place, vector, got):
    width = vector.shape[1]
    f32 = jnp.float32
    return call_kernel(
        finish_kernel,
        place,
        (vector, got),
        (shaped((6, width // 4), f32), shaped((1, width), f32), shaped((1, 128), f32)),
        flops=1,
        moved=1,
    )


def swap_ctx(value):
    return lax.ppermute(value, "ctx", [(0, 1), (1, 0)])


def swap_core(value):
    return lax.ppermute(value, "fsdp", [(i, i ^ 1) for i in range(4)])


def swap_row(value):
    return lax.ppermute(value, "fsdp", [(i, i ^ 2) for i in range(4)])


def swap_tp(value, distance):
    return lax.ppermute(value, "tp", [(i, i ^ distance) for i in range(4)])


def fsdp_pieces(piece):
    far = swap_row(piece)
    return (piece, far, swap_core(piece), swap_core(far))


def exchange_tp(entries):
    return [entries[0]] + [swap_tp(entries[r], r) for r in (1, 2, 3)]


def three_terms(value):
    high = lax.reduce_precision(value, 8, 7)
    rest = value - high
    middle = lax.reduce_precision(rest, 8, 7)
    return [high.astype(jnp.bfloat16), middle.astype(jnp.bfloat16), (rest - middle).astype(jnp.bfloat16)]


def tie(values, *others):
    return lax.optimization_barrier((values, others))[0]


def once(place, *arrays):
    return (place, arrays)


def paired_body(
    tokens,
    cotangent,
    segment_ids,
    valid_mask,
    latent_qkv,
    latent_out,
    latent_up,
    latent_down,
    qkv_quant,
    up_quant,
    out_quant,
    down_quant,
    bias_qv,
    bias_up,
    row_params,
    clip_in,
    clip_ctx,
    clip_hidden,
    t_qkv,
    t_out,
    t_up,
    t_down,
    t_bias_qv,
    t_bias_up,
    t_rows,
):
    local_len, seq_count, width = tokens.shape
    share = cotangent.shape[0]
    col_width = latent_qkv.shape[2]
    hidden_width = latent_up.shape[1]
    half_hidden = hidden_width // 2
    row_width = latent_qkv.shape[0]
    tp_rank = lax.axis_index("tp")
    ctx_rank = lax.axis_index("ctx")
    fsdp_rank = lax.axis_index("fsdp")
    f32, bf16 = jnp.float32, jnp.bfloat16
    place = jnp.stack([fsdp_rank, tp_rank, ctx_rank]).astype(jnp.int32)

    def by_distance(value):
        pairs = value.reshape(2, 2, *value.shape[1:])
        pairs = jnp.where((tp_rank & 1) > 0, pairs[:, ::-1], pairs)
        pairs = jnp.where((tp_rank >> 1) > 0, pairs[::-1], pairs)
        return pairs.reshape(value.shape)

    def mine(value, axis):
        return lax.dynamic_index_in_dim(value, ctx_rank, axis, keepdims=False)

    def theirs(value, axis):
        return lax.dynamic_index_in_dim(value, 1 - ctx_rank, axis, keepdims=False)

    def half_of(weight):
        return jnp.where(ctx_rank == 0, weight[..., :half_hidden], weight[..., half_hidden:])

    def add(left, right):
        return left.astype(f32) + right.astype(f32)

    rows = 2 * share
    bin_up = binarize(latent_up, up_quant[0][None], up_quant[1][None])
    bin_down = binarize(latent_down, down_quant[0][:, None], down_quant[1][:, None])
    terms = [term for v in (bias_up, clip_hidden, t_bias_up) for term in three_terms(half_of(v))]
    vectors = jnp.pad(jnp.stack(terms), ((0, 16 - len(terms)), (0, 0)))
    bin_out = binarize(latent_out, out_quant[0][:, None], out_quant[1][:, None])
    piece = jnp.concatenate(
        [
            half_of(bin_up),
            half_of(bin_down),
            jnp.concatenate([bin_out, t_out], axis=1),
            vectors,
        ],
        axis=0,
    )
    piece_two = swap_tp(piece, 2)
    rows = 2 * share
    tokens_then, segment_then = tie((tokens, segment_ids), piece)
    relative = by_distance(tokens_then.reshape(4, share, seq_count, width))
    own = mine(relative, 2).reshape(local_len, width)
    code = by_distance(
        jnp.transpose(segment_then * 2 + (valid_mask > 0).astype(jnp.int32)).reshape(
            4, share, seq_count
        )
    )
    code_sent = jnp.pad(theirs(code, 2).reshape(1, local_len), ((0, 15), (0, width - local_len)))
    tokens_sent = jnp.concatenate(
        [theirs(relative, 2).reshape(local_len, width), code_sent.astype(bf16)], axis=0
    )
    other = swap_ctx(tokens_sent)
    latent_qkv_then, t_qkv = tie((latent_qkv, t_qkv), tokens_sent)
    bin_qkv = jnp.transpose(
        binarize(latent_qkv_then, qkv_quant[0][None], qkv_quant[1][None]), (1, 0, 2)
    )
    qkv_piece = jnp.concatenate([bin_qkv, jnp.transpose(t_qkv, (1, 0, 2))], axis=2)
    qkv_pieces = fsdp_pieces(qkv_piece)
    t_up, t_down = tie((t_up, t_down), qkv_piece)
    teacher_piece = jnp.concatenate([half_of(t_up), half_of(t_down)], axis=0)
    clip_in_row, clip_row = clip_in[None], clip_ctx[None]

    own_rows = own[:share]
    cot_own, cot_sent = mine(cotangent, 1), theirs(cotangent, 1)
    full_qkv, a_own, qkv_own, token = project_own(once(place, own_rows, cot_own, cot_sent), own, qkv_pieces, bias_qv, clip_in_row)
    other = tie(other, token)
    code_all = jnp.concatenate(
        [mine(code, 2).reshape(local_len), other[local_len, :local_len].astype(jnp.int32)]
    )
    code_col, code_row = code_all[:, None], code_all[None, :]
    valid = (
        jnp.concatenate([code_all[:share], code_all[local_len : local_len + share]]) & 1
    ).astype(f32)[:, None]
    even = jnp.stack([piece, tie(piece_two, token)])
    odd, even_row = swap_tp(even, 1), swap_row(even)
    *context, a_other, other_rows, qkv, merged, lse = attention_forward(
        True, once(place, even, token), other, full_qkv, qkv_own, bias_qv, clip_in_row,
        clip_row, code_col, code_row,
    )
    contexts = exchange_tp(context)
    odd, even_row = tie((odd, even_row), lse)
    even_cores = (swap_core(even), swap_core(even_row))
    odd_row = swap_row(odd)
    *teacher_context, token = attention_forward(
        False, once(place, lse, *even_cores), other, qkv_pieces, own,
        t_bias_qv, clip_in_row, clip_row, code_col, code_row,
    )
    token = gate(place, token, *contexts[1:])
    odd, odd_row, teacher_piece = tie((odd, odd_row, teacher_piece), token)
    teacher_two = swap_tp(teacher_piece, 2)
    pieces = (
        even, even_row, *even_cores,
        odd, odd_row, swap_core(odd), swap_core(odd_row),
    )
    out_full, unit, scale, h_low, first_sums, token = out_norm(
        True, once(place, token), contexts, pieces, own_rows, other_rows, valid, row_params,
        (cot_sent,),
    )
    h_far = swap_ctx(h_low)
    teacher_contexts = exchange_tp([teacher_context[0], *tie(teacher_context[1:], token)])
    hidden_full, terms, hid_own, slope_own, part_own, _ = hidden_layer(
        True, False, once(place, token), h_low, rows, pieces
    )
    teacher_even = jnp.stack([teacher_piece, tie(teacher_two, terms, *teacher_contexts[1:])])
    teacher_odd, teacher_even_row = swap_tp(teacher_even, 1), swap_row(teacher_even)
    h_teacher, ht_low, token = out_norm(
        False, once(place, part_own), teacher_contexts, out_full, own_rows, other_rows, valid, t_rows,
    )
    ht_far = swap_ctx(ht_low)
    hid_far, slope_far, part_far, token = hidden_layer(
        True, True, once(place, token), h_far, rows, hidden_full, terms
    )
    part_got = swap_ctx(part_far)
    teacher_odd = tie(teacher_odd, token)
    teacher_even_row = tie(teacher_even_row, token, ht_far)
    teacher_odd_row = swap_row(teacher_odd)
    teacher_hidden = (
        teacher_even, teacher_even_row, swap_core(teacher_even), swap_core(teacher_even_row),
        teacher_odd, teacher_odd_row, swap_core(teacher_odd), swap_core(teacher_odd_row),
    )
    teacher_full, t_part_far, _ = hidden_layer(
        False, True, once(place, token), ht_far, rows, teacher_hidden, terms
    )
    t_part_got = swap_ctx(t_part_far)
    t_part_own, _ = hidden_layer(
        False, False, once(place, t_part_far), ht_low, rows, teacher_full, terms
    )
    layer_own, layer_other, d_second, d_ffn, second_sums = loss_step(
        place, unit, part_own, part_got, h_teacher, t_part_own, t_part_got,
        cot_own, h_far, valid, row_params, t_rows,
    )

    def home(own_part, other_part):
        got = other_part.astype(own_part.dtype)
        first = jnp.where(ctx_rank == 0, own_part, got)
        second = jnp.where(ctx_rank == 0, got, own_part)
        return jnp.stack([first, second], axis=1)

    d_ffn_far = swap_ctx(d_ffn)
    du_own, d_part_own, du_sums_own = hidden_pull(False, place, d_ffn, hidden_full, slope_own)
    du_far, d_part_far, du_sums_far = hidden_pull(True, place, d_ffn_far, hidden_full, slope_far)
    d_part_got = swap_ctx(d_part_far)
    keep_down, send_down = hidden_grads(
        once(place, du_sums_far), (d_ffn, d_ffn_far), (hid_own, hid_far)
    )
    got_down = swap_core(send_down)
    leave_down = add(keep_down[1], got_down[1]).astype(bf16)
    d_first, d_attn, third_sums, *d_context = first_pull(
        once(place, send_down), d_second, d_part_own, d_part_got, unit, scale, row_params, out_full
    )
    d_contexts = exchange_tp(d_context)
    keep_up, send_up = hidden_grads(once(place, third_sums), (h_low, h_far), (du_own, du_far))
    got_up = swap_core(send_up)
    leave_up = add(keep_up[1], got_up[1]).astype(bf16)
    vector = vector_rows(place, third_sums, second_sums, first_sums, du_sums_own, du_sums_far)
    keep_back, send_back, d_proj, d_bias_qv = attention_backward(
        once(place, leave_down, leave_up, vector),
        qkv, clip_row, merged, lse, code_col, code_row, d_contexts, full_qkv,
    )
    got_back = swap_tp(send_back, 1)
    got_down_row = tie(swap_row(leave_down), d_bias_qv)
    got_up_row = tie(swap_row(leave_up), d_bias_qv)
    row_down = add(add(keep_down[0], got_down[0]), got_down_row)
    row_up = add(add(keep_up[0], got_up[0]), got_up_row)
    keep_last, send_last = last_grads(
        once(place, send_back, got_down_row),
        d_attn, contexts, (a_own, a_other), d_proj, d_bias_qv,
    )
    got_last, vector_got = swap_core(send_last), swap_core(tie(vector, send_last))
    got_back = tie(got_back, send_last)
    leave_back = add(keep_back[1], got_back[1]).astype(bf16)
    got_back_two = swap_tp(leave_back, 2)
    layer_out = home(layer_own, swap_ctx(tie(layer_other, leave_back)))
    vector = tie(vector + vector_got, leave_back)
    vector_got = swap_ctx(vector)
    send_both = jnp.stack([row_down[1::2], row_up[1::2]]).astype(bf16)
    got_both = swap_tp(send_both, 1)
    leave_last = tie(add(keep_last[1], got_last[1]).astype(bf16), leave_back)
    got_last_row = swap_row(leave_last)
    vector = tie(vector + vector_got, leave_last)
    vector_got = swap_row(vector)
    entry = row_width
    row_last = add(add(keep_last[0], got_last[0]), got_last_row)
    send_one = row_last[entry : 2 * entry].astype(bf16)
    got_one = swap_tp(send_one, 1)
    leave_both = tie(
        jnp.stack([add(row_down[2], got_both[0, 1]), add(row_up[2], got_both[1, 1])]).astype(bf16), send_one
    )
    got_both_two = swap_tp(leave_both, 2)
    vector = tie(vector + vector_got, leave_both)
    vector_got = swap_tp(vector, 1)
    input_own, input_other = input_rows(
        once(place, leave_both), d_first, (keep_back, got_back, got_back_two), own_rows, other_rows, clip_in_row
    )
    input_grad = home(input_own, swap_ctx(input_other))
    out_two = add(row_last[0:entry], got_one)
    leave_two = out_two[:, col_width:].astype(bf16)
    got_two = swap_tp(leave_two, 2)
    low_both = add(
        jnp.stack([add(row_down[0], got_both[0, 0]), add(row_up[0], got_both[1, 0])]), got_both_two
    ).astype(bf16)
    low_out = add(out_two[:, :col_width], got_two)
    low_last = jnp.concatenate(
        [
            row_last[2 * entry : 3 * entry],
            jnp.concatenate([row_last[3 * entry : 4 * entry, :col_width], low_out], axis=1),
            row_last[4 * entry :],
        ],
        axis=0,
    ).astype(bf16)
    sum_last = add(low_last, swap_ctx(low_last))
    vector = tie(vector + vector_got, low_both)
    grad_rows, grad_up_bias, statistics = finish_vectors(place, vector, swap_tp(vector, 2))

    both_far = swap_ctx(low_both)
    grad_both = jnp.concatenate(
        [
            jnp.where(ctx_rank == 0, low_both, both_far),
            jnp.where(ctx_rank == 0, both_far, low_both),
        ],
        axis=-1,
    ).astype(f32)
    grad_up = straight(grad_both[1], latent_up, up_quant[0][None], up_quant[1][None])
    grad_down = straight(
        grad_both[0], latent_down, down_quant[0][:, None], down_quant[1][:, None]
    )
    grad_qkv = straight(
        jnp.stack(
            [
                sum_last[:entry, :col_width],
                sum_last[:entry, col_width:],
                sum_last[entry : 2 * entry, :col_width],
            ],
            axis=1,
        ),
        latent_qkv,
        qkv_quant[0][None],
        qkv_quant[1][None],
    )
    grad_out = straight(sum_last[entry : 2 * entry, col_width:], latent_out, out_quant[0][:, None], out_quant[1][:, None])
    grad_qv = sum_last[2 * entry : 2 * entry + 2, :col_width]
    grad_bias_up, statistics = grad_up_bias[0], statistics[0, :4]
    return (
        layer_out,
        input_grad,
        grad_qkv,
        grad_out,
        grad_up,
        grad_down,
        grad_rows,
        grad_qv,
        grad_bias_up,
        statistics,
    )


def general_body(
    tokens,
    cotangent,
    segment_ids,
    valid_mask,
    latent_qkv,
    latent_out,
    latent_up,
    latent_down,
    qkv_quant,
    up_quant,
    out_quant,
    down_quant,
    bias_qv,
    bias_up,
    row_params,
    clip_in,
    clip_ctx,
    clip_hidden,
    t_qkv,
    t_out,
    t_up,
    t_down,
    t_bias_qv,
    t_bias_up,
    t_rows,
):
    local_len, seq_count, width = tokens.shape
    share = cotangent.shape[0]
    col_width = latent_qkv.shape[2]
    hidden_width = latent_up.shape[1]
    row_width = latent_qkv.shape[0]
    local_heads = col_width // HEAD_DIM
    scale = HEAD_DIM ** (-0.5)
    tp_rank = lax.axis_index("tp")
    ctx_rank = lax.axis_index("ctx")
    fsdp_rank = lax.axis_index("fsdp")
    full_len = local_len * lax.axis_size("ctx")
    bin_qkv = binarize(latent_qkv, qkv_quant[0][None], qkv_quant[1][None])
    bin_out = binarize(latent_out, out_quant[0][:, None], out_quant[1][:, None])
    bin_up = binarize(latent_up, up_quant[0][None], up_quant[1][None])
    bin_down = binarize(latent_down, down_quant[0][:, None], down_quant[1][:, None])
    gathered = (
        lax.all_gather(bin_qkv, "fsdp", axis=0, tiled=True),
        lax.all_gather(bin_out, "fsdp", axis=0, tiled=True),
        lax.all_gather(bin_up, "fsdp", axis=0, tiled=True),
        lax.all_gather(bin_down, "fsdp", axis=0, tiled=True),
        lax.all_gather(t_qkv, "fsdp", axis=0, tiled=True),
        lax.all_gather(t_out, "fsdp", axis=0, tiled=True),
        lax.all_gather(t_up, "fsdp", axis=0, tiled=True),
        lax.all_gather(t_down, "fsdp", axis=0, tiled=True),
    )
    full_qkv, full_out, full_up, full_down, teach_qkv, teach_out, teach_up, teach_down = gathered
    stream = tokens.astype(jnp.float32)
    a_in = jnp.clip(stream, -clip_in, clip_in).astype(jnp.bfloat16)
    proj_student = jnp.einsum("tsd,dkh->tskh", a_in, full_qkv, preferred_element_type=jnp.float32)
    proj_teacher = jnp.einsum(
        "tsd,dkh->tskh", tokens, teach_qkv, preferred_element_type=jnp.float32
    )
    student_q = (proj_student[:, :, 0] + bias_qv[0]).astype(jnp.bfloat16)
    student_k = proj_student[:, :, 1].astype(jnp.bfloat16)
    student_v = (proj_student[:, :, 2] + bias_qv[1]).astype(jnp.bfloat16)
    teacher_q = (proj_teacher[:, :, 0] + t_bias_qv[0]).astype(jnp.bfloat16)
    teacher_k = proj_teacher[:, :, 1].astype(jnp.bfloat16)
    teacher_v = (proj_teacher[:, :, 2] + t_bias_qv[1]).astype(jnp.bfloat16)
    student_queries = headed(student_q)
    teacher_queries = headed(teacher_q)
    query_pos = ctx_rank * local_len + jnp.arange(local_len, dtype=jnp.int32)
    key_tags = jnp.transpose(jnp.where(valid_mask > 0, segment_ids, -1))
    empty_state = (
        jnp.full((seq_count, local_heads, local_len), floor_score, jnp.float32),
        jnp.zeros((seq_count, local_heads, local_len), jnp.float32),
        jnp.zeros((seq_count, local_heads, local_len, HEAD_DIM), jnp.float32),
    )
    buffers = (
        jnp.zeros((full_len, seq_count, col_width), jnp.bfloat16),
        jnp.zeros((full_len, seq_count, col_width), jnp.bfloat16),
        jnp.zeros((full_len, seq_count), jnp.int32),
    )
    carry = (empty_state, empty_state, buffers)
    pieces = (
        lax.all_gather(student_k, "ctx", axis=0, tiled=True),
        lax.all_gather(student_v, "ctx", axis=0, tiled=True),
        lax.all_gather(teacher_k, "ctx", axis=0, tiled=True),
        lax.all_gather(teacher_v, "ctx", axis=0, tiled=True),
        lax.all_gather(key_tags, "ctx", axis=0, tiled=True),
    )
    start = jnp.int32(0)
    count = pieces[0].shape[0]
    block = key_block(count)

    def inner(states, index):
        offset = index * block
        parts = [lax.dynamic_slice_in_dim(piece, offset, block, 0) for piece in pieces]
        key_pos = offset + jnp.arange(block, dtype=jnp.int32)
        allowed = allowed_pairs(segment_ids, query_pos, parts[4], key_pos)
        states = (
            online_step(
                states[0], student_queries, headed(parts[0]), headed(parts[1]), allowed, scale
            ),
            online_step(
                states[1], teacher_queries, headed(parts[2]), headed(parts[3]), allowed, scale
            ),
        )
        return (states, None)

    states, _ = lax.scan(inner, (carry[0], carry[1]), jnp.arange(count // block, dtype=jnp.int32))
    kept = tuple(
        (
            lax.dynamic_update_slice_in_dim(buffer, piece, start, 0)
            for buffer, piece in zip(carry[2], (pieces[0], pieces[1], pieces[4]))
        )
    )
    student_state, teacher_state, kept = (states[0], states[1], kept)
    attended, log_total = finish(student_state)
    teacher_attended, _ = finish(teacher_state)
    attended_flat = attended.reshape(local_len, seq_count, col_width)
    ctx_ratio = jnp.tanh(attended_flat / clip_ctx)
    context = (clip_ctx * ctx_ratio).astype(jnp.bfloat16)
    teacher_context = teacher_attended.reshape(local_len, seq_count, col_width).astype(jnp.bfloat16)
    rows_student = context
    rows_teacher = teacher_context
    attn_both = lax.psum_scatter(
        jnp.concatenate(
            [
                jnp.einsum(
                    "tsh,dh->tsd", rows_student, full_out, preferred_element_type=jnp.float32
                ),
                jnp.einsum(
                    "tsh,dh->tsd", rows_teacher, teach_out, preferred_element_type=jnp.float32
                ),
            ],
            axis=-1,
        ).astype(jnp.bfloat16),
        "tp",
        scatter_dimension=0,
        tiled=True,
    ).astype(jnp.float32)
    attn_student = attn_both[..., :width] + row_params[0]
    attn_teacher = attn_both[..., width:] + t_rows[0]
    stream_rows = lax.dynamic_slice_in_dim(stream, tp_rank * share, share, 0)
    first_sum = stream_rows + attn_student
    h_one = layer_norm(first_sum, row_params[2], row_params[3])
    h_teacher = layer_norm(stream_rows + attn_teacher, t_rows[2], t_rows[3])
    h_full, h_teacher_full = (
        lax.all_gather(h_one.astype(jnp.bfloat16), "tp", axis=0, tiled=True),
        lax.all_gather(h_teacher.astype(jnp.bfloat16), "tp", axis=0, tiled=True),
    )
    upper = jnp.einsum("tsd,df->tsf", h_full, full_up, preferred_element_type=jnp.float32) + bias_up
    activated = exact_gelu(upper)
    hid_ratio = jnp.tanh(activated / clip_hidden)
    hidden = (clip_hidden * hid_ratio).astype(jnp.bfloat16)
    upper_teacher = (
        jnp.einsum("tsd,df->tsf", h_teacher_full, teach_up, preferred_element_type=jnp.float32)
        + t_bias_up
    )
    hidden_teacher = exact_gelu(upper_teacher).astype(jnp.bfloat16)
    rows_student = hidden
    rows_teacher = hidden_teacher
    ffn_both = lax.psum_scatter(
        jnp.concatenate(
            [
                jnp.einsum(
                    "tsf,df->tsd", rows_student, full_down, preferred_element_type=jnp.float32
                ),
                jnp.einsum(
                    "tsf,df->tsd", rows_teacher, teach_down, preferred_element_type=jnp.float32
                ),
            ],
            axis=-1,
        ).astype(jnp.bfloat16),
        "tp",
        scatter_dimension=0,
        tiled=True,
    ).astype(jnp.float32)
    ffn_student = ffn_both[..., :width] + row_params[1]
    ffn_teacher = ffn_both[..., width:] + t_rows[1]
    second_sum = h_one + ffn_student
    out = layer_norm(second_sum, row_params[4], row_params[5])
    teacher_out = layer_norm(h_teacher + ffn_teacher, t_rows[4], t_rows[5])
    layer_out = out.astype(jnp.bfloat16)
    valid_rows = jnp.transpose(
        lax.dynamic_slice_in_dim(valid_mask, tp_rank * share, share, 1)
    ).astype(jnp.float32)[..., None]
    difference = out - teacher_out
    grad_out_total = cotangent.astype(jnp.float32) + valid_rows * difference
    stat_terms = jnp.stack(
        [
            jnp.sum(valid_rows) + 0.0 * jnp.sum(stream_rows[:1, :1, :1]),
            jnp.sum(valid_rows * stream_rows * stream_rows),
            jnp.sum(valid_rows * attn_student * attn_student),
            jnp.sum(valid_rows * ffn_student * ffn_student),
            jnp.sum(valid_rows * difference * difference),
        ]
    )
    _, second_pull = jax.vjp(layer_norm, second_sum, row_params[4], row_params[5])
    d_second, d_gain_two, d_bias_two = second_pull(grad_out_total)
    d_ffn = d_second.astype(jnp.bfloat16)
    d_bias_down = jnp.sum(d_ffn.astype(jnp.float32), axis=(0, 1))
    d_ffn_full = lax.all_gather(d_ffn, "tp", axis=0, tiled=True)
    grad_bin_down = jnp.einsum(
        "tsd,tsf->df", d_ffn_full, hidden, preferred_element_type=jnp.float32
    )
    d_hidden = jnp.einsum("tsd,df->tsf", d_ffn_full, full_down, preferred_element_type=jnp.float32)
    d_hidden = d_hidden * (1.0 - hid_ratio * hid_ratio)
    _, gelu_pull = jax.vjp(exact_gelu, upper)
    d_upper = gelu_pull(d_hidden)[0].astype(jnp.bfloat16)
    d_bias_up = jnp.sum(d_upper.astype(jnp.float32), axis=(0, 1))
    grad_bin_up = jnp.einsum("tsd,tsf->df", h_full, d_upper, preferred_element_type=jnp.float32)
    rows = d_upper
    d_h_one = d_second + lax.psum_scatter(
        jnp.einsum("tsf,df->tsd", rows, full_up, preferred_element_type=jnp.float32).astype(
            jnp.bfloat16
        ),
        "tp",
        scatter_dimension=0,
        tiled=True,
    ).astype(jnp.float32)
    _, first_pull = jax.vjp(layer_norm, first_sum, row_params[2], row_params[3])
    d_first, d_gain_one, d_bias_one = first_pull(d_h_one)
    d_attn = d_first.astype(jnp.bfloat16)
    d_bias_out = jnp.sum(d_attn.astype(jnp.float32), axis=(0, 1))
    d_attn_full = lax.all_gather(d_attn, "tp", axis=0, tiled=True)
    grad_bin_out = jnp.einsum(
        "tsd,tsh->dh", d_attn_full, context, preferred_element_type=jnp.float32
    )
    d_context = jnp.einsum("tsd,dh->tsh", d_attn_full, full_out, preferred_element_type=jnp.float32)
    d_attended = (d_context * (1.0 - ctx_ratio * ctx_ratio)).astype(jnp.bfloat16)
    d_attended_heads = headed(d_attended)
    delta = jnp.transpose(
        jnp.sum(d_attended_heads.astype(jnp.float32) * attended, axis=-1), (1, 2, 0)
    )
    key_all, value_all, tag_all = kept
    back_block = key_block(full_len)

    def back_step(grad_q, index):
        offset = index * back_block
        keys = headed(lax.dynamic_slice_in_dim(key_all, offset, back_block, 0))
        values = headed(lax.dynamic_slice_in_dim(value_all, offset, back_block, 0))
        block_tags = lax.dynamic_slice_in_dim(tag_all, offset, back_block, 0)
        key_pos = offset + jnp.arange(back_block, dtype=jnp.int32)
        allowed = allowed_pairs(segment_ids, query_pos, block_tags, key_pos)
        current = grad_q
        scores = (
            jnp.einsum("tshe,kshe->shtk", student_queries, keys, preferred_element_type=jnp.float32)
            * scale
        )
        probs = jnp.where(allowed, jnp.exp(scores - log_total[..., None]), 0.0)
        d_probs = jnp.einsum(
            "tshe,kshe->shtk", d_attended_heads, values, preferred_element_type=jnp.float32
        )
        d_scores = (probs * (d_probs - delta[..., None])).astype(jnp.bfloat16)
        current = (
            current
            + jnp.einsum("shtk,kshe->shte", d_scores, keys, preferred_element_type=jnp.float32)
            * scale
        )
        grad_k = (
            jnp.einsum(
                "shtk,tshe->kshe", d_scores, student_queries, preferred_element_type=jnp.float32
            )
            * scale
        )
        grad_v = jnp.einsum(
            "shtk,tshe->kshe",
            probs.astype(jnp.bfloat16),
            d_attended_heads,
            preferred_element_type=jnp.float32,
        )
        joined = jnp.concatenate(
            [
                grad_k.reshape(back_block, seq_count, col_width),
                grad_v.reshape(back_block, seq_count, col_width),
            ],
            axis=-1,
        )
        return (current, joined)

    grad_q, key_terms = lax.scan(
        back_step,
        jnp.zeros((seq_count, local_heads, local_len, HEAD_DIM), jnp.float32),
        jnp.arange(full_len // back_block, dtype=jnp.int32),
    )
    key_terms = key_terms.reshape(full_len, seq_count, 2 * col_width)
    key_sums = lax.psum_scatter(
        key_terms.astype(jnp.bfloat16), "ctx", scatter_dimension=0, tiled=True
    ).astype(jnp.float32)
    grad_q_flat = jnp.transpose(grad_q, (2, 0, 1, 3)).reshape(local_len, seq_count, col_width)
    d_proj = jnp.stack(
        [grad_q_flat, key_sums[..., :col_width], key_sums[..., col_width:]], axis=2
    ).astype(jnp.bfloat16)
    d_bias_qv = jnp.stack(
        [
            jnp.sum(d_proj[:, :, 0].astype(jnp.float32), axis=(0, 1)),
            jnp.sum(d_proj[:, :, 2].astype(jnp.float32), axis=(0, 1)),
        ]
    )
    grad_bin_qkv = jnp.einsum("tsd,tskh->dkh", a_in, d_proj, preferred_element_type=jnp.float32)
    rows = d_proj
    through = lax.psum_scatter(
        jnp.einsum("tskh,dkh->tsd", rows, full_qkv, preferred_element_type=jnp.float32).astype(
            jnp.bfloat16
        ),
        "tp",
        scatter_dimension=0,
        tiled=True,
    ).astype(jnp.float32)
    input_grad = d_first + through * (jnp.abs(stream_rows) < clip_in).astype(jnp.float32)
    shards = (
        lax.psum_scatter(
            grad_bin_qkv.astype(jnp.bfloat16), "fsdp", scatter_dimension=0, tiled=True
        ).astype(jnp.float32),
        lax.psum_scatter(
            grad_bin_out.astype(jnp.bfloat16), "fsdp", scatter_dimension=0, tiled=True
        ).astype(jnp.float32),
        lax.psum_scatter(
            grad_bin_up.astype(jnp.bfloat16), "fsdp", scatter_dimension=0, tiled=True
        ).astype(jnp.float32),
        lax.psum_scatter(
            grad_bin_down.astype(jnp.bfloat16), "fsdp", scatter_dimension=0, tiled=True
        ).astype(jnp.float32),
    )
    summed = (
        lax.psum(shards[0].astype(jnp.bfloat16), "ctx").astype(jnp.float32),
        lax.psum(shards[1].astype(jnp.bfloat16), "ctx").astype(jnp.float32),
        lax.psum(shards[2].astype(jnp.bfloat16), "ctx").astype(jnp.float32),
        lax.psum(shards[3].astype(jnp.bfloat16), "ctx").astype(jnp.float32),
    )
    grad_qkv = straight(summed[0], latent_qkv, qkv_quant[0][None], qkv_quant[1][None])
    grad_out = straight(summed[1], latent_out, out_quant[0][:, None], out_quant[1][:, None])
    grad_up = straight(summed[2], latent_up, up_quant[0][None], up_quant[1][None])
    grad_down = straight(summed[3], latent_down, down_quant[0][:, None], down_quant[1][:, None])
    vector_grads = jnp.stack(
        [d_bias_out, d_bias_down, d_gain_one, d_bias_one, d_gain_two, d_bias_two]
    )
    placed_qv = lax.dynamic_update_slice_in_dim(
        jnp.zeros((2, width), jnp.float32), d_bias_qv, tp_rank * col_width, 1
    )
    placed_up = lax.dynamic_update_slice_in_dim(
        jnp.zeros((hidden_width * lax.axis_size("tp"),), jnp.float32),
        d_bias_up,
        tp_rank * hidden_width,
        0,
    )
    stat_sums, vector_sums, qv_sums, up_sums = lax.psum(
        (stat_terms, vector_grads, placed_qv, placed_up), ("fsdp", "ctx", "tp")
    )
    grad_rows = lax.dynamic_slice_in_dim(vector_sums, fsdp_rank * row_width, row_width, 1)
    grad_qv = lax.dynamic_slice_in_dim(qv_sums, tp_rank * col_width, col_width, 1)
    grad_bias_up = lax.dynamic_slice_in_dim(up_sums, tp_rank * hidden_width, hidden_width, 0)
    denom = stat_sums[0] * width
    statistics = jnp.stack(
        [
            jnp.sqrt(stat_sums[1] / denom),
            jnp.sqrt(stat_sums[2] / denom),
            jnp.sqrt(stat_sums[3] / denom),
            stat_sums[4] / denom,
        ]
    )
    return (
        layer_out,
        input_grad,
        grad_qkv,
        grad_out,
        grad_up,
        grad_down,
        grad_rows,
        grad_qv,
        grad_bias_up,
        statistics,
    )


def pick_body(mesh):
    sizes = dict(mesh.shape)
    if sizes["fsdp"] == 4 and sizes["tp"] == 4 and sizes["ctx"] == 2:
        return paired_body
    return general_body


def solution(mesh):
    return jax.shard_map(
        pick_body(mesh),
        mesh=mesh,
        in_specs=(
            P("ctx", "fsdp", None),
            P(("ctx", "tp"), "fsdp", None),
            P("fsdp", "ctx"),
            P("fsdp", "ctx"),
            P("fsdp", None, "tp"),
            P("fsdp", "tp"),
            P("fsdp", "tp"),
            P("fsdp", "tp"),
            P(None, None, "tp"),
            P(None, "tp"),
            P(None, "fsdp"),
            P(None, "fsdp"),
            P(None, "tp"),
            P("tp"),
            P(),
            P(),
            P("tp"),
            P("tp"),
            P("fsdp", None, "tp"),
            P("fsdp", "tp"),
            P("fsdp", "tp"),
            P("fsdp", "tp"),
            P(None, "tp"),
            P("tp"),
            P(),
        ),
        out_specs=(
            P(("ctx", "tp"), "fsdp", None),
            P(("ctx", "tp"), "fsdp", None),
            P("fsdp", None, "tp"),
            P("fsdp", "tp"),
            P("fsdp", "tp"),
            P("fsdp", "tp"),
            P(None, "fsdp"),
            P(None, "tp"),
            P("tp"),
            P(),
        ),
        check_vma=False,
    )
```
